256 devices in a mesh: mesh: 8 (over z), rve: 32 (over y, x, core).
Axes of the slice: x: 4, y: 4, z: 8, core: 2. Of those that a mesh axis runs over, the one named last changes fastest.
Arguments:
- displacement: float32 [3, 1024], P(None, ('mesh', 'rve')), may hold values from -6 to 6
- shape_grads: float32 [3, 8, 4096], P(None, None, ('mesh', 'rve')), may hold values from -2 to 2
- point_weights: float32 [4096], P(('mesh', 'rve')), may hold values from 0.5 to 2
- conn: int32 [8, 512], P(None, ('mesh', 'rve')), may hold values from 0 to 143
- halo_nodes: int32 [2, 64], P(None, 'mesh'), may hold values from 0 to 127
- warm_strain: float32 [4096, 6, 4096], P(('mesh', 'rve')), may hold values from -4 to 4
- moduli: float32 [4096, 2, 4096], P(('mesh', 'rve')), may hold values from 0.2 to 2
- owner: int32 [4096], P(('mesh', 'rve')), may hold values from 0 to 31, as said below
- sweeps: int32 [4096], P(('mesh', 'rve')), may hold values from 1 to 2, as said below
Outputs:
- nodal_force: float32 [3, 1024], P(None, ('mesh', 'rve'))
- gp_stress: float32 [6, 4096], P(None, ('mesh', 'rve'))
- micro_strain: float32 [4096, 6, 4096], P(('mesh', 'rve'))
The draws below stay inside these ranges and needn't reach their ends.
Inputs may be any that keep to these rules, and one draw needn't show every extreme that they name: The owner lies in the Gauss point's own mesh row. The 16 Gauss points of one device go 2 each to 8 different owners, and every owner receives exactly 16 Gauss points. `sweeps`: counts may be skewed by owner: all Gauss points of some owners take 2.
All inputs are finite; a program needn't handle non-finite values.
Results may differ from the reference program's by a relative error of at most 0.0003.
Values sent between devices are 32-bit elements; how exact they have to be, the bound alone decides.
A program may use at most 128 MiB of HBM per device.

```python
import math
import jax
import jax.numpy as jnp
from jax import lax

RES = 16
VOX = 4096
GP_DEV = 16
CAP = 2
NODE_DEV = 4
HALO = 8
GPS = 4096
ELEMS = 512
NODES = 1024
N_MESH = 8
N_RVE = 32


def shared_routes(key):
    base = jax.random.fold_in(key, 11)
    row_count = GPS // (N_RVE * GP_DEV)
    key_list = jax.random.split(base, 4)
    shift_order = jax.vmap(lambda subkey: jax.random.permutation(subkey, N_RVE))(jax.random.split(key_list[0], row_count))
    slot_order = jax.vmap(lambda subkey: jax.random.permutation(subkey, GP_DEV))(jax.random.split(key_list[1], row_count * N_RVE))
    slot_order = slot_order.reshape(row_count, N_RVE, GP_DEV)
    group_index = slot_order // CAP
    owners = (shift_order[:, :, None] + group_index) % N_RVE
    heavy_rank = jax.vmap(lambda subkey: jax.random.permutation(subkey, N_RVE))(jax.random.split(key_list[2], row_count))
    owner_rank = jnp.take_along_axis(heavy_rank, owners.reshape(row_count, N_RVE * GP_DEV), axis=1)
    heavy_owner = owner_rank.reshape(row_count, N_RVE, GP_DEV) < max(1, N_RVE // 8)
    light_count = 1 + (jax.random.randint(key_list[3], (row_count, N_RVE, GP_DEV), 0, 4) == 0).astype(jnp.int32)
    counts = jnp.where(heavy_owner, 2, light_count)
    return (owners.reshape(GPS).astype(jnp.int32), counts.reshape(GPS).astype(jnp.int32))


def draw_owner(key, part):
    return shared_routes(key)[0]


def draw_sweeps(key, part):
    return shared_routes(key)[1]


def plant(values, stream_key, low, top_value):
    longest = values.shape.index(max(values.shape))
    spots = []
    for shift in (0, 1):
        where = [jax.random.randint(jax.random.fold_in(stream_key, axis), (), 0, length) for axis, length in enumerate(values.shape)]
        where[longest] = (where[longest] + shift) % values.shape[longest]
        spots.append(tuple(where))
    return values.at[spots[0]].set(low).at[spots[1]].set(top_value)


def block_scale(stream_key, dims, shards, smallest, high):
    loudness, own = 1.0, jax.random.fold_in(stream_key, 6)
    for axis_at, shards_of in shards:
        draws = jnp.exp(jax.random.uniform(jax.random.fold_in(own, axis_at), (shards_of,), jnp.float32, smallest / len(shards), high / len(shards)))
        loudness = loudness * jnp.repeat(draws, dims[axis_at] // shards_of).reshape([-1 if axis == axis_at else 1 for axis in range(len(dims))])
    return loudness


def noise(rng, extent, scale, bound, pieces=(), held_as=jnp.bfloat16):
    drawn = scale * jax.random.normal(rng, extent, jnp.float32)
    if pieces:
        drawn = drawn * block_scale(rng, extent, pieces, -0.22, 0.18)
    return jnp.clip(drawn, -bound, bound).astype(held_as)


def setup_inputs(seed: int = 0) -> dict:
    seeds = jax.random.split(jax.random.key(seed), 10)
    displacement = noise(seeds[0], (3, NODES), 1.0, 6.0, ((1, 256),), jnp.float32)
    shape_grads = noise(seeds[1], (3, 8, GPS), 8 ** -0.5, 2.0, ((2, 256),), jnp.float32)
    point_weights = jnp.clip(jnp.exp(math.log(2.0) - 1.3862944 * jax.random.uniform(seeds[2], (GPS,), jnp.float32) ** block_scale(seeds[2], (GPS,), ((0, 256),), -0.2, 0.2)), 0.5, 2.0)
    conn = plant(jax.random.randint(seeds[3], (8, ELEMS), 0, NODE_DEV * N_RVE + 2 * HALO), jax.random.fold_in(seeds[3], 1), 0, (NODE_DEV * N_RVE + 2 * HALO) - 1).astype(jnp.int32)
    halo_nodes = plant(jax.random.randint(seeds[4], (2, HALO * N_MESH), 0, NODE_DEV * N_RVE), jax.random.fold_in(seeds[4], 1), 0, (NODE_DEV * N_RVE) - 1).astype(jnp.int32)
    warm_strain = noise(seeds[5], (GPS, 6, VOX), 0.5, 4.0, ((0, 256),), jnp.float32)
    moduli = jnp.clip(jnp.exp(math.log(2.0) - 2.3025851 * jax.random.uniform(seeds[6], (GPS, 2, VOX), jnp.float32) ** block_scale(seeds[6], (GPS, 2, VOX), ((0, 256),), -0.2, 0.2)), 0.2, 2.0)
    owner = draw_owner(jax.random.fold_in(seeds[9], 71), 0)
    sweeps = draw_sweeps(jax.random.fold_in(seeds[9], 71), 0)
    return {"displacement": displacement, "shape_grads": shape_grads, "point_weights": point_weights, "conn": conn, "halo_nodes": halo_nodes, "warm_strain": warm_strain, "moduli": moduli, "owner": owner, "sweeps": sweeps}


ref_modulus = 1.1
half_inverse = 1.0 / 2.2
coupling = 2.2 / (1.1 * 3.3)
index_pairs = ((0, 0), (1, 1), (2, 2), (1, 2), (0, 2), (0, 1))
diagonal_entries = (1.0, 1.0, 1.0, 0.0, 0.0, 0.0)

def unit_normals(grid_side):
    wave = jnp.arange(grid_side, dtype=jnp.int32)
    signed = jnp.where(wave < grid_side // 2, wave, wave - grid_side).astype(jnp.float32)
    cube = (grid_side, grid_side, grid_side)
    along_x = jnp.broadcast_to(signed[:, None, None], cube).reshape(-1)
    along_y = jnp.broadcast_to(signed[None, :, None], cube).reshape(-1)
    along_z = jnp.broadcast_to(signed[None, None, :], cube).reshape(-1)
    length_sq = along_x * along_x + along_y * along_y + along_z * along_z
    safe_length = jnp.sqrt(jnp.where(length_sq > 0, length_sq, 1.0))
    inverse_len = jnp.where(length_sq > 0, 1.0 / safe_length, 0.0)
    return jnp.stack([along_x * inverse_len, along_y * inverse_len, along_z * inverse_len])

def green_apply(polar, normals):
    vectors = (normals[0], normals[1], normals[2])
    entries = [polar[..., component, :] for component in range(6)]
    traction_x = entries[0] * vectors[0] + entries[5] * vectors[1] + entries[4] * vectors[2]
    traction_y = entries[5] * vectors[0] + entries[1] * vectors[1] + entries[3] * vectors[2]
    traction_z = entries[4] * vectors[0] + entries[3] * vectors[1] + entries[2] * vectors[2]
    tractions = (traction_x, traction_y, traction_z)
    normal_load = vectors[0] * traction_x + vectors[1] * traction_y + vectors[2] * traction_z
    result = []
    for first_axis, second_axis in index_pairs:
        pair_term = vectors[first_axis] * tractions[second_axis] + vectors[second_axis] * tractions[first_axis]
        result.append(pair_term * half_inverse - coupling * vectors[first_axis] * vectors[second_axis] * normal_load)
    return jnp.stack(result, axis=-2)

def stress_of(strain_field, lame_first, shear_modulus):
    trace_sum = strain_field[:, 0] + strain_field[:, 1] + strain_field[:, 2]
    diagonal_mask = jnp.array(diagonal_entries, jnp.float32)
    return 2.0 * shear_modulus[:, None, :] * strain_field + (lame_first * trace_sum)[:, None, :] * diagonal_mask[None, :, None]

def sweep_once(strain_field, macro_rows, lame_first, shear_modulus, normals):
    batch_size = strain_field.shape[0]
    trace_sum = strain_field[:, 0] + strain_field[:, 1] + strain_field[:, 2]
    diagonal_mask = jnp.array(diagonal_entries, jnp.float32)
    polar = 2.0 * (shear_modulus - ref_modulus)[:, None, :] * strain_field
    polar = polar + ((lame_first - ref_modulus) * trace_sum)[:, None, :] * diagonal_mask[None, :, None]
    spectrum = jnp.fft.fftn(polar.reshape(batch_size, 6, RES, RES, RES), axes=(2, 3, 4)).reshape(batch_size, 6, VOX)
    real_green = green_apply(spectrum.real, normals)
    imag_green = green_apply(spectrum.imag, normals)
    merged = lax.complex(real_green, imag_green).reshape(batch_size, 6, RES, RES, RES)
    fluctuation = jnp.fft.ifftn(merged, axes=(2, 3, 4)).real.reshape(batch_size, 6, VOX)
    return macro_rows[:, :, None] - fluctuation

def reference(displacement, shape_grads, point_weights, conn, halo_nodes, warm_strain, moduli, owner, sweeps):
    row_count = N_MESH
    part_nodes = NODE_DEV * N_RVE
    per_part = ELEMS // row_count
    highest = lax.Precision.HIGHEST
    moved = displacement.reshape(3, row_count, part_nodes).transpose(1, 0, 2)
    lists = halo_nodes.reshape(2, row_count, HALO)
    down_values = jax.vmap(lambda table, picks: table[:, picks])(moved, lists[0])
    up_values = jax.vmap(lambda table, picks: table[:, picks])(moved, lists[1])
    zero_face = jnp.zeros((1, 3, HALO), jnp.float32)
    from_below = jnp.concatenate([zero_face, up_values[:-1]], axis=0)
    from_above = jnp.concatenate([down_values[1:], zero_face], axis=0)
    extended = jnp.concatenate([moved, from_below, from_above], axis=2)
    links = conn.reshape(8, row_count, per_part).transpose(1, 0, 2)
    elem_disp = jax.vmap(lambda table, picks: table[:, picks])(extended, links)
    gradients = shape_grads.reshape(3, 8, row_count, per_part, 8)
    grad_disp = jnp.einsum('piae,japeq->ijpeq', elem_disp, gradients, precision=highest).reshape(3, 3, GPS)
    macro_strain = jnp.stack([grad_disp[0, 0], grad_disp[1, 1], grad_disp[2, 2], (grad_disp[1, 2] + grad_disp[2, 1]) * 0.5, (grad_disp[0, 2] + grad_disp[2, 0]) * 0.5, (grad_disp[0, 1] + grad_disp[1, 0]) * 0.5])
    normals = unit_normals(RES)

    def solve_block(operands):
        macro_rows, warm_rows, moduli_rows, count_rows = operands
        lame_first = moduli_rows[:, 0]
        shear_modulus = moduli_rows[:, 1]
        strain_field = warm_rows - lax.optimization_barrier(jnp.mean(warm_rows, axis=2, keepdims=True)) + macro_rows[:, :, None]
        for sweep_index in range(2):
            updated = sweep_once(strain_field, macro_rows, lame_first, shear_modulus, normals)
            strain_field = jnp.where((count_rows > sweep_index)[:, None, None], updated, strain_field)
        mean_stress = lax.optimization_barrier(jnp.mean(stress_of(strain_field, lame_first, shear_modulus), axis=2))
        return (strain_field, mean_stress)
    blocks = GPS // GP_DEV
    operands = (macro_strain.T.reshape(blocks, GP_DEV, 6), warm_strain.reshape(blocks, GP_DEV, 6, VOX), moduli.reshape(blocks, GP_DEV, 2, VOX), sweeps.reshape(blocks, GP_DEV))
    strain_all, stress_all = lax.map(solve_block, operands)
    strain_all = strain_all.reshape(GPS, 6, VOX)
    gp_stress = stress_all.reshape(GPS, 6).T
    point_index = jnp.arange(GPS, dtype=jnp.int32)
    row_of = point_index // (GP_DEV * N_RVE)
    sort_keys = (row_of * N_RVE + owner.astype(jnp.int32)) * GPS + point_index
    order = jnp.argsort(sort_keys, stable=True).astype(jnp.int32)
    micro_strain = strain_all[order]
    comps = gp_stress
    symmetric = jnp.stack([jnp.stack([comps[0], comps[5], comps[4]]), jnp.stack([comps[5], comps[1], comps[3]]), jnp.stack([comps[4], comps[3], comps[2]])])
    weighted = symmetric * point_weights[None, None, :]
    element_force = jnp.einsum('ijpeq,japeq->piae', weighted.reshape(3, 3, row_count, per_part, 8), gradients, precision=highest)
    width_ext = part_nodes + 2 * HALO
    spread = jax.vmap(lambda forces, picks: jnp.zeros((3, width_ext), jnp.float32).at[:, picks].add(forces))(element_force, links)
    own_part = spread[:, :, :part_nodes]
    below_part = spread[:, :, part_nodes:part_nodes + HALO]
    above_part = spread[:, :, part_nodes + HALO:]
    incoming_low = jnp.concatenate([zero_face, above_part[:-1]], axis=0)
    incoming_high = jnp.concatenate([below_part[1:], zero_face], axis=0)

    def settle(own_rows, low_rows, high_rows, low_list, high_list):
        return own_rows.at[:, low_list].add(low_rows).at[:, high_list].add(high_rows)
    own_part = jax.vmap(settle)(own_part, incoming_low, incoming_high, lists[0], lists[1])
    nodal_force = own_part.transpose(1, 0, 2).reshape(3, NODES)
    return (nodal_force, gp_stress, micro_strain)
```

```python
import functools
import math

import jax
import jax.numpy as jnp
import numpy as np
from jax import lax
from jax.experimental import pallas as pl
from jax.experimental.pallas import tpu as pltpu
from jax.sharding import PartitionSpec as P

RES = 16
PLANE = 256
LANES = 128
TILES = 32
COMPS = 6
HALF = 8
ROWS = COMPS * HALF
SPAN = 8 * HALF
MESH = pl.DeviceIdType.MESH
f32 = jnp.float32
bf16 = jnp.bfloat16
index_pairs = ((0, 0), (1, 1), (2, 2), (1, 2), (0, 2), (0, 1))
coef_rows = [(c, d) for c in range(6) for d in range(c, 6)]
coef_at = {}
for _at, (_c, _d) in enumerate(coef_rows):
    coef_at[(_c, _d)] = _at
    coef_at[(_d, _c)] = _at


def half_planes():
    own = [(0, 0), (0, 8), (8, 0), (8, 8)]
    pairs, seen = [], set(own)
    for y in range(RES):
        for z in range(RES):
            if (y, z) not in seen:
                seen.add((y, z))
                seen.add(((-y) % RES, (-z) % RES))
                pairs.append((y, z))
    lane_a = pairs + [(0, 0), (0, 8)]
    lane_b = pairs + [(8, 0), (8, 8)]
    return np.array(lane_a), np.array(lane_b), len(pairs)


def green_matrix(kx, ky, kz):
    def one(x, y, z):
        k = np.stack([x % RES, y % RES, z % RES]).astype(np.int64)
        xi = np.where(k < RES // 2, k, k - RES).astype(np.float64)
        size = np.sqrt((xi * xi).sum(0))
        n = np.where(size > 0, xi / np.where(size > 0, size, 1.0), 0.0)
        out = np.zeros((6, 6) + size.shape)
        for d, (i, j) in enumerate(index_pairs):
            t = np.zeros((3,) + size.shape)
            t[i] += n[j]
            if i != j:
                t[j] += n[i]
            s = (n * t).sum(0)
            weight = 1.0 if i == j else 2.0
            for c, (k_, h_) in enumerate(index_pairs):
                value = (n[k_] * t[h_] + n[h_] * t[k_]) / 2.2
                value = value - (2.2 / (1.1 * 3.3)) * n[k_] * n[h_] * s
                out[c, d] = value / weight
        return out

    return 0.5 * (one(kx, ky, kz) + one(-kx, -ky, -kz))


@functools.lru_cache(None)
def tables():
    lane_a, lane_b, count = half_planes()
    v = np.arange(PLANE)
    vy, vz = v // RES, v % RES
    angle = 2.0 * math.pi / RES

    def phase(lane):
        return angle * ((np.outer(vy, lane[:, 0]) + np.outer(vz, lane[:, 1])) % RES)

    paired = (np.arange(LANES) < count)[None, :]
    forward = np.concatenate(
        [np.cos(phase(lane_a)), np.where(paired, -np.sin(phase(lane_b)), np.cos(phase(lane_b)))], axis=1
    )
    coef = np.zeros((RES, 2, 24, LANES))
    for slot in range(RES):
        for part in range(2):
            ky, kz, kx, scale = [], [], [], []
            for lane in range(LANES):
                if lane < count:
                    y, z, x, weight = *lane_a[lane], slot, 2.0
                elif slot in (0, RES // 2):
                    y, z = lane_a[lane] if part == 0 else lane_b[lane]
                    x, weight = slot, 1.0
                else:
                    y, z = lane_a[lane] if slot < RES // 2 else lane_b[lane]
                    x, weight = (slot if slot < RES // 2 else RES - slot), 0.5
                ky.append(y), kz.append(z), kx.append(x), scale.append(weight / RES**3)
            matrix = green_matrix(np.array(kx), np.array(ky), np.array(kz)) * np.array(scale)
            for row, (c, d) in enumerate(coef_rows):
                coef[slot, part, row] = matrix[c, d]

    def split(table):
        high = jnp.asarray(table, f32).astype(bf16)
        low = (np.asarray(table, np.float64) - np.asarray(high).astype(np.float64)).astype(np.float32)
        return np.asarray(high), np.asarray(jnp.asarray(low).astype(bf16))

    with jax.ensure_compile_time_eval():
        fh, fl = split(forward)
        ih, il = split(forward.T)
    return np.stack([fh, fl, ih, il]), coef.astype(np.float32), count


def complex_mul(a, b):
    re, im = a
    cr, ci = b
    if abs(ci) < 1e-12 and abs(cr - 1) < 1e-12:
        return a
    if abs(cr) < 1e-12:
        return (im, -re) if ci < 0 else (-im, re)
    if abs(abs(cr) - abs(ci)) < 1e-12:
        h = abs(cr)
        sr, si = cr > 0, ci > 0
        if sr and not si:
            return (h * (re + im), h * (im - re))
        if not sr and not si:
            return (h * (im - re), -h * (re + im))
        if sr and si:
            return (h * (re - im), h * (im + re))
        return (-h * (re + im), h * (re - im))
    return (cr * re - ci * im, cr * im + ci * re)


def four_point(a, b, c, d, sign):
    s0 = (a[0] + c[0], a[1] + c[1])
    s1 = (a[0] - c[0], a[1] - c[1])
    s2 = (b[0] + d[0], b[1] + d[1])
    s3 = (b[0] - d[0], b[1] - d[1])
    turned = (s3[1], -s3[0]) if sign < 0 else (-s3[1], s3[0])
    return (
        (s0[0] + s2[0], s0[1] + s2[1]),
        (s1[0] + turned[0], s1[1] + turned[1]),
        (s0[0] - s2[0], s0[1] - s2[1]),
        (s1[0] - turned[0], s1[1] - turned[1]),
    )


def sixteen_point(values, sign):
    columns = []
    for r in range(4):
        out = four_point(values[r], values[r + 4], values[r + 8], values[r + 12], sign)
        columns.append(
            [
                complex_mul(out[k], (math.cos(2 * math.pi * r * k / 16), sign * math.sin(2 * math.pi * r * k / 16)))
                for k in range(4)
            ]
        )
    result = [None] * 16
    for k in range(4):
        out = four_point(columns[0][k], columns[1][k], columns[2][k], columns[3][k], sign)
        for m in range(4):
            result[k + 4 * m] = out[m]
    return result


def iota(shape, dim):
    return lax.broadcasted_iota(jnp.int32, shape, dim)


def sum_lanes(x):
    return jnp.sum(x, axis=1, keepdims=True)


def sum_rows(x):
    return jnp.sum(x, axis=0, keepdims=True)


def split_bf16(x):
    high = x.astype(bf16)
    low = (x - high.astype(f32)).astype(bf16)
    return high, low


def three_pass(high, low, table_high, table_low):
    def dot(a, b):
        return jnp.dot(a, b, preferred_element_type=f32)

    return dot(high, table_high) + (dot(low, table_high) + dot(high, table_low))


def main_kernel(
    count_paired, n_rve, n_mesh,
    disp_h, grads_h, weight_h, conn_h, halo_h, owner_h, sweeps_h, warm_h, moduli_h, plane_h, coef_h,
    nodal_o, stress_o, got2,
    warm_v, moduli_v, plane_v, coef_v, field, mod, tau_h, tau_l, spec, got1_a, got1_b, stage,
    tile_v, gathered, halo_out, halo_in, force_out, force_in, own_out, own_in,
    perm_v, perm_s, table_v, table_s, column_v,
    disp_s, grads_v, weight_v, conn_v, halo_v, owner_v, sweeps_v, small_sem,
    in_sem, idx_sem, gather_send, gather_recv, halo_send, halo_recv,
    send1, recv1, send2, recv2, fhalo_send, fhalo_recv, own_send, own_recv,
):
    me = lax.axis_index("rve")
    part = lax.axis_index("mesh")
    others = n_rve - 1
    got1 = (got1_a, got1_b)
    last_row = others * SPAN + HALF - 1
    has_below = part > 0
    has_above = part < n_mesh - 1

    small = [
        pltpu.make_async_copy(source, target, small_sem.at[at])
        for at, (source, target) in enumerate((
            (owner_h, owner_v), (sweeps_h, sweeps_v), (disp_h, disp_s), (halo_h, halo_v),
            (conn_h, conn_v), (grads_h, grads_v), (weight_h, weight_v),
        ))
    ]
    for load in small:
        load.start()

    def load_tile(t):
        at = pl.multiple_of(t * LANES, LANES)
        return pltpu.make_async_copy(
            warm_h.at[:, pl.ds(at, LANES)], warm_v.at[t, pl.ds(0, COMPS * 16), :], in_sem.at[0]
        )

    def start_tile(t, carry):
        load_tile(t).start()
        return carry

    lax.fori_loop(0, TILES, start_tile, 0)
    big_loads = [
        pltpu.make_async_copy(moduli_h, moduli_v, in_sem.at[1]),
        pltpu.make_async_copy(plane_h, plane_v, in_sem.at[2]),
        pltpu.make_async_copy(coef_h, coef_v, in_sem.at[3]),
    ]
    for load in big_loads:
        load.start()

    barrier = pltpu.get_barrier_semaphore()

    def greet(k, carry):
        pl.semaphore_signal(barrier, inc=1, device_id={"rve": lax.rem(me + k, n_rve)}, device_id_type=MESH)
        return carry

    lax.fori_loop(1, n_rve, greet, 0)

    @pl.when(has_below)
    def _():
        pl.semaphore_signal(barrier, inc=1, device_id={"mesh": part - 1}, device_id_type=MESH)

    @pl.when(has_above)
    def _():
        pl.semaphore_signal(barrier, inc=1, device_id={"mesh": part + 1}, device_id_type=MESH)

    for load in small:
        load.wait()

    owner_row = owner_v[...].astype(f32)
    sub16, lane16 = iota((16, 16), 0), iota((16, 16), 1)
    owner_col = sum_lanes(jnp.where(sub16 == lane16, jnp.broadcast_to(owner_row, (16, 16)), 0.0))
    place = 0.5 * sum_rows(jnp.where(owner_col < owner_row, 1.0, 0.0))
    rank = sum_rows(jnp.where((owner_col == owner_row) & (sub16 < lane16), 1.0, 0.0))
    slot_row = 8.0 * rank + place
    chosen = jnp.where(slot_row == sub16.astype(f32), 1.0, 0.0)
    perm_col = sum_lanes(chosen * lane16.astype(f32))
    perm_v[...] = jnp.broadcast_to(perm_col, (16, LANES)).astype(jnp.int32)
    count_col = sum_lanes(chosen * sweeps_v[...].astype(f32))
    load_perm = pltpu.make_async_copy(perm_v, perm_s, idx_sem.at[0])
    load_perm.start()

    lane_row = iota((1, LANES), 1).astype(f32)
    sends_row = 0.5 * sum_rows(jnp.where(owner_col == lane_row, 1.0, 0.0))
    sub4, lane4 = iota((4, LANES), 0), iota((4, LANES), 1)
    tile = jnp.where(sub4 == 3, sends_row, 0.0)
    for i in range(3):
        for node in range(4):
            tile = jnp.where((sub4 == i) & (lane4 == 4 * me + node), disp_s[i, node], tile)
    tile_v[...] = tile
    gathered[me] = tile

    extra = jnp.where(has_below, 1, 0) + jnp.where(has_above, 1, 0)
    pl.semaphore_wait(barrier, others + extra)

    def to_all(source, target, send, recv):
        def body(k, carry):
            to = lax.rem(me + k, n_rve)
            pltpu.make_async_remote_copy(
                source, target, send, recv, device_id={"rve": to}, device_id_type=MESH
            ).start()
            return carry

        lax.fori_loop(1, n_rve, body, 0)

    def wait_bytes(view, sem):
        pltpu.make_async_copy(view, view, sem).wait()

    to_all(tile_v, gathered.at[me], gather_send, gather_recv)

    load_perm.wait()
    big_loads[0].wait()

    wait_bytes(warm_v.at[:, pl.ds(0, COMPS * 16), :], in_sem.at[0])
    for half in range(2):
        for pos in range(HALF):
            point = jnp.clip(perm_s[half * HALF + pos, 0], 0, 15)

            def place_tile(t, carry):
                at = pl.multiple_of(t * LANES, LANES)
                field[half, t, pl.ds(pos, COMPS, stride=HALF), :] = warm_v[t, pl.ds(point, COMPS, stride=16), :]
                mod[half, t, pl.ds(pos, 2, stride=HALF), :] = moduli_v[point, :, pl.ds(at, LANES)]
                return carry

            lax.fori_loop(0, TILES, place_tile, 0)

    def mean_of(half):
        def body(t, sums):
            return tuple(sums[c] + field[half, t, c * HALF : (c + 1) * HALF, :] for c in range(COMPS))

        sums = lax.fori_loop(0, TILES, body, tuple(jnp.zeros((HALF, LANES), f32) for _ in range(COMPS)))
        return [sum_lanes(s) * (1.0 / 4096.0) for s in sums]

    means = [mean_of(0), mean_of(1)]

    wait_bytes(gathered.at[pl.ds(0, others)], gather_recv)
    moved = jnp.sum(gathered[...], axis=0)
    lane8, sub8 = iota((HALF, LANES), 1).astype(f32), iota((HALF, LANES), 0).astype(f32)
    eye8 = iota((HALF, HALF), 0) == iota((HALF, HALF), 1)
    halo_rows = halo_v[...].astype(f32)
    halo_hot = []
    for side in range(2):
        col = sum_lanes(jnp.where(eye8, jnp.broadcast_to(halo_rows[side : side + 1], (HALF, HALF)), 0.0))
        halo_hot.append(jnp.where(col == lane8, 1.0, 0.0))
    out_tile = jnp.zeros((HALF, LANES), f32)
    for side in range(2):
        for i in range(3):
            col = sum_lanes(halo_hot[side] * moved[i : i + 1])
            out_tile = jnp.where(lane8 == 3 * side + i, col, out_tile)
    halo_out[...] = out_tile

    def swap_halo(source, target, send, recv):
        @pl.when(has_below)
        def _():
            pltpu.make_async_remote_copy(
                source, target.at[1], send.at[0], recv.at[1], device_id={"mesh": part - 1}, device_id_type=MESH
            ).start()

        @pl.when(has_above)
        def _():
            pltpu.make_async_remote_copy(
                source, target.at[0], send.at[1], recv.at[0], device_id={"mesh": part + 1}, device_id_type=MESH
            ).start()

    def take_halo(source, target, recv):
        @pl.when(has_below)
        def _():
            wait_bytes(target.at[0], recv.at[0])

        @pl.when(jnp.logical_not(has_below))
        def _():
            target[0] = jnp.zeros((HALF, LANES), f32)

        @pl.when(has_above)
        def _():
            wait_bytes(target.at[1], recv.at[1])

        @pl.when(jnp.logical_not(has_above))
        def _():
            target[1] = jnp.zeros((HALF, LANES), f32)

    swap_halo(halo_out, halo_in, halo_send, halo_recv)

    sends = jnp.concatenate([gathered[s, 3:4] for s in range(n_rve)], axis=0)
    lower = jnp.where(iota((n_rve, n_rve), 1) < iota((n_rve, n_rve), 0), 1.0, 0.0).astype(bf16)
    upper = jnp.where(iota((LANES, LANES), 0) < iota((LANES, LANES), 1), 1.0, 0.0).astype(bf16)
    sends_b = sends.astype(bf16)
    order = jnp.dot(lower, sends_b, preferred_element_type=f32)
    places = jnp.dot(sends_b, upper, preferred_element_type=f32)
    rows_at = iota((n_rve, LANES), 0).astype(f32) * float(SPAN) + places
    table = jnp.zeros((HALF, LANES), f32)
    for k in range(HALF):
        row = sum_rows(jnp.where((sends > 0.5) & (order == float(k)), rows_at, 0.0))
        table = jnp.where(sub8 == float(k), row, table)
    table_v[...] = table.astype(jnp.int32)
    load_table = pltpu.make_async_copy(table_v, table_s, idx_sem.at[1])
    load_table.start()

    conn_rows = conn_v[...].astype(f32)
    own_hot, far_hot = [], []
    for e in range(2):
        col = sum_lanes(jnp.where(eye8, jnp.broadcast_to(conn_rows[e : e + 1], (HALF, HALF)), 0.0))
        own_hot.append(jnp.where(col == lane8, 1.0, 0.0))
        far_hot.append(jnp.where(col - float(LANES) == lane8, 1.0, 0.0))
    first_element = iota((HALF, 16), 1) < 8

    take_halo(halo_out, halo_in, halo_recv)
    below, above = halo_in[0], halo_in[1]
    spread_disp = []
    for i in range(3):
        far = sum_rows(jnp.where(lane8 == sub8, below[:, 3 + i : 4 + i], 0.0))
        far = far + sum_rows(jnp.where(lane8 == sub8 + 8.0, above[:, i : i + 1], 0.0))
        cols = [sum_lanes(own_hot[e] * moved[i : i + 1] + far_hot[e] * far) for e in range(2)]
        spread_disp.append(jnp.where(first_element, cols[0], cols[1]))
    grads = [grads_v[j] for j in range(3)]
    g = [[sum_rows(spread_disp[i] * grads[j]) for j in range(3)] for i in range(3)]
    macro = [
        g[0][0], g[1][1], g[2][2],
        (g[1][2] + g[2][1]) * 0.5, (g[0][2] + g[2][0]) * 0.5, (g[0][1] + g[1][0]) * 0.5,
    ]
    macro_cols = [sum_lanes(chosen * row) for row in macro]
    for c in range(COMPS):
        for half in range(2):
            col = macro_cols[c][half * HALF : (half + 1) * HALF]
            column_v[half, 0, c] = jnp.broadcast_to(col - means[half][c], (HALF, LANES))
            column_v[half, 1, c] = jnp.broadcast_to(col, (HALF, LANES))
    for half in range(2):
        column_v[half, 2, 0] = jnp.broadcast_to(count_col[half * HALF : (half + 1) * HALF], (HALF, LANES))

    big_loads[1].wait()
    big_loads[2].wait()
    odd_lane = iota((HALF, LANES), 1) >= count_paired

    def sweep(half, number):
        def polarize(u, carry):
            for b in range(2):
                cats = [[] for _ in range(COMPS)]
                for step in range(2):
                    t = (2 * u + step) * 2 + b
                    eps = [field[half, t, c * HALF : (c + 1) * HALF, :] for c in range(COMPS)]
                    if number == 0:
                        eps = [eps[c] + column_v[half, 0, c] for c in range(COMPS)]
                    lam = mod[half, t, 0:HALF, :] - 1.1
                    shear = 2.0 * mod[half, t, HALF : 2 * HALF, :] - 2.2
                    pressure = lam * (eps[0] + eps[1] + eps[2])
                    double = shear + shear
                    for c in range(3):
                        cats[c].append(shear * eps[c] + pressure)
                    for c in range(3, 6):
                        cats[c].append(double * eps[c])
                for c in range(COMPS):
                    high, low = split_bf16(jnp.concatenate(cats[c], axis=0))
                    at = pl.multiple_of(u * 16, 16)
                    tau_h[c, pl.ds(at, 16), b * LANES : (b + 1) * LANES] = high
                    tau_l[c, pl.ds(at, 16), b * LANES : (b + 1) * LANES] = low
            return carry

        lax.fori_loop(0, 8, polarize, 0)

        def forward(c, carry):
            planed = three_pass(tau_h[c], tau_l[c], plane_v[0], plane_v[1])
            values = [
                (planed[x * HALF : (x + 1) * HALF, :LANES], planed[x * HALF : (x + 1) * HALF, LANES:])
                for x in range(RES)
            ]
            z = sixteen_point(values, -1)
            for k in range(1, 8):
                a, b = z[k], z[RES - k]
                z[k] = (jnp.where(odd_lane, a[0] + b[0], a[0]), jnp.where(odd_lane, a[1] - b[1], a[1]))
                z[RES - k] = (jnp.where(odd_lane, a[1] + b[1], b[0]), jnp.where(odd_lane, b[0] - a[0], b[1]))
            for k in range(RES):
                spec[k, 0, c] = z[k][0]
                spec[k, 1, c] = z[k][1]
            return carry

        lax.fori_loop(0, COMPS, forward, 0)

        def green(k, carry):
            for part_at in range(2):
                ins = [spec[k, part_at, c] for c in range(COMPS)]
                rows = [coef_v[k, part_at, r : r + 1, :] for r in range(len(coef_rows))]
                for c in range(COMPS):
                    total = rows[coef_at[(c, 0)]] * ins[0]
                    for d in range(1, COMPS):
                        total = total + rows[coef_at[(c, d)]] * ins[d]
                    spec[k, part_at, c] = total
            return carry

        lax.fori_loop(0, RES, green, 0)

        def backward(c, carry):
            z = [(spec[k, 0, c], spec[k, 1, c]) for k in range(RES)]
            for k in range(1, 8):
                a, b = z[k], z[RES - k]
                z[k] = (jnp.where(odd_lane, a[0] - b[1], a[0]), jnp.where(odd_lane, a[1] + b[0], a[1]))
                z[RES - k] = (jnp.where(odd_lane, a[0] + b[1], b[0]), jnp.where(odd_lane, b[0] - a[1], b[1]))
            values = sixteen_point(z, 1)
            lined = jnp.concatenate(
                [
                    jnp.concatenate([values[x][0] for x in range(RES)], axis=0),
                    jnp.concatenate([values[x][1] for x in range(RES)], axis=0),
                ],
                axis=1,
            )
            high, low = split_bf16(lined)
            fluct = three_pass(high, low, plane_v[2], plane_v[3])
            level = column_v[half, 1, c]
            again = column_v[half, 2, 0] > float(number) + 0.5
            at = pl.multiple_of(c * HALF, HALF)
            for x in range(RES):
                for b in range(2):
                    new = level - fluct[x * HALF : (x + 1) * HALF, b * LANES : (b + 1) * LANES]
                    t = 2 * x + b
                    if number > 0:
                        new = jnp.where(again, new, field[half, t, pl.ds(at, HALF), :])
                    field[half, t, pl.ds(at, HALF), :] = new
            return carry

        lax.fori_loop(0, COMPS, backward, 0)

    def mean_stress(half):
        def body(t, sums):
            eps = [field[half, t, c * HALF : (c + 1) * HALF, :] for c in range(COMPS)]
            lam = mod[half, t, 0:HALF, :]
            shear = mod[half, t, HALF : 2 * HALF, :]
            new = [sums[c] + shear * eps[c] for c in range(COMPS)]
            return (*new, sums[6] + lam * (eps[0] + eps[1] + eps[2]))

        sums = lax.fori_loop(0, TILES, body, tuple(jnp.zeros((HALF, LANES), f32) for _ in range(7)))
        result = []
        for c in range(COMPS):
            total = 2.0 * sums[c]
            if c < 3:
                total = total + sums[6]
            result.append(sum_lanes(total) * (1.0 / 4096.0))
        return result

    def send_spread(half):
        rows = pl.multiple_of(me * SPAN, SPAN)
        got1[half][pl.ds(rows, ROWS), :] = field[half, me, pl.ds(0, ROWS), :]

        def body(k, carry):
            to = lax.rem(me + k, n_rve)
            pltpu.make_async_remote_copy(
                field.at[half, to, pl.ds(0, ROWS), :], got1[half].at[pl.ds(rows, ROWS), :], send1.at[half], recv1.at[half],
                device_id={"rve": to}, device_id_type=MESH,
            ).start()
            return carry

        lax.fori_loop(1, n_rve, body, 0)

    def send_owned(half):
        wait_bytes(got2.at[half, pl.ds(0, others)], recv1.at[half])

        def body(k, carry):
            to = lax.rem(me + k, n_rve)
            for at in range(HALF):
                row = jnp.clip(table_s[at, to], 0, last_row)
                stage[half, to, pl.ds(at, COMPS, stride=HALF), :] = got1[half][
                    pl.ds(row, COMPS, stride=HALF), :
                ]

            @pl.when(k > 0)
            def _():
                pltpu.make_async_remote_copy(
                    stage.at[half, to, pl.ds(0, ROWS), :], got2.at[half, me], send2.at[half], recv2.at[half],
                    device_id={"rve": to}, device_id_type=MESH,
                ).start()

            return carry

        lax.fori_loop(1, n_rve, body, 0)
        body(0, 0)
        keep = pltpu.make_async_copy(stage.at[half, me, pl.ds(0, ROWS), :], got2.at[half, me], in_sem.at[4 + half])
        keep.start()
        return keep

    load_table.wait()
    sweep(0, 0)
    sweep(0, 1)
    send_spread(0)
    stress = [mean_stress(0)]
    sweep(1, 0)
    keep0 = send_owned(0)
    sweep(1, 1)
    send_spread(1)
    stress.append(mean_stress(1))

    weights = weight_v[...]
    sigma = []
    for c in range(COMPS):
        col = jnp.concatenate([stress[0][c], stress[1][c]], axis=0)
        row = sum_rows(chosen * col)
        stress_o[c : c + 1, :] = row
        sigma.append(row * weights)
    grid = ((0, 5, 4), (5, 1, 3), (4, 3, 2))
    force_tile = jnp.zeros((HALF, LANES), f32)
    own_rows = []
    for i in range(3):
        point_force = sigma[grid[i][0]] * grads[0] + sigma[grid[i][1]] * grads[1] + sigma[grid[i][2]] * grads[2]
        cols = [
            sum_lanes(jnp.where(first_element, point_force, 0.0)),
            sum_lanes(jnp.where(first_element, 0.0, point_force)),
        ]
        own_rows.append(sum_rows(own_hot[0] * cols[0] + own_hot[1] * cols[1]))
        far = sum_rows(far_hot[0] * cols[0] + far_hot[1] * cols[1])
        force_tile = jnp.where(sub8 == float(i), far, force_tile)
    force_out[...] = force_tile
    swap_halo(force_out, force_in, fhalo_send, fhalo_recv)
    keep1 = send_owned(1)
    take_halo(force_out, force_in, fhalo_recv)
    below, above = force_in[0], force_in[1]
    own_tile = jnp.zeros((4, LANES), f32)
    for i in range(3):
        low = sum_lanes(jnp.where(lane8 == sub8 + 8.0, below[i : i + 1], 0.0))
        high = sum_lanes(jnp.where(lane8 == sub8, above[i : i + 1], 0.0))
        row = own_rows[i] + sum_rows(halo_hot[0] * low + halo_hot[1] * high)
        own_tile = jnp.where(sub4 == i, row, own_tile)
    own_out[...] = own_tile
    own_in[me] = own_tile
    to_all(own_out, own_in.at[me], own_send, own_recv)
    wait_bytes(own_in.at[pl.ds(0, others)], own_recv)
    total = jnp.sum(own_in[...], axis=0)
    mine = jnp.zeros((4, LANES), f32)
    for node in range(4):
        mine = jnp.where(lane4 == node, sum_lanes(jnp.where(lane4 == 4 * me + node, total, 0.0)), mine)
    nodal_o[...] = mine[:3, :4]

    keep0.wait()
    keep1.wait()
    for half in range(2):
        wait_bytes(got2.at[half, pl.ds(0, others)], recv2.at[half])
    wait_bytes(gathered.at[pl.ds(0, others)], gather_send)
    wait_bytes(own_in.at[pl.ds(0, others)], own_send)
    for half in range(2):
        wait_bytes(got2.at[half, pl.ds(0, others)], send1.at[half])
        wait_bytes(got2.at[half, pl.ds(0, others)], send2.at[half])
    for send, source in ((halo_send, halo_out), (fhalo_send, force_out)):
        @pl.when(has_below)
        def _(send=send, source=source):
            wait_bytes(source, send.at[0])

        @pl.when(has_above)
        def _(send=send, source=source):
            wait_bytes(source, send.at[1])


def lay_out_kernel(got_h, nodal_ref, stress_ref, out_h, nodal_o, stress_o, taken, mixed, in_sem, out_sem):
    parts = mixed.shape[0]
    group = TILES // parts

    def copy_in(at):
        return pltpu.make_async_copy(got_h.at[:, pl.ds(at * group, group)], taken.at[at], in_sem.at[at])

    def copy_out(at):
        return pltpu.make_async_copy(
            mixed.at[at], out_h.at[:, pl.ds(at * group * LANES, group * LANES)], out_sem.at[at]
        )

    for at in range(parts):
        copy_in(at).start()
    nodal_o[...] = nodal_ref[...]
    stress_o[...] = stress_ref[...]
    for at in range(parts):
        copy_in(at).wait()
        for t in range(group):
            for c in range(COMPS):
                first, second = (taken[at, half, t, c * HALF : (c + 1) * HALF, :] for half in range(2))
                pair = jnp.concatenate([first[:, None], second[:, None]], axis=1).reshape(2 * HALF, LANES)
                mixed[at, 2 * HALF * c : 2 * HALF * (c + 1), t * LANES : (t + 1) * LANES] = pair
        copy_out(at).start()
    for at in range(parts):
        copy_out(at).wait()


def lay_out(got, nodal, stress):
    parts = 8
    vmem = pl.BlockSpec(memory_space=pltpu.VMEM)
    hbm = pl.BlockSpec(memory_space=pltpu.HBM)
    return pl.pallas_call(
        lay_out_kernel,
        in_specs=[hbm, vmem, vmem],
        out_specs=[hbm, vmem, vmem],
        out_shape=[
            jax.ShapeDtypeStruct((2 * ROWS, TILES * LANES), f32),
            jax.ShapeDtypeStruct(nodal.shape, f32),
            jax.ShapeDtypeStruct(stress.shape, f32),
        ],
        scratch_shapes=[
            pltpu.VMEM((parts, 2, TILES // parts, ROWS, LANES), f32),
            pltpu.VMEM((parts, 2 * ROWS, TILES // parts * LANES), f32),
            pltpu.SemaphoreType.DMA((parts,)),
            pltpu.SemaphoreType.DMA((parts,)),
        ],
        compiler_params=pltpu.CompilerParams(vmem_limit_bytes=63 * 1024 * 1024),
        name="lay_out",
    )(got, nodal, stress)


def solution(mesh):
    n_rve, n_mesh = mesh.shape["rve"], mesh.shape["mesh"]
    planes, coef, count_paired = tables()

    def on_device(displacement, shape_grads, point_weights, conn, halo_nodes, warm_strain, moduli, owner, sweeps):
        points, voxels = warm_strain.shape[0], warm_strain.shape[2]
        warm = warm_strain.transpose(1, 0, 2).reshape(COMPS * points, voxels)
        vmem = pl.BlockSpec(memory_space=pltpu.VMEM)
        hbm = pl.BlockSpec(memory_space=pltpu.HBM)
        dma = pltpu.SemaphoreType.DMA
        scratch = [
            pltpu.VMEM((TILES, 8 * points, LANES), f32),
            pltpu.VMEM((points, 2, voxels), f32),
            pltpu.VMEM(planes.shape, bf16),
            pltpu.VMEM(coef.shape, f32),
            pltpu.VMEM((2, TILES, SPAN, LANES), f32),
            pltpu.VMEM((2, TILES, SPAN, LANES), f32),
            pltpu.VMEM((COMPS, RES * HALF, PLANE), bf16),
            pltpu.VMEM((COMPS, RES * HALF, PLANE), bf16),
            pltpu.VMEM((RES, 2, COMPS, HALF, LANES), f32),
            pltpu.VMEM((n_rve * SPAN, LANES), f32),
            pltpu.VMEM((n_rve * SPAN, LANES), f32),
            pltpu.VMEM((2, n_rve, SPAN, LANES), f32),
            pltpu.VMEM((4, LANES), f32),
            pltpu.VMEM((n_rve, 4, LANES), f32),
            pltpu.VMEM((HALF, LANES), f32),
            pltpu.VMEM((2, HALF, LANES), f32),
            pltpu.VMEM((HALF, LANES), f32),
            pltpu.VMEM((2, HALF, LANES), f32),
            pltpu.VMEM((4, LANES), f32),
            pltpu.VMEM((n_rve, 4, LANES), f32),
            pltpu.VMEM((16, LANES), jnp.int32),
            pltpu.SMEM((16, LANES), jnp.int32),
            pltpu.VMEM((HALF, LANES), jnp.int32),
            pltpu.SMEM((HALF, LANES), jnp.int32),
            pltpu.VMEM((2, 3, COMPS, HALF, LANES), f32),
            pltpu.SMEM((3, 4), f32),
            pltpu.VMEM(shape_grads.shape, f32),
            pltpu.VMEM((1, points), f32),
            pltpu.VMEM((2, 8), jnp.int32),
            pltpu.VMEM((2, 8), jnp.int32),
            pltpu.VMEM((1, points), jnp.int32),
            pltpu.VMEM((1, points), jnp.int32),
            dma((7,)),
            dma((6,)), dma((2,)), dma, dma, dma((2,)), dma((2,)),
            dma((2,)), dma((2,)), dma((2,)), dma((2,)), dma((2,)), dma((2,)), dma, dma,
        ]
        nodal, stress, got = pl.pallas_call(
            functools.partial(main_kernel, count_paired, n_rve, n_mesh),
            in_specs=[hbm] * 11,
            out_specs=[vmem, vmem, hbm],
            out_shape=[
                jax.ShapeDtypeStruct((3, 4), f32),
                jax.ShapeDtypeStruct((COMPS, points), f32),
                jax.ShapeDtypeStruct((2, n_rve, ROWS, LANES), f32),
            ],
            scratch_shapes=scratch,
            compiler_params=pltpu.CompilerParams(
                collective_id=0, has_side_effects=True, vmem_limit_bytes=63 * 1024 * 1024
            ),
            name="solve_and_exchange",
        )(
            displacement, shape_grads, point_weights.reshape(1, points), conn.T, halo_nodes,
            owner.reshape(1, points), sweeps.reshape(1, points), warm, moduli,
            jnp.asarray(planes), jnp.asarray(coef),
        )
        micro, nodal, stress = lay_out(got, nodal, stress)
        micro = micro.reshape(COMPS, points, voxels).transpose(1, 0, 2)
        return nodal, stress, micro

    both = ("mesh", "rve")
    in_specs = (
        P(None, both), P(None, None, both), P(both), P(None, both), P(None, "mesh"),
        P(both, None, None), P(both, None, None), P(both), P(both),
    )
    out_specs = (P(None, both), P(None, both), P(both, None, None))
    return jax.shard_map(on_device, mesh=mesh, in_specs=in_specs, out_specs=out_specs, check_vma=False)
```

```python
import functools
import math

import jax
import jax.numpy as jnp
import numpy as np
from jax import lax
from jax.experimental import pallas as pl
from jax.experimental.pallas import tpu as pltpu
from jax.sharding import PartitionSpec as P

RES = 16
PLANE = 256
LANES = 128
TILES = 32
COMPS = 6
HALF = 8
ROWS = COMPS * HALF
SPAN = 8 * HALF
MESH = pl.DeviceIdType.MESH
f32 = jnp.float32
bf16 = jnp.bfloat16
index_pairs = ((0, 0), (1, 1), (2, 2), (1, 2), (0, 2), (0, 1))
coef_rows = [(c, d) for c in range(6) for d in range(c, 6)]
coef_at = {}
for _at, (_c, _d) in enumerate(coef_rows):
    coef_at[(_c, _d)] = _at
    coef_at[(_d, _c)] = _at


def half_planes():
    own = [(0, 0), (0, 8), (8, 0), (8, 8)]
    pairs, seen = [], set(own)
    for y in range(RES):
        for z in range(RES):
            if (y, z) not in seen:
                seen.add((y, z))
                seen.add(((-y) % RES, (-z) % RES))
                pairs.append((y, z))
    lane_a = pairs + [(0, 0), (0, 8)]
    lane_b = pairs + [(8, 0), (8, 8)]
    return np.array(lane_a), np.array(lane_b), len(pairs)


def green_matrix(kx, ky, kz):
    def one(x, y, z):
        k = np.stack([x % RES, y % RES, z % RES]).astype(np.int64)
        xi = np.where(k < RES // 2, k, k - RES).astype(np.float64)
        size = np.sqrt((xi * xi).sum(0))
        n = np.where(size > 0, xi / np.where(size > 0, size, 1.0), 0.0)
        out = np.zeros((6, 6) + size.shape)
        for d, (i, j) in enumerate(index_pairs):
            t = np.zeros((3,) + size.shape)
            t[i] += n[j]
            if i != j:
                t[j] += n[i]
            s = (n * t).sum(0)
            weight = 1.0 if i == j else 2.0
            for c, (k_, h_) in enumerate(index_pairs):
                value = (n[k_] * t[h_] + n[h_] * t[k_]) / 2.2
                value = value - (2.2 / (1.1 * 3.3)) * n[k_] * n[h_] * s
                out[c, d] = value / weight
        return out

    return 0.5 * (one(kx, ky, kz) + one(-kx, -ky, -kz))


@functools.lru_cache(None)
def tables():
    lane_a, lane_b, count = half_planes()
    v = np.arange(PLANE)
    vy, vz = v // RES, v % RES
    angle = 2.0 * math.pi / RES

    def phase(lane):
        return angle * ((np.outer(vy, lane[:, 0]) + np.outer(vz, lane[:, 1])) % RES)

    paired = (np.arange(LANES) < count)[None, :]
    forward = np.concatenate(
        [np.cos(phase(lane_a)), np.where(paired, -np.sin(phase(lane_b)), np.cos(phase(lane_b)))], axis=1
    )
    coef = np.zeros((RES, 2, 24, LANES))
    for slot in range(RES):
        for part in range(2):
            ky, kz, kx, scale = [], [], [], []
            for lane in range(LANES):
                if lane < count:
                    y, z, x, weight = *lane_a[lane], slot, 2.0
                elif slot in (0, RES // 2):
                    y, z = lane_a[lane] if part == 0 else lane_b[lane]
                    x, weight = slot, 1.0
                else:
                    y, z = lane_a[lane] if slot < RES // 2 else lane_b[lane]
                    x, weight = (slot if slot < RES // 2 else RES - slot), 0.5
                ky.append(y), kz.append(z), kx.append(x), scale.append(weight / RES**3)
            matrix = green_matrix(np.array(kx), np.array(ky), np.array(kz)) * np.array(scale)
            for row, (c, d) in enumerate(coef_rows):
                coef[slot, part, row] = matrix[c, d]

    def split(table):
        high = jnp.asarray(table, f32).astype(bf16)
        low = (np.asarray(table, np.float64) - np.asarray(high).astype(np.float64)).astype(np.float32)
        return np.asarray(high), np.asarray(jnp.asarray(low).astype(bf16))

    with jax.ensure_compile_time_eval():
        fh, fl = split(forward)
        ih, il = split(forward.T)
    return np.stack([fh, fl, ih, il]), coef.astype(np.float32), count


def complex_mul(a, b):
    re, im = a
    cr, ci = b
    if abs(ci) < 1e-12 and abs(cr - 1) < 1e-12:
        return a
    if abs(cr) < 1e-12:
        return (im, -re) if ci < 0 else (-im, re)
    if abs(abs(cr) - abs(ci)) < 1e-12:
        h = abs(cr)
        sr, si = cr > 0, ci > 0
        if sr and not si:
            return (h * (re + im), h * (im - re))
        if not sr and not si:
            return (h * (im - re), -h * (re + im))
        if sr and si:
            return (h * (re - im), h * (im + re))
        return (-h * (re + im), h * (re - im))
    return (cr * re - ci * im, cr * im + ci * re)


def four_point(a, b, c, d, sign):
    s0 = (a[0] + c[0], a[1] + c[1])
    s1 = (a[0] - c[0], a[1] - c[1])
    s2 = (b[0] + d[0], b[1] + d[1])
    s3 = (b[0] - d[0], b[1] - d[1])
    turned = (s3[1], -s3[0]) if sign < 0 else (-s3[1], s3[0])
    return (
        (s0[0] + s2[0], s0[1] + s2[1]),
        (s1[0] + turned[0], s1[1] + turned[1]),
        (s0[0] - s2[0], s0[1] - s2[1]),
        (s1[0] - turned[0], s1[1] - turned[1]),
    )


def sixteen_point(values, sign):
    columns = []
    for r in range(4):
        out = four_point(values[r], values[r + 4], values[r + 8], values[r + 12], sign)
        columns.append(
            [
                complex_mul(out[k], (math.cos(2 * math.pi * r * k / 16), sign * math.sin(2 * math.pi * r * k / 16)))
                for k in range(4)
            ]
        )
    result = [None] * 16
    for k in range(4):
        out = four_point(columns[0][k], columns[1][k], columns[2][k], columns[3][k], sign)
        for m in range(4):
            result[k + 4 * m] = out[m]
    return result


def iota(shape, dim):
    return lax.broadcasted_iota(jnp.int32, shape, dim)


def sum_lanes(x):
    return jnp.sum(x, axis=1, keepdims=True)


def sum_rows(x):
    return jnp.sum(x, axis=0, keepdims=True)


def split_bf16(x):
    high = x.astype(bf16)
    low = (x - high.astype(f32)).astype(bf16)
    return high, low


def three_pass(high, low, table_high, table_low):
    def dot(a, b):
        return jnp.dot(a, b, preferred_element_type=f32)

    return dot(high, table_high) + (dot(low, table_high) + dot(high, table_low))


def main_kernel(
    count_paired, n_rve, n_mesh,
    disp_h, grads_h, weight_h, conn_h, halo_h, owner_h, sweeps_h, warm_h, moduli_h, plane_h, coef_h,
    nodal_o, stress_o, got2,
    warm_v, moduli_v, plane_v, coef_v, field, mod, tau_h, tau_l, spec, got1_a, got1_b, stage,
    tile_v, gathered, halo_out, halo_in, force_out, force_in, own_out, own_in,
    perm_v, perm_s, table_v, table_s, column_v,
    disp_s, grads_v, weight_v, conn_v, halo_v, owner_v, sweeps_v, small_sem,
    in_sem, idx_sem, gather_send, gather_recv, halo_send, halo_recv,
    send1, recv1, send2, recv2, fhalo_send, fhalo_recv, own_send, own_recv,
):
    me = lax.axis_index("rve")
    part = lax.axis_index("mesh")
    others = n_rve - 1
    got1 = (got1_a, got1_b)
    last_row = others * SPAN + HALF - 1
    has_below = part > 0
    has_above = part < n_mesh - 1

    small = [
        pltpu.make_async_copy(source, target, small_sem.at[at])
        for at, (source, target) in enumerate((
            (owner_h, owner_v), (sweeps_h, sweeps_v), (disp_h, disp_s), (halo_h, halo_v),
            (conn_h, conn_v), (grads_h, grads_v), (weight_h, weight_v),
        ))
    ]
    for load in small:
        load.start()

    def load_tile(t):
        at = pl.multiple_of(t * LANES, LANES)
        return pltpu.make_async_copy(
            warm_h.at[:, pl.ds(at, LANES)], warm_v.at[t, pl.ds(0, COMPS * 16), :], in_sem.at[0]
        )

    def start_tile(t, carry):
        load_tile(t).start()
        return carry

    lax.fori_loop(0, TILES, start_tile, 0)
    big_loads = [
        pltpu.make_async_copy(moduli_h, moduli_v, in_sem.at[1]),
        pltpu.make_async_copy(plane_h, plane_v, in_sem.at[2]),
        pltpu.make_async_copy(coef_h, coef_v, in_sem.at[3]),
    ]
    for load in big_loads:
        load.start()

    barrier = pltpu.get_barrier_semaphore()

    def greet(k, carry):
        pl.semaphore_signal(barrier, inc=1, device_id={"rve": lax.rem(me + k, n_rve)}, device_id_type=MESH)
        return carry

    lax.fori_loop(1, n_rve, greet, 0)

    @pl.when(has_below)
    def _():
        pl.semaphore_signal(barrier, inc=1, device_id={"mesh": part - 1}, device_id_type=MESH)

    @pl.when(has_above)
    def _():
        pl.semaphore_signal(barrier, inc=1, device_id={"mesh": part + 1}, device_id_type=MESH)

    for load in small:
        load.wait()

    owner_row = owner_v[...].astype(f32)
    sub16, lane16 = iota((16, 16), 0), iota((16, 16), 1)
    owner_col = sum_lanes(jnp.where(sub16 == lane16, jnp.broadcast_to(owner_row, (16, 16)), 0.0))
    place = 0.5 * sum_rows(jnp.where(owner_col < owner_row, 1.0, 0.0))
    rank = sum_rows(jnp.where((owner_col == owner_row) & (sub16 < lane16), 1.0, 0.0))
    slot_row = 8.0 * rank + place
    chosen = jnp.where(slot_row == sub16.astype(f32), 1.0, 0.0)
    perm_col = sum_lanes(chosen * lane16.astype(f32))
    perm_v[...] = jnp.broadcast_to(perm_col, (16, LANES)).astype(jnp.int32)
    count_col = sum_lanes(chosen * sweeps_v[...].astype(f32))
    load_perm = pltpu.make_async_copy(perm_v, perm_s, idx_sem.at[0])
    load_perm.start()

    lane_row = iota((1, LANES), 1).astype(f32)
    sends_row = 0.5 * sum_rows(jnp.where(owner_col == lane_row, 1.0, 0.0))
    sub4, lane4 = iota((4, LANES), 0), iota((4, LANES), 1)
    tile = jnp.where(sub4 == 3, sends_row, 0.0)
    for i in range(3):
        for node in range(4):
            tile = jnp.where((sub4 == i) & (lane4 == 4 * me + node), disp_s[i, node], tile)
    tile_v[...] = tile
    gathered[me] = tile

    extra = jnp.where(has_below, 1, 0) + jnp.where(has_above, 1, 0)
    pl.semaphore_wait(barrier, others + extra)

    def to_all(source, target, send, recv):
        def body(k, carry):
            to = lax.rem(me + k, n_rve)
            pltpu.make_async_remote_copy(
                source, target, send, recv, device_id={"rve": to}, device_id_type=MESH
            ).start()
            return carry

        lax.fori_loop(1, n_rve, body, 0)

    def wait_bytes(view, sem):
        pltpu.make_async_copy(view, view, sem).wait()

    to_all(tile_v, gathered.at[me], gather_send, gather_recv)

    load_perm.wait()
    big_loads[0].wait()

    wait_bytes(warm_v.at[:, pl.ds(0, COMPS * 16), :], in_sem.at[0])
    places_at = [
        (half, pos, jnp.clip(perm_s[half * HALF + pos, 0], 0, 15)) for half in range(2) for pos in range(HALF)
    ]

    def place_tile(t, carry):
        at = pl.multiple_of(t * LANES, LANES)
        for half, pos, point in places_at:
            field[half, t, pl.ds(pos, COMPS, stride=HALF), :] = warm_v[t, pl.ds(point, COMPS, stride=16), :]
            mod[half, t, pl.ds(pos, 2, stride=HALF), :] = moduli_v[point, :, pl.ds(at, LANES)]
        return carry

    lax.fori_loop(0, TILES, place_tile, 0)

    def add_up(t, sums):
        return tuple(
            sums[half * COMPS + c] + field[half, t, c * HALF : (c + 1) * HALF, :]
            for half in range(2)
            for c in range(COMPS)
        )

    sums = lax.fori_loop(
        0, TILES, add_up, tuple(jnp.zeros((HALF, LANES), f32) for _ in range(2 * COMPS)), unroll=4
    )
    means = [[sum_lanes(sums[half * COMPS + c]) * (1.0 / 4096.0) for c in range(COMPS)] for half in range(2)]

    wait_bytes(gathered.at[pl.ds(0, others)], gather_recv)
    moved = jnp.sum(gathered[...], axis=0)
    lane8, sub8 = iota((HALF, LANES), 1).astype(f32), iota((HALF, LANES), 0).astype(f32)
    eye8 = iota((HALF, HALF), 0) == iota((HALF, HALF), 1)
    halo_rows = halo_v[...].astype(f32)
    halo_hot = []
    for side in range(2):
        col = sum_lanes(jnp.where(eye8, jnp.broadcast_to(halo_rows[side : side + 1], (HALF, HALF)), 0.0))
        halo_hot.append(jnp.where(col == lane8, 1.0, 0.0))
    out_tile = jnp.zeros((HALF, LANES), f32)
    for side in range(2):
        for i in range(3):
            col = sum_lanes(halo_hot[side] * moved[i : i + 1])
            out_tile = jnp.where(lane8 == 3 * side + i, col, out_tile)
    halo_out[...] = out_tile

    def swap_halo(source, target, send, recv):
        @pl.when(has_below)
        def _():
            pltpu.make_async_remote_copy(
                source, target.at[1], send.at[0], recv.at[1], device_id={"mesh": part - 1}, device_id_type=MESH
            ).start()

        @pl.when(has_above)
        def _():
            pltpu.make_async_remote_copy(
                source, target.at[0], send.at[1], recv.at[0], device_id={"mesh": part + 1}, device_id_type=MESH
            ).start()

    def take_halo(source, target, recv):
        @pl.when(has_below)
        def _():
            wait_bytes(target.at[0], recv.at[0])

        @pl.when(jnp.logical_not(has_below))
        def _():
            target[0] = jnp.zeros((HALF, LANES), f32)

        @pl.when(has_above)
        def _():
            wait_bytes(target.at[1], recv.at[1])

        @pl.when(jnp.logical_not(has_above))
        def _():
            target[1] = jnp.zeros((HALF, LANES), f32)

    swap_halo(halo_out, halo_in, halo_send, halo_recv)

    sends = jnp.concatenate([gathered[s, 3:4] for s in range(n_rve)], axis=0)
    lower = jnp.where(iota((n_rve, n_rve), 1) < iota((n_rve, n_rve), 0), 1.0, 0.0).astype(bf16)
    upper = jnp.where(iota((LANES, LANES), 0) < iota((LANES, LANES), 1), 1.0, 0.0).astype(bf16)
    sends_b = sends.astype(bf16)
    order = jnp.dot(lower, sends_b, preferred_element_type=f32)
    places = jnp.dot(sends_b, upper, preferred_element_type=f32)
    rows_at = iota((n_rve, LANES), 0).astype(f32) * float(SPAN) + places
    table = jnp.zeros((HALF, LANES), f32)
    for k in range(HALF):
        row = sum_rows(jnp.where((sends > 0.5) & (order == float(k)), rows_at, 0.0))
        table = jnp.where(sub8 == float(k), row, table)
    table_v[...] = table.astype(jnp.int32)
    load_table = pltpu.make_async_copy(table_v, table_s, idx_sem.at[1])
    load_table.start()

    conn_rows = conn_v[...].astype(f32)
    own_hot, far_hot = [], []
    for e in range(2):
        col = sum_lanes(jnp.where(eye8, jnp.broadcast_to(conn_rows[e : e + 1], (HALF, HALF)), 0.0))
        own_hot.append(jnp.where(col == lane8, 1.0, 0.0))
        far_hot.append(jnp.where(col - float(LANES) == lane8, 1.0, 0.0))
    first_element = iota((HALF, 16), 1) < 8

    take_halo(halo_out, halo_in, halo_recv)
    below, above = halo_in[0], halo_in[1]
    spread_disp = []
    for i in range(3):
        far = sum_rows(jnp.where(lane8 == sub8, below[:, 3 + i : 4 + i], 0.0))
        far = far + sum_rows(jnp.where(lane8 == sub8 + 8.0, above[:, i : i + 1], 0.0))
        cols = [sum_lanes(own_hot[e] * moved[i : i + 1] + far_hot[e] * far) for e in range(2)]
        spread_disp.append(jnp.where(first_element, cols[0], cols[1]))
    grads = [grads_v[j] for j in range(3)]
    g = [[sum_rows(spread_disp[i] * grads[j]) for j in range(3)] for i in range(3)]
    macro = [
        g[0][0], g[1][1], g[2][2],
        (g[1][2] + g[2][1]) * 0.5, (g[0][2] + g[2][0]) * 0.5, (g[0][1] + g[1][0]) * 0.5,
    ]
    macro_cols = [sum_lanes(chosen * row) for row in macro]
    for c in range(COMPS):
        for half in range(2):
            col = macro_cols[c][half * HALF : (half + 1) * HALF]
            column_v[half, 0, c] = jnp.broadcast_to(col - means[half][c], (HALF, LANES))
            column_v[half, 1, c] = jnp.broadcast_to(col, (HALF, LANES))
    for half in range(2):
        column_v[half, 2, 0] = jnp.broadcast_to(count_col[half * HALF : (half + 1) * HALF], (HALF, LANES))

    big_loads[1].wait()
    big_loads[2].wait()
    odd_lane = iota((HALF, LANES), 1) >= count_paired

    def sweep(half, number):
        def polarize(u, carry):
            for b in range(2):
                cats = [[] for _ in range(COMPS)]
                for step in range(2):
                    t = (2 * u + step) * 2 + b
                    eps = [field[half, t, c * HALF : (c + 1) * HALF, :] for c in range(COMPS)]
                    if number == 0:
                        eps = [eps[c] + column_v[half, 0, c] for c in range(COMPS)]
                    lam = mod[half, t, 0:HALF, :] - 1.1
                    shear = 2.0 * mod[half, t, HALF : 2 * HALF, :] - 2.2
                    pressure = lam * (eps[0] + eps[1] + eps[2])
                    double = shear + shear
                    for c in range(3):
                        cats[c].append(shear * eps[c] + pressure)
                    for c in range(3, 6):
                        cats[c].append(double * eps[c])
                for c in range(COMPS):
                    high, low = split_bf16(jnp.concatenate(cats[c], axis=0))
                    at = pl.multiple_of(u * 16, 16)
                    tau_h[c, pl.ds(at, 16), b * LANES : (b + 1) * LANES] = high
                    tau_l[c, pl.ds(at, 16), b * LANES : (b + 1) * LANES] = low
            return carry

        lax.fori_loop(0, 8, polarize, 0, unroll=2)

        def forward(c, carry):
            planed = three_pass(tau_h[c], tau_l[c], plane_v[0], plane_v[1])
            values = [
                (planed[x * HALF : (x + 1) * HALF, :LANES], planed[x * HALF : (x + 1) * HALF, LANES:])
                for x in range(RES)
            ]
            z = sixteen_point(values, -1)
            for k in range(1, 8):
                a, b = z[k], z[RES - k]
                z[k] = (jnp.where(odd_lane, a[0] + b[0], a[0]), jnp.where(odd_lane, a[1] - b[1], a[1]))
                z[RES - k] = (jnp.where(odd_lane, a[1] + b[1], b[0]), jnp.where(odd_lane, b[0] - a[0], b[1]))
            for k in range(RES):
                spec[k, 0, c] = z[k][0]
                spec[k, 1, c] = z[k][1]
            return carry

        lax.fori_loop(0, COMPS, forward, 0, unroll=2)

        def green(k, carry):
            for part_at in range(2):
                ins = [spec[k, part_at, c] for c in range(COMPS)]
                rows = [coef_v[k, part_at, r : r + 1, :] for r in range(len(coef_rows))]
                for c in range(COMPS):
                    total = rows[coef_at[(c, 0)]] * ins[0]
                    for d in range(1, COMPS):
                        total = total + rows[coef_at[(c, d)]] * ins[d]
                    spec[k, part_at, c] = total
            return carry

        lax.fori_loop(0, RES, green, 0, unroll=2)

        def backward(c, carry):
            z = [(spec[k, 0, c], spec[k, 1, c]) for k in range(RES)]
            for k in range(1, 8):
                a, b = z[k], z[RES - k]
                z[k] = (jnp.where(odd_lane, a[0] - b[1], a[0]), jnp.where(odd_lane, a[1] + b[0], a[1]))
                z[RES - k] = (jnp.where(odd_lane, a[0] + b[1], b[0]), jnp.where(odd_lane, b[0] - a[1], b[1]))
            values = sixteen_point(z, 1)
            lined = jnp.concatenate(
                [
                    jnp.concatenate([values[x][0] for x in range(RES)], axis=0),
                    jnp.concatenate([values[x][1] for x in range(RES)], axis=0),
                ],
                axis=1,
            )
            high, low = split_bf16(lined)
            fluct = three_pass(high, low, plane_v[2], plane_v[3])
            level = column_v[half, 1, c]
            again = column_v[half, 2, 0] > float(number) + 0.5
            at = pl.multiple_of(c * HALF, HALF)
            for x in range(RES):
                for b in range(2):
                    new = level - fluct[x * HALF : (x + 1) * HALF, b * LANES : (b + 1) * LANES]
                    t = 2 * x + b
                    if number > 0:
                        new = jnp.where(again, new, field[half, t, pl.ds(at, HALF), :])
                    field[half, t, pl.ds(at, HALF), :] = new
            return carry

        lax.fori_loop(0, COMPS, backward, 0, unroll=2)

    def mean_stress(half):
        def body(t, sums):
            eps = [field[half, t, c * HALF : (c + 1) * HALF, :] for c in range(COMPS)]
            lam = mod[half, t, 0:HALF, :]
            shear = mod[half, t, HALF : 2 * HALF, :]
            new = [sums[c] + shear * eps[c] for c in range(COMPS)]
            return (*new, sums[6] + lam * (eps[0] + eps[1] + eps[2]))

        sums = lax.fori_loop(0, TILES, body, tuple(jnp.zeros((HALF, LANES), f32) for _ in range(7)), unroll=4)
        result = []
        for c in range(COMPS):
            total = 2.0 * sums[c]
            if c < 3:
                total = total + sums[6]
            result.append(sum_lanes(total) * (1.0 / 4096.0))
        return result

    def send_spread(half):
        rows = pl.multiple_of(me * SPAN, SPAN)
        got1[half][pl.ds(rows, ROWS), :] = field[half, me, pl.ds(0, ROWS), :]

        def body(k, carry):
            to = lax.rem(me + k, n_rve)
            pltpu.make_async_remote_copy(
                field.at[half, to, pl.ds(0, ROWS), :], got1[half].at[pl.ds(rows, ROWS), :], send1.at[half], recv1.at[half],
                device_id={"rve": to}, device_id_type=MESH,
            ).start()
            return carry

        lax.fori_loop(1, n_rve, body, 0)

    def send_owned(half):
        wait_bytes(got2.at[half, pl.ds(0, others)], recv1.at[half])

        def body(k, carry):
            to = lax.rem(me + k, n_rve)
            for at in range(HALF):
                row = jnp.clip(table_s[at, to], 0, last_row)
                stage[half, to, pl.ds(at, COMPS, stride=HALF), :] = got1[half][
                    pl.ds(row, COMPS, stride=HALF), :
                ]

            @pl.when(k > 0)
            def _():
                pltpu.make_async_remote_copy(
                    stage.at[half, to, pl.ds(0, ROWS), :], got2.at[half, me], send2.at[half], recv2.at[half],
                    device_id={"rve": to}, device_id_type=MESH,
                ).start()

            return carry

        lax.fori_loop(1, n_rve, body, 0)
        body(0, 0)
        keep = pltpu.make_async_copy(stage.at[half, me, pl.ds(0, ROWS), :], got2.at[half, me], in_sem.at[4 + half])
        keep.start()
        return keep

    load_table.wait()
    sweep(0, 0)
    sweep(0, 1)
    send_spread(0)
    stress = [mean_stress(0)]
    sweep(1, 0)
    keep0 = send_owned(0)
    sweep(1, 1)
    send_spread(1)
    stress.append(mean_stress(1))

    weights = weight_v[...]
    sigma = []
    for c in range(COMPS):
        col = jnp.concatenate([stress[0][c], stress[1][c]], axis=0)
        row = sum_rows(chosen * col)
        stress_o[c : c + 1, :] = row
        sigma.append(row * weights)
    grid = ((0, 5, 4), (5, 1, 3), (4, 3, 2))
    force_tile = jnp.zeros((HALF, LANES), f32)
    own_rows = []
    for i in range(3):
        point_force = sigma[grid[i][0]] * grads[0] + sigma[grid[i][1]] * grads[1] + sigma[grid[i][2]] * grads[2]
        cols = [
            sum_lanes(jnp.where(first_element, point_force, 0.0)),
            sum_lanes(jnp.where(first_element, 0.0, point_force)),
        ]
        own_rows.append(sum_rows(own_hot[0] * cols[0] + own_hot[1] * cols[1]))
        far = sum_rows(far_hot[0] * cols[0] + far_hot[1] * cols[1])
        force_tile = jnp.where(sub8 == float(i), far, force_tile)
    force_out[...] = force_tile
    swap_halo(force_out, force_in, fhalo_send, fhalo_recv)
    take_halo(force_out, force_in, fhalo_recv)
    below, above = force_in[0], force_in[1]
    own_tile = jnp.zeros((4, LANES), f32)
    for i in range(3):
        low = sum_lanes(jnp.where(lane8 == sub8 + 8.0, below[i : i + 1], 0.0))
        high = sum_lanes(jnp.where(lane8 == sub8, above[i : i + 1], 0.0))
        row = own_rows[i] + sum_rows(halo_hot[0] * low + halo_hot[1] * high)
        own_tile = jnp.where(sub4 == i, row, own_tile)
    own_out[...] = own_tile
    own_in[me] = own_tile
    to_all(own_out, own_in.at[me], own_send, own_recv)
    keep1 = send_owned(1)
    wait_bytes(own_in.at[pl.ds(0, others)], own_recv)
    total = jnp.sum(own_in[...], axis=0)
    mine = jnp.zeros((4, LANES), f32)
    for node in range(4):
        mine = jnp.where(lane4 == node, sum_lanes(jnp.where(lane4 == 4 * me + node, total, 0.0)), mine)
    nodal_o[...] = mine[:3, :4]

    keep0.wait()
    keep1.wait()
    for half in range(2):
        wait_bytes(got2.at[half, pl.ds(0, others)], recv2.at[half])
    wait_bytes(gathered.at[pl.ds(0, others)], gather_send)
    wait_bytes(own_in.at[pl.ds(0, others)], own_send)
    for half in range(2):
        wait_bytes(got2.at[half, pl.ds(0, others)], send1.at[half])
        wait_bytes(got2.at[half, pl.ds(0, others)], send2.at[half])
    for send, source in ((halo_send, halo_out), (fhalo_send, force_out)):
        @pl.when(has_below)
        def _(send=send, source=source):
            wait_bytes(source, send.at[0])

        @pl.when(has_above)
        def _(send=send, source=source):
            wait_bytes(source, send.at[1])


def lay_out_kernel(got_h, nodal_ref, stress_ref, out_h, nodal_o, stress_o, taken, mixed, in_sem, out_sem):
    parts = taken.shape[0]
    group = TILES // parts

    def copy_in(at):
        return pltpu.make_async_copy(got_h.at[:, pl.ds(at * group, group)], taken.at[at], in_sem.at[at])

    def copy_out(t):
        return pltpu.make_async_copy(
            mixed.at[t, pl.ds(0, 2 * ROWS), :], out_h.at[:, pl.ds(t * LANES, LANES)], out_sem.at[t]
        )

    for at in range(parts):
        copy_in(at).start()
    nodal_o[...] = nodal_ref[...]
    stress_o[...] = stress_ref[...]
    for at in range(parts):
        copy_in(at).wait()
        for t in range(group):
            for c in range(COMPS):
                for half in range(2):
                    mixed[at * group + t, pl.ds(2 * HALF * c + half, HALF, stride=2), :] = taken[
                        at, half, t, c * HALF : (c + 1) * HALF, :
                    ]
            copy_out(at * group + t).start()
    for t in range(TILES):
        copy_out(t).wait()


def lay_out(got, nodal, stress):
    parts = 8
    vmem = pl.BlockSpec(memory_space=pltpu.VMEM)
    hbm = pl.BlockSpec(memory_space=pltpu.HBM)
    return pl.pallas_call(
        lay_out_kernel,
        in_specs=[hbm, vmem, vmem],
        out_specs=[hbm, vmem, vmem],
        out_shape=[
            jax.ShapeDtypeStruct((2 * ROWS, TILES * LANES), f32),
            jax.ShapeDtypeStruct(nodal.shape, f32),
            jax.ShapeDtypeStruct(stress.shape, f32),
        ],
        scratch_shapes=[
            pltpu.VMEM((parts, 2, TILES // parts, ROWS, LANES), f32),
            pltpu.VMEM((TILES, 2 * ROWS + 8, LANES), f32),
            pltpu.SemaphoreType.DMA((parts,)),
            pltpu.SemaphoreType.DMA((TILES,)),
        ],
        compiler_params=pltpu.CompilerParams(vmem_limit_bytes=63 * 1024 * 1024),
        name="lay_out",
    )(got, nodal, stress)


def solution(mesh):
    n_rve, n_mesh = mesh.shape["rve"], mesh.shape["mesh"]
    planes, coef, count_paired = tables()

    def on_device(displacement, shape_grads, point_weights, conn, halo_nodes, warm_strain, moduli, owner, sweeps):
        points, voxels = warm_strain.shape[0], warm_strain.shape[2]
        warm = warm_strain.transpose(1, 0, 2).reshape(COMPS * points, voxels)
        vmem = pl.BlockSpec(memory_space=pltpu.VMEM)
        hbm = pl.BlockSpec(memory_space=pltpu.HBM)
        dma = pltpu.SemaphoreType.DMA
        scratch = [
            pltpu.VMEM((TILES, 8 * points, LANES), f32),
            pltpu.VMEM((points, 2, voxels), f32),
            pltpu.VMEM(planes.shape, bf16),
            pltpu.VMEM(coef.shape, f32),
            pltpu.VMEM((2, TILES, SPAN, LANES), f32),
            pltpu.VMEM((2, TILES, SPAN, LANES), f32),
            pltpu.VMEM((COMPS, RES * HALF, PLANE), bf16),
            pltpu.VMEM((COMPS, RES * HALF, PLANE), bf16),
            pltpu.VMEM((RES, 2, COMPS, HALF, LANES), f32),
            pltpu.VMEM((n_rve * SPAN, LANES), f32),
            pltpu.VMEM((n_rve * SPAN, LANES), f32),
            pltpu.VMEM((2, n_rve, SPAN, LANES), f32),
            pltpu.VMEM((4, LANES), f32),
            pltpu.VMEM((n_rve, 4, LANES), f32),
            pltpu.VMEM((HALF, LANES), f32),
            pltpu.VMEM((2, HALF, LANES), f32),
            pltpu.VMEM((HALF, LANES), f32),
            pltpu.VMEM((2, HALF, LANES), f32),
            pltpu.VMEM((4, LANES), f32),
            pltpu.VMEM((n_rve, 4, LANES), f32),
            pltpu.VMEM((16, LANES), jnp.int32),
            pltpu.SMEM((16, LANES), jnp.int32),
            pltpu.VMEM((HALF, LANES), jnp.int32),
            pltpu.SMEM((HALF, LANES), jnp.int32),
            pltpu.VMEM((2, 3, COMPS, HALF, LANES), f32),
            pltpu.SMEM((3, 4), f32),
            pltpu.VMEM(shape_grads.shape, f32),
            pltpu.VMEM((1, points), f32),
            pltpu.VMEM((2, 8), jnp.int32),
            pltpu.VMEM((2, 8), jnp.int32),
            pltpu.VMEM((1, points), jnp.int32),
            pltpu.VMEM((1, points), jnp.int32),
            dma((7,)),
            dma((6,)), dma((2,)), dma, dma, dma((2,)), dma((2,)),
            dma((2,)), dma((2,)), dma((2,)), dma((2,)), dma((2,)), dma((2,)), dma, dma,
        ]
        nodal, stress, got = pl.pallas_call(
            functools.partial(main_kernel, count_paired, n_rve, n_mesh),
            in_specs=[hbm] * 11,
            out_specs=[vmem, vmem, hbm],
            out_shape=[
                jax.ShapeDtypeStruct((3, 4), f32),
                jax.ShapeDtypeStruct((COMPS, points), f32),
                jax.ShapeDtypeStruct((2, n_rve, ROWS, LANES), f32),
            ],
            scratch_shapes=scratch,
            compiler_params=pltpu.CompilerParams(
                collective_id=0, has_side_effects=True, vmem_limit_bytes=63 * 1024 * 1024
            ),
            name="solve_and_exchange",
        )(
            displacement, shape_grads, point_weights.reshape(1, points), conn.T, halo_nodes,
            owner.reshape(1, points), sweeps.reshape(1, points), warm, moduli,
            jnp.asarray(planes), jnp.asarray(coef),
        )
        micro, nodal, stress = lay_out(got, nodal, stress)
        micro = micro.reshape(COMPS, points, voxels).transpose(1, 0, 2)
        return nodal, stress, micro

    both = ("mesh", "rve")
    in_specs = (
        P(None, both), P(None, None, both), P(both), P(None, both), P(None, "mesh"),
        P(both, None, None), P(both, None, None), P(both), P(both),
    )
    out_specs = (P(None, both), P(None, both), P(both, None, None))
    return jax.shard_map(on_device, mesh=mesh, in_specs=in_specs, out_specs=out_specs, check_vma=False)
```

```python
import functools
import math

import jax
import jax.numpy as jnp
import numpy as np
from jax import lax
from jax.experimental import pallas as pl
from jax.experimental.pallas import tpu as pltpu
from jax.sharding import PartitionSpec as P

RES = 16
PLANE = 256
LANES = 128
TILES = 32
COMPS = 6
HALF = 8
ROWS = COMPS * HALF
SPAN = 8 * HALF
SENT = 4 * HALF
SHORT = 3 * HALF
EXTRA = 13
MIXED_LANE = 112
ENCODE, CHOOSE, DECODE, TABLE_ROWS = 21, 39, 41, 56
MESH = pl.DeviceIdType.MESH
f32 = jnp.float32
bf16 = jnp.bfloat16
index_pairs = ((0, 0), (1, 1), (2, 2), (1, 2), (0, 2), (0, 1))
coef_rows = [(c, d) for c in range(6) for d in range(c, 6)]
coef_at = {}
for _at, (_c, _d) in enumerate(coef_rows):
    coef_at[(_c, _d)] = _at
    coef_at[(_d, _c)] = _at


def half_planes():
    own = [(0, 0), (0, 8), (8, 0), (8, 8)]
    pairs, seen = [], set(own)
    for y in range(RES):
        for z in range(RES):
            if (y, z) not in seen:
                seen.add((y, z))
                seen.add(((-y) % RES, (-z) % RES))
                pairs.append((y, z))
    pairs.sort(key=lambda q: RES // 2 in q)
    lane_a = pairs + [(0, 0), (0, 8)]
    lane_b = pairs + [(8, 0), (8, 8)]
    return np.array(lane_a), np.array(lane_b), len(pairs)


def green_matrix(kx, ky, kz):
    def one(x, y, z):
        k = np.stack([x % RES, y % RES, z % RES]).astype(np.int64)
        xi = np.where(k < RES // 2, k, k - RES).astype(np.float64)
        size = np.sqrt((xi * xi).sum(0))
        n = np.where(size > 0, xi / np.where(size > 0, size, 1.0), 0.0)
        out = np.zeros((6, 6) + size.shape)
        for d, (i, j) in enumerate(index_pairs):
            t = np.zeros((3,) + size.shape)
            t[i] += n[j]
            if i != j:
                t[j] += n[i]
            s = (n * t).sum(0)
            weight = 1.0 if i == j else 2.0
            for c, (k_, h_) in enumerate(index_pairs):
                value = (n[k_] * t[h_] + n[h_] * t[k_]) / 2.2
                value = value - (2.2 / (1.1 * 3.3)) * n[k_] * n[h_] * s
                out[c, d] = value / weight
        return out

    return 0.5 * (one(kx, ky, kz) + one(-kx, -ky, -kz))


def transport_rows(k):
    xi = np.array([i if i < RES // 2 else i - RES for i in k], np.float64)
    size = np.sqrt((xi * xi).sum())
    n = xi / size if size > 0 else xi
    edge = [i == RES // 2 for i in k]
    back = np.zeros((6, 3))
    mixed = {}
    for c, (i, j) in enumerate(index_pairs):
        if i == j:
            back[c, i] = n[i]
        elif edge[i] == edge[j]:
            back[c, i], back[c, j] = 0.5 * n[j], 0.5 * n[i]
        else:
            mixed[c] = True
    rows = np.zeros(TABLE_ROWS)
    into = np.linalg.pinv(back)
    rows[ENCODE : ENCODE + 18] = into.reshape(-1)
    first, second = (sorted(mixed, reverse=True) + [5, 4])[:2]
    rows[CHOOSE], rows[CHOOSE + 1] = float(first == 5), float(second == 4)
    rows[DECODE : DECODE + 3] = n
    rows[DECODE + 3 : DECODE + 9] = back[3, 1], back[3, 2], back[4, 0], back[4, 2], back[5, 0], back[5, 1]
    if mixed:
        rows[DECODE + 9] = float(first == 5)
        rows[DECODE + 10] = float(first == 4)
        rows[DECODE + 11] = float(second == 4)
        rows[DECODE + 12] = float(second == 3)
    return rows


@functools.lru_cache(None)
def tables():
    lane_a, lane_b, count = half_planes()
    v = np.arange(PLANE)
    vy, vz = v // RES, v % RES
    angle = 2.0 * math.pi / RES

    def phase(lane):
        return angle * ((np.outer(vy, lane[:, 0]) + np.outer(vz, lane[:, 1])) % RES)

    paired = (np.arange(LANES) < count)[None, :]
    forward = np.concatenate(
        [np.cos(phase(lane_a)), np.where(paired, -np.sin(phase(lane_b)), np.cos(phase(lane_b)))], axis=1
    )
    coef = np.zeros((RES, 2, TABLE_ROWS, LANES))
    moved_by = functools.lru_cache(None)(transport_rows)
    for slot in range(RES):
        for part in range(2):
            ky, kz, kx, scale = [], [], [], []
            for lane in range(LANES):
                if lane < count:
                    y, z, x, weight = *lane_a[lane], slot, 2.0
                elif slot in (0, RES // 2):
                    y, z = lane_a[lane] if part == 0 else lane_b[lane]
                    x, weight = slot, 1.0
                else:
                    y, z = lane_a[lane] if slot < RES // 2 else lane_b[lane]
                    x, weight = (slot if slot < RES // 2 else RES - slot), 0.5
                ky.append(y), kz.append(z), kx.append(x), scale.append(weight / RES**3)
            for lane in range(LANES):
                coef[slot, part, :, lane] = moved_by((kx[lane] % RES, int(ky[lane]) % RES, int(kz[lane]) % RES))
            matrix = green_matrix(np.array(kx), np.array(ky), np.array(kz)) * np.array(scale)
            for row, (c, d) in enumerate(coef_rows):
                coef[slot, part, row] = matrix[c, d]

    def split(table):
        high = jnp.asarray(table, f32).astype(bf16)
        low = (np.asarray(table, np.float64) - np.asarray(high).astype(np.float64)).astype(np.float32)
        return np.asarray(high), np.asarray(jnp.asarray(low).astype(bf16))

    with jax.ensure_compile_time_eval():
        fh, fl = split(forward)
        ih, il = split(forward.T)
    return np.stack([fh, fl, ih, il]), coef.astype(np.float32), count


def complex_mul(a, b):
    re, im = a
    cr, ci = b
    if abs(ci) < 1e-12 and abs(cr - 1) < 1e-12:
        return a
    if abs(cr) < 1e-12:
        return (im, -re) if ci < 0 else (-im, re)
    if abs(abs(cr) - abs(ci)) < 1e-12:
        h = abs(cr)
        sr, si = cr > 0, ci > 0
        if sr and not si:
            return (h * (re + im), h * (im - re))
        if not sr and not si:
            return (h * (im - re), -h * (re + im))
        if sr and si:
            return (h * (re - im), h * (im + re))
        return (-h * (re + im), h * (re - im))
    return (cr * re - ci * im, cr * im + ci * re)


def four_point(a, b, c, d, sign):
    s0 = (a[0] + c[0], a[1] + c[1])
    s1 = (a[0] - c[0], a[1] - c[1])
    s2 = (b[0] + d[0], b[1] + d[1])
    s3 = (b[0] - d[0], b[1] - d[1])
    turned = (s3[1], -s3[0]) if sign < 0 else (-s3[1], s3[0])
    return (
        (s0[0] + s2[0], s0[1] + s2[1]),
        (s1[0] + turned[0], s1[1] + turned[1]),
        (s0[0] - s2[0], s0[1] - s2[1]),
        (s1[0] - turned[0], s1[1] - turned[1]),
    )


def sixteen_point(values, sign):
    columns = []
    for r in range(4):
        out = four_point(values[r], values[r + 4], values[r + 8], values[r + 12], sign)
        columns.append(
            [
                complex_mul(out[k], (math.cos(2 * math.pi * r * k / 16), sign * math.sin(2 * math.pi * r * k / 16)))
                for k in range(4)
            ]
        )
    result = [None] * 16
    for k in range(4):
        out = four_point(columns[0][k], columns[1][k], columns[2][k], columns[3][k], sign)
        for m in range(4):
            result[k + 4 * m] = out[m]
    return result


def iota(shape, dim):
    return lax.broadcasted_iota(jnp.int32, shape, dim)


def sum_lanes(x):
    return jnp.sum(x, axis=1, keepdims=True)


def sum_rows(x):
    return jnp.sum(x, axis=0, keepdims=True)


def split_bf16(x):
    high = x.astype(bf16)
    low = (x - high.astype(f32)).astype(bf16)
    return high, low


def three_pass(high, low, table_high, table_low):
    def dot(a, b):
        return jnp.dot(a, b, preferred_element_type=f32)

    return dot(high, table_high) + (dot(low, table_high) + dot(high, table_low))


def main_kernel(
    count_paired, n_rve, n_mesh,
    disp_h, grads_h, weight_h, conn_h, halo_h, owner_h, sweeps_h, warm_h, moduli_h, plane_h, coef_h,
    nodal_o, stress_o, out_h,
    warm_v, moduli_v, plane_v, coef_v, field, mod, tau_h, tau_l, spec_a, spec_b, payload, got1_a, got1_b, got2, mixed, sums_v, stage,
    tile_v, gathered, halo_out, halo_in, force_out, force_in, own_out, own_in,
    perm_v, perm_s, table_v, table_s, column_v,
    disp_s, grads_v, weight_v, conn_v, halo_v, owner_v, sweeps_v, small_sem,
    in_sem, out_sem, idx_sem, gather_send, gather_recv, halo_send, halo_recv,
    send1, recv1, send2, recv2, fhalo_send, fhalo_recv, own_send, own_recv,
):
    me = lax.axis_index("rve")
    part = lax.axis_index("mesh")
    others = n_rve - 1
    got1 = (got1_a, got1_b)
    last_row = others * SENT + HALF - 1
    has_below = part > 0
    has_above = part < n_mesh - 1

    small = [
        pltpu.make_async_copy(source, target, small_sem.at[at])
        for at, (source, target) in enumerate((
            (owner_h, owner_v), (sweeps_h, sweeps_v), (disp_h, disp_s), (halo_h, halo_v),
            (conn_h, conn_v), (grads_h, grads_v), (weight_h, weight_v),
        ))
    ]
    for load in small:
        load.start()

    def load_tile(t):
        at = pl.multiple_of(t * LANES, LANES)
        return pltpu.make_async_copy(
            warm_h.at[:, pl.ds(at, LANES)], warm_v.at[t, pl.ds(0, COMPS * 16), :], in_sem.at[0]
        )

    def start_tile(t, carry):
        load_tile(t).start()
        return carry

    lax.fori_loop(0, TILES, start_tile, 0)
    big_loads = [
        pltpu.make_async_copy(moduli_h, moduli_v, in_sem.at[1]),
        pltpu.make_async_copy(plane_h, plane_v, in_sem.at[2]),
        pltpu.make_async_copy(coef_h, coef_v, in_sem.at[3]),
    ]
    for load in big_loads:
        load.start()

    barrier = pltpu.get_barrier_semaphore()

    def greet(k, carry):
        pl.semaphore_signal(barrier, inc=1, device_id={"rve": lax.rem(me + k, n_rve)}, device_id_type=MESH)
        return carry

    lax.fori_loop(1, n_rve, greet, 0)

    @pl.when(has_below)
    def _():
        pl.semaphore_signal(barrier, inc=1, device_id={"mesh": part - 1}, device_id_type=MESH)

    @pl.when(has_above)
    def _():
        pl.semaphore_signal(barrier, inc=1, device_id={"mesh": part + 1}, device_id_type=MESH)

    for load in small:
        load.wait()

    owner_row = owner_v[...].astype(f32)
    sub16, lane16 = iota((16, 16), 0), iota((16, 16), 1)
    owner_col = sum_lanes(jnp.where(sub16 == lane16, jnp.broadcast_to(owner_row, (16, 16)), 0.0))
    place = 0.5 * sum_rows(jnp.where(owner_col < owner_row, 1.0, 0.0))
    rank = sum_rows(jnp.where((owner_col == owner_row) & (sub16 < lane16), 1.0, 0.0))
    slot_row = 8.0 * rank + place
    chosen = jnp.where(slot_row == sub16.astype(f32), 1.0, 0.0)
    perm_col = sum_lanes(chosen * lane16.astype(f32))
    perm_v[...] = jnp.broadcast_to(perm_col, (16, LANES)).astype(jnp.int32)
    count_col = sum_lanes(chosen * sweeps_v[...].astype(f32))
    load_perm = pltpu.make_async_copy(perm_v, perm_s, idx_sem.at[0])
    load_perm.start()

    lane_row = iota((1, LANES), 1).astype(f32)
    sends_row = 0.5 * sum_rows(jnp.where(owner_col == lane_row, 1.0, 0.0))
    sub4, lane4 = iota((4, LANES), 0), iota((4, LANES), 1)
    tile = jnp.where(sub4 == 3, sends_row, 0.0)
    for i in range(3):
        for node in range(4):
            tile = jnp.where((sub4 == i) & (lane4 == 4 * me + node), disp_s[i, node], tile)
    tile_v[...] = tile
    gathered[me] = tile

    extra = jnp.where(has_below, 1, 0) + jnp.where(has_above, 1, 0)
    pl.semaphore_wait(barrier, others + extra)

    def to_all(source, target, send, recv):
        def body(k, carry):
            to = lax.rem(me + k, n_rve)
            pltpu.make_async_remote_copy(
                source, target, send, recv, device_id={"rve": to}, device_id_type=MESH
            ).start()
            return carry

        lax.fori_loop(1, n_rve, body, 0)

    def wait_bytes(view, sem):
        pltpu.make_async_copy(view, view, sem).wait()

    to_all(tile_v, gathered.at[me], gather_send, gather_recv)

    load_perm.wait()
    big_loads[0].wait()

    wait_bytes(warm_v.at[:, pl.ds(0, COMPS * 16), :], in_sem.at[0])
    places_at = [
        (half, pos, jnp.clip(perm_s[half * HALF + pos, 0], 0, 15)) for half in range(2) for pos in range(HALF)
    ]

    def place_tile(t, carry):
        at = pl.multiple_of(t * LANES, LANES)
        for half, pos, point in places_at:
            field[half, t, pl.ds(pos, COMPS, stride=HALF), :] = warm_v[t, pl.ds(point, COMPS, stride=16), :]
            mod[half, t, pl.ds(pos, 2, stride=HALF), :] = moduli_v[point, :, pl.ds(at, LANES)]
        return carry

    lax.fori_loop(0, TILES, place_tile, 0)

    def add_up(t, sums):
        return tuple(
            sums[half * COMPS + c] + field[half, t, c * HALF : (c + 1) * HALF, :]
            for half in range(2)
            for c in range(COMPS)
        )

    sums = lax.fori_loop(
        0, TILES, add_up, tuple(jnp.zeros((HALF, LANES), f32) for _ in range(2 * COMPS)), unroll=4
    )
    means = [[sum_lanes(sums[half * COMPS + c]) * (1.0 / 4096.0) for c in range(COMPS)] for half in range(2)]

    wait_bytes(gathered.at[pl.ds(0, others)], gather_recv)
    moved = jnp.sum(gathered[...], axis=0)
    lane8, sub8 = iota((HALF, LANES), 1).astype(f32), iota((HALF, LANES), 0).astype(f32)
    eye8 = iota((HALF, HALF), 0) == iota((HALF, HALF), 1)
    halo_rows = halo_v[...].astype(f32)
    halo_hot = []
    for side in range(2):
        col = sum_lanes(jnp.where(eye8, jnp.broadcast_to(halo_rows[side : side + 1], (HALF, HALF)), 0.0))
        halo_hot.append(jnp.where(col == lane8, 1.0, 0.0))
    out_tile = jnp.zeros((HALF, LANES), f32)
    for side in range(2):
        for i in range(3):
            col = sum_lanes(halo_hot[side] * moved[i : i + 1])
            out_tile = jnp.where(lane8 == 3 * side + i, col, out_tile)
    halo_out[...] = out_tile

    def swap_halo(source, target, send, recv):
        @pl.when(has_below)
        def _():
            pltpu.make_async_remote_copy(
                source, target.at[1], send.at[0], recv.at[1], device_id={"mesh": part - 1}, device_id_type=MESH
            ).start()

        @pl.when(has_above)
        def _():
            pltpu.make_async_remote_copy(
                source, target.at[0], send.at[1], recv.at[0], device_id={"mesh": part + 1}, device_id_type=MESH
            ).start()

    def take_halo(source, target, recv):
        @pl.when(has_below)
        def _():
            wait_bytes(target.at[0], recv.at[0])

        @pl.when(jnp.logical_not(has_below))
        def _():
            target[0] = jnp.zeros((HALF, LANES), f32)

        @pl.when(has_above)
        def _():
            wait_bytes(target.at[1], recv.at[1])

        @pl.when(jnp.logical_not(has_above))
        def _():
            target[1] = jnp.zeros((HALF, LANES), f32)

    swap_halo(halo_out, halo_in, halo_send, halo_recv)

    sends = jnp.concatenate([gathered[s, 3:4] for s in range(n_rve)], axis=0)
    lower = jnp.where(iota((n_rve, n_rve), 1) < iota((n_rve, n_rve), 0), 1.0, 0.0).astype(bf16)
    upper = jnp.where(iota((LANES, LANES), 0) < iota((LANES, LANES), 1), 1.0, 0.0).astype(bf16)
    sends_b = sends.astype(bf16)
    order = jnp.dot(lower, sends_b, preferred_element_type=f32)
    places = jnp.dot(sends_b, upper, preferred_element_type=f32)
    rows_at = iota((n_rve, LANES), 0).astype(f32) * float(SENT) + places
    table = jnp.zeros((HALF, LANES), f32)
    for k in range(HALF):
        row = sum_rows(jnp.where((sends > 0.5) & (order == float(k)), rows_at, 0.0))
        table = jnp.where(sub8 == float(k), row, table)
    table_v[...] = table.astype(jnp.int32)
    load_table = pltpu.make_async_copy(table_v, table_s, idx_sem.at[1])
    load_table.start()

    conn_rows = conn_v[...].astype(f32)
    own_hot, far_hot = [], []
    for e in range(2):
        col = sum_lanes(jnp.where(eye8, jnp.broadcast_to(conn_rows[e : e + 1], (HALF, HALF)), 0.0))
        own_hot.append(jnp.where(col == lane8, 1.0, 0.0))
        far_hot.append(jnp.where(col - float(LANES) == lane8, 1.0, 0.0))
    first_element = iota((HALF, 16), 1) < 8

    take_halo(halo_out, halo_in, halo_recv)
    below, above = halo_in[0], halo_in[1]
    spread_disp = []
    for i in range(3):
        far = sum_rows(jnp.where(lane8 == sub8, below[:, 3 + i : 4 + i], 0.0))
        far = far + sum_rows(jnp.where(lane8 == sub8 + 8.0, above[:, i : i + 1], 0.0))
        cols = [sum_lanes(own_hot[e] * moved[i : i + 1] + far_hot[e] * far) for e in range(2)]
        spread_disp.append(jnp.where(first_element, cols[0], cols[1]))
    grads = [grads_v[j] for j in range(3)]
    g = [[sum_rows(spread_disp[i] * grads[j]) for j in range(3)] for i in range(3)]
    macro = [
        g[0][0], g[1][1], g[2][2],
        (g[1][2] + g[2][1]) * 0.5, (g[0][2] + g[2][0]) * 0.5, (g[0][1] + g[1][0]) * 0.5,
    ]
    macro_cols = [sum_lanes(chosen * row) for row in macro]
    for c in range(COMPS):
        for half in range(2):
            col = macro_cols[c][half * HALF : (half + 1) * HALF]
            column_v[half, 0, c] = jnp.broadcast_to(col - means[half][c], (HALF, LANES))
            column_v[half, 1, c] = jnp.broadcast_to(col, (HALF, LANES))
    for half in range(2):
        column_v[half, 2, 0] = jnp.broadcast_to(count_col[half * HALF : (half + 1) * HALF], (HALF, LANES))

    big_loads[1].wait()
    big_loads[2].wait()
    odd_lane = iota((HALF, LANES), 1) >= count_paired

    def table_row(k, part_at, row):
        return coef_v[k, part_at, row : row + 1, :]

    def spectrum_of(half, number, spec):
        def polarize(u, carry):
            for b in range(2):
                cats = [[] for _ in range(COMPS)]
                for step in range(2):
                    t = (2 * u + step) * 2 + b
                    eps = [field[half, t, c * HALF : (c + 1) * HALF, :] for c in range(COMPS)]
                    if number == 0:
                        eps = [eps[c] + column_v[half, 0, c] for c in range(COMPS)]
                    lam = mod[half, t, 0:HALF, :] - 1.1
                    shear = 2.0 * mod[half, t, HALF : 2 * HALF, :] - 2.2
                    pressure = lam * (eps[0] + eps[1] + eps[2])
                    double = shear + shear
                    for c in range(3):
                        cats[c].append(shear * eps[c] + pressure)
                    for c in range(3, 6):
                        cats[c].append(double * eps[c])
                for c in range(COMPS):
                    high, low = split_bf16(jnp.concatenate(cats[c], axis=0))
                    at = pl.multiple_of(u * 16, 16)
                    tau_h[c, pl.ds(at, 16), b * LANES : (b + 1) * LANES] = high
                    tau_l[c, pl.ds(at, 16), b * LANES : (b + 1) * LANES] = low
            return carry

        lax.fori_loop(0, 8, polarize, 0, unroll=2)

        def forward(c, carry):
            planed = three_pass(tau_h[c], tau_l[c], plane_v[0], plane_v[1])
            values = [
                (planed[x * HALF : (x + 1) * HALF, :LANES], planed[x * HALF : (x + 1) * HALF, LANES:])
                for x in range(RES)
            ]
            z = sixteen_point(values, -1)
            for k in range(1, 8):
                a, b = z[k], z[RES - k]
                z[k] = (jnp.where(odd_lane, a[0] + b[0], a[0]), jnp.where(odd_lane, a[1] - b[1], a[1]))
                z[RES - k] = (jnp.where(odd_lane, a[1] + b[1], b[0]), jnp.where(odd_lane, b[0] - a[0], b[1]))
            for k in range(RES):
                spec[k, 0, c] = z[k][0]
                spec[k, 1, c] = z[k][1]
            return carry

        lax.fori_loop(0, COMPS, forward, 0, unroll=2)

        def green(k, carry):
            again = column_v[half, 2, 0] > float(number) + 0.5
            for part_at in range(2):
                ins = [spec[k, part_at, c] for c in range(COMPS)]
                rows = [table_row(k, part_at, r) for r in range(len(coef_rows))]
                for c in range(COMPS):
                    total = rows[coef_at[(c, 0)]] * ins[0]
                    for d in range(1, COMPS):
                        total = total + rows[coef_at[(c, d)]] * ins[d]
                    if number > 0:
                        total = jnp.where(again, total, spec_a[k, part_at, c])
                    spec[k, part_at, c] = total
            return carry

        lax.fori_loop(0, RES, green, 0, unroll=2)

    def strain_from(half, spec, take):
        def backward(c, carry):
            z = [(spec[k, 0, c], spec[k, 1, c]) for k in range(RES)]
            for k in range(1, 8):
                a, b = z[k], z[RES - k]
                z[k] = (jnp.where(odd_lane, a[0] - b[1], a[0]), jnp.where(odd_lane, a[1] + b[0], a[1]))
                z[RES - k] = (jnp.where(odd_lane, a[0] + b[1], b[0]), jnp.where(odd_lane, b[0] - a[1], b[1]))
            values = sixteen_point(z, 1)
            lined = jnp.concatenate(
                [
                    jnp.concatenate([values[x][0] for x in range(RES)], axis=0),
                    jnp.concatenate([values[x][1] for x in range(RES)], axis=0),
                ],
                axis=1,
            )
            high, low = split_bf16(lined)
            fluct = three_pass(high, low, plane_v[2], plane_v[3])
            level = column_v[half, 1, c]
            take(
                c,
                [
                    level - fluct[t // 2 * HALF : (t // 2 + 1) * HALF, t % 2 * LANES : (t % 2 + 1) * LANES]
                    for t in range(TILES)
                ],
            )
            return carry

        lax.fori_loop(0, COMPS, backward, 0, unroll=2)

    def keep_field(half):
        def take(c, tiles):
            at = pl.multiple_of(c * HALF, HALF)
            for t in range(TILES):
                field[half, t, pl.ds(at, HALF), :] = tiles[t]

        strain_from(half, spec_a, take)

    def mean_stress(half):
        def take(c, tiles):
            for which in range(2):
                parts = [
                    mod[half, t, which * HALF : (which + 1) * HALF, :] * tiles[t] for t in range(TILES)
                ]
                while len(parts) > 1:
                    parts = [p + q for p, q in zip(parts[::2], parts[1::2])]
                sums_v[which, c] = parts[0]

        strain_from(half, spec_b, take)
        pressure = sums_v[0, 0] + sums_v[0, 1] + sums_v[0, 2]
        result = []
        for c in range(COMPS):
            total = 2.0 * sums_v[1, c]
            if c < 3:
                total = total + pressure
            result.append(sum_lanes(total) * (1.0 / 4096.0))
        return result

    packed_group = iota((HALF, LANES), 1) // 16

    def encode(half):
        def extras(k, part_at, eps):
            first = jnp.where(table_row(k, part_at, CHOOSE) > 0.5, eps[5], eps[4])
            second = jnp.where(table_row(k, part_at, CHOOSE + 1) > 0.5, eps[4], eps[3])
            return first, second

        def body(i, carry):
            packed = jnp.zeros((HALF, LANES), f32)
            for step in range(2):
                k = 2 * i + step
                for part_at in range(2):
                    eps = [spec_b[k, part_at, c] for c in range(COMPS)]
                    for j in range(3):
                        total = table_row(k, part_at, ENCODE + 6 * j) * eps[0]
                        for c in range(1, COMPS):
                            total = total + table_row(k, part_at, ENCODE + 6 * j + c) * eps[c]
                        payload[half, 2 * k + part_at, j * HALF : (j + 1) * HALF, :] = total
                    for e, value in enumerate(extras(k, part_at, eps)):
                        piece = (2 * step + part_at) * 2 + e
                        shift = (16 * piece + 16) % LANES
                        if shift:
                            value = pltpu.roll(value, shift, 1)
                        packed = jnp.where(packed_group == piece, value, packed)
            payload[half, i, SHORT:SENT, :] = packed
            return carry

        lax.fori_loop(0, 8, body, 0)
        for part_at in range(2):
            eps = [spec_b[RES // 2, part_at, c] for c in range(COMPS)]
            for e, value in enumerate(extras(RES // 2, part_at, eps)):
                payload[half, 8 + 2 * part_at + e, SHORT:SENT, :] = value
        levels = jnp.zeros((HALF, LANES), f32)
        for c in range(COMPS):
            levels = jnp.where(lane8 == float(c), column_v[half, 1, c], levels)
        payload[half, EXTRA - 1, SHORT:SENT, :] = levels

    def decode(half):
        def restore(k, part_at, first, second):
            d = [got2[half, 2 * k + part_at, j * HALF : (j + 1) * HALF, :] for j in range(3)]
            row = [table_row(k, part_at, DECODE + r) for r in range(13)]
            for c in range(3):
                spec_a[k, part_at, c] = row[c] * d[c]
            spec_a[k, part_at, 3] = row[3] * d[1] + row[4] * d[2] + row[12] * second
            spec_a[k, part_at, 4] = row[5] * d[0] + row[6] * d[2] + (row[10] * first + row[11] * second)
            spec_a[k, part_at, 5] = row[7] * d[0] + row[8] * d[1] + row[9] * first

        def body(i, carry):
            packed = got2[half, i, SHORT:SENT, :]
            for step in range(2):
                for part_at in range(2):
                    values = []
                    for e in range(2):
                        piece = (2 * step + part_at) * 2 + e
                        shift = (LANES - (16 * piece + 16) % LANES) % LANES
                        values.append(pltpu.roll(packed, shift, 1) if shift else packed)
                    restore(2 * i + step, part_at, *values)
            return carry

        lax.fori_loop(0, 8, body, 0)
        for part_at in range(2):
            restore(
                RES // 2, part_at,
                got2[half, 8 + 2 * part_at, SHORT:SENT, :], got2[half, 9 + 2 * part_at, SHORT:SENT, :],
            )
        levels = got2[half, EXTRA - 1, SHORT:SENT, :]
        for c in range(COMPS):
            column_v[half, 1, c] = jnp.broadcast_to(levels[:, c : c + 1], (HALF, LANES))

        def take(c, tiles):
            at = pl.multiple_of(c * 2 * HALF, 2 * HALF)
            for t in range(TILES):
                mixed[t, pl.ds(at + half, HALF, stride=2), :] = tiles[t]

        strain_from(half, spec_a, take)

    long_rows = jnp.where(me < EXTRA, 1, 0) == 1

    def by_me(action):
        @pl.when(long_rows)
        def _():
            action(SENT)

        @pl.when(jnp.logical_not(long_rows))
        def _():
            action(SHORT)

    def wait_mine(sem):
        by_me(lambda rows: wait_bytes(got2.at[0, pl.ds(0, others), pl.ds(0, rows), :], sem))

    def wait_all(sem):
        full = EXTRA * SENT + (n_rve - EXTRA) * SHORT
        by_me(lambda rows: wait_bytes(got1_a.at[pl.ds(0, full - rows), :], sem))

    def send_spread(half):
        at = pl.multiple_of(me * SENT, SENT)
        for j in range(4):
            rows = pl.multiple_of(me * SENT + j * HALF, HALF)
            got1[half][pl.ds(rows, HALF), :] = payload[half, me, j * HALF : (j + 1) * HALF, :]

        def body(k, carry):
            to = lax.rem(me + k, n_rve)

            def send(rows):
                pltpu.make_async_remote_copy(
                    payload.at[half, to, pl.ds(0, rows), :], got1[half].at[pl.ds(at, rows), :],
                    send1.at[half], recv1.at[half], device_id={"rve": to}, device_id_type=MESH,
                ).start()

            @pl.when(to < EXTRA)
            def _():
                send(SENT)

            @pl.when(to >= EXTRA)
            def _():
                send(SHORT)

            return carry

        lax.fori_loop(1, n_rve, body, 0)

    def send_owned(half):
        wait_mine(recv1.at[half])

        def collect(to):
            for at in range(HALF):
                row = jnp.clip(table_s[at, to], 0, last_row)
                stage[half, to, pl.ds(at, 4, stride=HALF), :] = got1[half][pl.ds(row, 4, stride=HALF), :]

        def body(k, carry):
            to = lax.rem(me + k, n_rve)
            collect(to)
            by_me(
                lambda rows: pltpu.make_async_remote_copy(
                    stage.at[half, to, pl.ds(0, rows), :], got2.at[half, me, pl.ds(0, rows), :],
                    send2.at[half], recv2.at[half], device_id={"rve": to}, device_id_type=MESH,
                ).start()
            )
            return carry

        lax.fori_loop(1, n_rve, body, 0)
        collect(me)
        for j in range(4):
            got2[half, me, j * HALF : (j + 1) * HALF, :] = stage[half, me, j * HALF : (j + 1) * HALF, :]

    load_table.wait()
    spectrum_of(0, 0, spec_a)
    keep_field(0)
    spectrum_of(0, 1, spec_b)
    encode(0)
    send_spread(0)
    stress = [mean_stress(0)]
    spectrum_of(1, 0, spec_a)
    keep_field(1)
    send_owned(0)
    spectrum_of(1, 1, spec_b)
    encode(1)
    send_spread(1)
    stress.append(mean_stress(1))

    weights = weight_v[...]
    sigma = []
    for c in range(COMPS):
        col = jnp.concatenate([stress[0][c], stress[1][c]], axis=0)
        row = sum_rows(chosen * col)
        stress_o[c : c + 1, :] = row
        sigma.append(row * weights)
    grid = ((0, 5, 4), (5, 1, 3), (4, 3, 2))
    force_tile = jnp.zeros((HALF, LANES), f32)
    own_rows = []
    for i in range(3):
        point_force = sigma[grid[i][0]] * grads[0] + sigma[grid[i][1]] * grads[1] + sigma[grid[i][2]] * grads[2]
        cols = [
            sum_lanes(jnp.where(first_element, point_force, 0.0)),
            sum_lanes(jnp.where(first_element, 0.0, point_force)),
        ]
        own_rows.append(sum_rows(own_hot[0] * cols[0] + own_hot[1] * cols[1]))
        far = sum_rows(far_hot[0] * cols[0] + far_hot[1] * cols[1])
        force_tile = jnp.where(sub8 == float(i), far, force_tile)
    force_out[...] = force_tile
    swap_halo(force_out, force_in, fhalo_send, fhalo_recv)
    take_halo(force_out, force_in, fhalo_recv)
    below, above = force_in[0], force_in[1]
    own_tile = jnp.zeros((4, LANES), f32)
    for i in range(3):
        low = sum_lanes(jnp.where(lane8 == sub8 + 8.0, below[i : i + 1], 0.0))
        high = sum_lanes(jnp.where(lane8 == sub8, above[i : i + 1], 0.0))
        row = own_rows[i] + sum_rows(halo_hot[0] * low + halo_hot[1] * high)
        own_tile = jnp.where(sub4 == i, row, own_tile)
    own_out[...] = own_tile
    own_in[me] = own_tile
    to_all(own_out, own_in.at[me], own_send, own_recv)
    send_owned(1)
    wait_all(recv2.at[0])
    decode(0)
    wait_bytes(own_in.at[pl.ds(0, others)], own_recv)
    total = jnp.sum(own_in[...], axis=0)
    mine = jnp.zeros((4, LANES), f32)
    for node in range(4):
        mine = jnp.where(lane4 == node, sum_lanes(jnp.where(lane4 == 4 * me + node, total, 0.0)), mine)
    nodal_o[...] = mine[:3, :4]

    wait_all(recv2.at[1])
    decode(1)

    def copy_out(t):
        at = pl.multiple_of(t * LANES, LANES)
        return pltpu.make_async_copy(
            mixed.at[t, pl.ds(0, 2 * ROWS), :], out_h.at[:, pl.ds(at, LANES)], out_sem
        )

    def start_out(t, carry):
        copy_out(t).start()
        return carry

    lax.fori_loop(0, TILES, start_out, 0)
    wait_bytes(mixed.at[:, pl.ds(0, 2 * ROWS), :], out_sem)
    wait_bytes(gathered.at[pl.ds(0, others)], gather_send)
    wait_bytes(own_in.at[pl.ds(0, others)], own_send)
    for half in range(2):
        wait_all(send1.at[half])
        wait_mine(send2.at[half])
    for send, source in ((halo_send, halo_out), (fhalo_send, force_out)):
        @pl.when(has_below)
        def _(send=send, source=source):
            wait_bytes(source, send.at[0])

        @pl.when(has_above)
        def _(send=send, source=source):
            wait_bytes(source, send.at[1])


def hand_over_kernel(field_h, nodal_ref, stress_ref, field_o, nodal_o, stress_o, held, in_sem, out_sem):
    starts = range(0, 2 * ROWS, HALF)
    taken = [
        pltpu.make_async_copy(field_h.at[pl.ds(at, HALF), :], held.at[pl.ds(at, HALF), :], in_sem.at[n])
        for n, at in enumerate(starts)
    ]
    given = [
        pltpu.make_async_copy(held.at[pl.ds(at, HALF), :], field_o.at[pl.ds(at, HALF), :], out_sem.at[n])
        for n, at in enumerate(starts)
    ]
    for copy in taken:
        copy.start()
    nodal_o[...] = nodal_ref[...]
    stress_o[...] = stress_ref[...]
    for copy, onward in zip(taken, given):
        copy.wait()
        onward.start()
    for onward in given:
        onward.wait()


def hand_over(field, nodal, stress):
    vmem = pl.BlockSpec(memory_space=pltpu.VMEM)
    hbm = pl.BlockSpec(memory_space=pltpu.HBM)
    return pl.pallas_call(
        hand_over_kernel,
        in_specs=[hbm, vmem, vmem],
        out_specs=[hbm, vmem, vmem],
        out_shape=[jax.ShapeDtypeStruct(x.shape, f32) for x in (field, nodal, stress)],
        scratch_shapes=[
            pltpu.VMEM(field.shape, f32),
            pltpu.SemaphoreType.DMA((2 * ROWS // HALF,)),
            pltpu.SemaphoreType.DMA((2 * ROWS // HALF,)),
        ],
        compiler_params=pltpu.CompilerParams(vmem_limit_bytes=63 * 1024 * 1024),
        name="hand_over",
    )(field, nodal, stress)


def solution(mesh):
    n_rve, n_mesh = mesh.shape["rve"], mesh.shape["mesh"]
    planes, coef, count_paired = tables()

    def on_device(displacement, shape_grads, point_weights, conn, halo_nodes, warm_strain, moduli, owner, sweeps):
        points, voxels = warm_strain.shape[0], warm_strain.shape[2]
        warm = warm_strain.transpose(1, 0, 2).reshape(COMPS * points, voxels)
        vmem = pl.BlockSpec(memory_space=pltpu.VMEM)
        hbm = pl.BlockSpec(memory_space=pltpu.HBM)
        dma = pltpu.SemaphoreType.DMA
        scratch = [
            pltpu.VMEM((TILES, 8 * points, LANES), f32),
            pltpu.VMEM((points, 2, voxels), f32),
            pltpu.VMEM(planes.shape, bf16),
            pltpu.VMEM(coef.shape, f32),
            pltpu.VMEM((2, TILES, SPAN, LANES), f32),
            pltpu.VMEM((2, TILES, SPAN, LANES), f32),
            pltpu.VMEM((COMPS, RES * HALF, PLANE), bf16),
            pltpu.VMEM((COMPS, RES * HALF, PLANE), bf16),
            pltpu.VMEM((RES, 2, COMPS, HALF, LANES), f32),
            pltpu.VMEM((RES, 2, COMPS, HALF, LANES), f32),
            pltpu.VMEM((2, n_rve, SENT, LANES), f32),
            pltpu.VMEM((n_rve * SENT + SPAN, LANES), f32),
            pltpu.VMEM((n_rve * SENT + SPAN, LANES), f32),
            pltpu.VMEM((2, n_rve, SENT, LANES), f32),
            pltpu.VMEM((TILES, 2 * ROWS + HALF, LANES), f32),
            pltpu.VMEM((2, COMPS, HALF, LANES), f32),
            pltpu.VMEM((2, n_rve, SPAN, LANES), f32),
            pltpu.VMEM((4, LANES), f32),
            pltpu.VMEM((n_rve, 4, LANES), f32),
            pltpu.VMEM((HALF, LANES), f32),
            pltpu.VMEM((2, HALF, LANES), f32),
            pltpu.VMEM((HALF, LANES), f32),
            pltpu.VMEM((2, HALF, LANES), f32),
            pltpu.VMEM((4, LANES), f32),
            pltpu.VMEM((n_rve, 4, LANES), f32),
            pltpu.VMEM((16, LANES), jnp.int32),
            pltpu.SMEM((16, LANES), jnp.int32),
            pltpu.VMEM((HALF, LANES), jnp.int32),
            pltpu.SMEM((HALF, LANES), jnp.int32),
            pltpu.VMEM((2, 3, COMPS, HALF, LANES), f32),
            pltpu.SMEM((3, 4), f32),
            pltpu.VMEM(shape_grads.shape, f32),
            pltpu.VMEM((1, points), f32),
            pltpu.VMEM((2, 8), jnp.int32),
            pltpu.VMEM((2, 8), jnp.int32),
            pltpu.VMEM((1, points), jnp.int32),
            pltpu.VMEM((1, points), jnp.int32),
            dma((7,)),
            dma((4,)), dma, dma((2,)), dma, dma, dma((2,)), dma((2,)),
            dma((2,)), dma((2,)), dma((2,)), dma((2,)), dma((2,)), dma((2,)), dma, dma,
        ]
        nodal, stress, out = pl.pallas_call(
            functools.partial(main_kernel, count_paired, n_rve, n_mesh),
            in_specs=[hbm] * 11,
            out_specs=[vmem, vmem, hbm],
            out_shape=[
                jax.ShapeDtypeStruct((3, 4), f32),
                jax.ShapeDtypeStruct((COMPS, points), f32),
                jax.ShapeDtypeStruct((2 * ROWS, voxels), f32),
            ],
            scratch_shapes=scratch,
            compiler_params=pltpu.CompilerParams(
                collective_id=0, has_side_effects=True, vmem_limit_bytes=63 * 1024 * 1024
            ),
            name="solve_and_exchange",
        )(
            displacement, shape_grads, point_weights.reshape(1, points), conn.T, halo_nodes,
            owner.reshape(1, points), sweeps.reshape(1, points), warm, moduli,
            jnp.asarray(planes), jnp.asarray(coef),
        )
        micro, nodal, stress = hand_over(out, nodal, stress)
        micro = micro.reshape(COMPS, points, voxels).transpose(1, 0, 2)
        return nodal, stress, micro

    both = ("mesh", "rve")
    in_specs = (
        P(None, both), P(None, None, both), P(both), P(None, both), P(None, "mesh"),
        P(both, None, None), P(both, None, None), P(both), P(both),
    )
    out_specs = (P(None, both), P(None, both), P(both, None, None))
    return jax.shard_map(on_device, mesh=mesh, in_specs=in_specs, out_specs=out_specs, check_vma=False)
```

```python
import functools
import math

import jax
import jax.numpy as jnp
import numpy as np
from jax import lax
from jax.experimental import pallas as pl
from jax.experimental.pallas import tpu as pltpu
from jax.sharding import PartitionSpec as P

RES = 16
PLANE = 256
LANES = 128
TILES = 32
COMPS = 6
HALF = 8
ROWS = COMPS * HALF
SPAN = 8 * HALF
SENT = 4 * HALF
SHORT = 3 * HALF
EXTRA = 13
MIXED_LANE = 112
ENCODE, CHOOSE, DECODE, TABLE_ROWS = 21, 39, 41, 56
MESH = pl.DeviceIdType.MESH
f32 = jnp.float32
bf16 = jnp.bfloat16
index_pairs = ((0, 0), (1, 1), (2, 2), (1, 2), (0, 2), (0, 1))
coef_rows = [(c, d) for c in range(6) for d in range(c, 6)]
coef_at = {}
for _at, (_c, _d) in enumerate(coef_rows):
    coef_at[(_c, _d)] = _at
    coef_at[(_d, _c)] = _at


def half_planes():
    own = [(0, 0), (0, 8), (8, 0), (8, 8)]
    pairs, seen = [], set(own)
    for y in range(RES):
        for z in range(RES):
            if (y, z) not in seen:
                seen.add((y, z))
                seen.add(((-y) % RES, (-z) % RES))
                pairs.append((y, z))
    pairs.sort(key=lambda q: RES // 2 in q)
    lane_a = pairs + [(0, 0), (0, 8)]
    lane_b = pairs + [(8, 0), (8, 8)]
    return np.array(lane_a), np.array(lane_b), len(pairs)


def green_matrix(kx, ky, kz):
    def one(x, y, z):
        k = np.stack([x % RES, y % RES, z % RES]).astype(np.int64)
        xi = np.where(k < RES // 2, k, k - RES).astype(np.float64)
        size = np.sqrt((xi * xi).sum(0))
        n = np.where(size > 0, xi / np.where(size > 0, size, 1.0), 0.0)
        out = np.zeros((6, 6) + size.shape)
        for d, (i, j) in enumerate(index_pairs):
            t = np.zeros((3,) + size.shape)
            t[i] += n[j]
            if i != j:
                t[j] += n[i]
            s = (n * t).sum(0)
            weight = 1.0 if i == j else 2.0
            for c, (k_, h_) in enumerate(index_pairs):
                value = (n[k_] * t[h_] + n[h_] * t[k_]) / 2.2
                value = value - (2.2 / (1.1 * 3.3)) * n[k_] * n[h_] * s
                out[c, d] = value / weight
        return out

    return 0.5 * (one(kx, ky, kz) + one(-kx, -ky, -kz))


def transport_rows(k):
    xi = np.array([i if i < RES // 2 else i - RES for i in k], np.float64)
    size = np.sqrt((xi * xi).sum())
    n = xi / size if size > 0 else xi
    edge = [i == RES // 2 for i in k]
    back = np.zeros((6, 3))
    mixed = {}
    for c, (i, j) in enumerate(index_pairs):
        if i == j:
            back[c, i] = n[i]
        elif edge[i] == edge[j]:
            back[c, i], back[c, j] = 0.5 * n[j], 0.5 * n[i]
        else:
            mixed[c] = True
    rows = np.zeros(TABLE_ROWS)
    into = np.linalg.pinv(back)
    rows[ENCODE : ENCODE + 18] = into.reshape(-1)
    first, second = (sorted(mixed, reverse=True) + [5, 4])[:2]
    rows[CHOOSE], rows[CHOOSE + 1] = float(first == 5), float(second == 4)
    rows[DECODE : DECODE + 3] = n
    rows[DECODE + 3 : DECODE + 9] = back[3, 1], back[3, 2], back[4, 0], back[4, 2], back[5, 0], back[5, 1]
    if mixed:
        rows[DECODE + 9] = float(first == 5)
        rows[DECODE + 10] = float(first == 4)
        rows[DECODE + 11] = float(second == 4)
        rows[DECODE + 12] = float(second == 3)
    return rows


@functools.lru_cache(None)
def tables():
    lane_a, lane_b, count = half_planes()
    v = np.arange(PLANE)
    vy, vz = v // RES, v % RES
    angle = 2.0 * math.pi / RES

    def phase(lane):
        return angle * ((np.outer(vy, lane[:, 0]) + np.outer(vz, lane[:, 1])) % RES)

    paired = (np.arange(LANES) < count)[None, :]
    forward = np.concatenate(
        [np.cos(phase(lane_a)), np.where(paired, -np.sin(phase(lane_b)), np.cos(phase(lane_b)))], axis=1
    )
    coef = np.zeros((RES, 2, TABLE_ROWS, LANES))
    moved_by = functools.lru_cache(None)(transport_rows)
    for slot in range(RES):
        for part in range(2):
            ky, kz, kx, scale = [], [], [], []
            for lane in range(LANES):
                if lane < count:
                    y, z, x, weight = *lane_a[lane], slot, 2.0
                elif slot in (0, RES // 2):
                    y, z = lane_a[lane] if part == 0 else lane_b[lane]
                    x, weight = slot, 1.0
                else:
                    y, z = lane_a[lane] if slot < RES // 2 else lane_b[lane]
                    x, weight = (slot if slot < RES // 2 else RES - slot), 0.5
                ky.append(y), kz.append(z), kx.append(x), scale.append(weight / RES**3)
            for lane in range(LANES):
                coef[slot, part, :, lane] = moved_by((kx[lane] % RES, int(ky[lane]) % RES, int(kz[lane]) % RES))
            matrix = green_matrix(np.array(kx), np.array(ky), np.array(kz)) * np.array(scale)
            for row, (c, d) in enumerate(coef_rows):
                coef[slot, part, row] = matrix[c, d]

    def split(table):
        high = jnp.asarray(table, f32).astype(bf16)
        low = (np.asarray(table, np.float64) - np.asarray(high).astype(np.float64)).astype(np.float32)
        return np.asarray(high), np.asarray(jnp.asarray(low).astype(bf16))

    with jax.ensure_compile_time_eval():
        fh, fl = split(forward)
        ih, il = split(forward.T)
    return np.stack([fh, fl, ih, il]), coef.astype(np.float32), count


def complex_mul(a, b):
    re, im = a
    cr, ci = b
    if abs(ci) < 1e-12 and abs(cr - 1) < 1e-12:
        return a
    if abs(cr) < 1e-12:
        return (im, -re) if ci < 0 else (-im, re)
    if abs(abs(cr) - abs(ci)) < 1e-12:
        h = abs(cr)
        sr, si = cr > 0, ci > 0
        if sr and not si:
            return (h * (re + im), h * (im - re))
        if not sr and not si:
            return (h * (im - re), -h * (re + im))
        if sr and si:
            return (h * (re - im), h * (im + re))
        return (-h * (re + im), h * (re - im))
    return (cr * re - ci * im, cr * im + ci * re)


def four_point(a, b, c, d, sign):
    s0 = (a[0] + c[0], a[1] + c[1])
    s1 = (a[0] - c[0], a[1] - c[1])
    s2 = (b[0] + d[0], b[1] + d[1])
    s3 = (b[0] - d[0], b[1] - d[1])
    turned = (s3[1], -s3[0]) if sign < 0 else (-s3[1], s3[0])
    return (
        (s0[0] + s2[0], s0[1] + s2[1]),
        (s1[0] + turned[0], s1[1] + turned[1]),
        (s0[0] - s2[0], s0[1] - s2[1]),
        (s1[0] - turned[0], s1[1] - turned[1]),
    )


def sixteen_point(values, sign):
    columns = []
    for r in range(4):
        out = four_point(values[r], values[r + 4], values[r + 8], values[r + 12], sign)
        columns.append(
            [
                complex_mul(out[k], (math.cos(2 * math.pi * r * k / 16), sign * math.sin(2 * math.pi * r * k / 16)))
                for k in range(4)
            ]
        )
    result = [None] * 16
    for k in range(4):
        out = four_point(columns[0][k], columns[1][k], columns[2][k], columns[3][k], sign)
        for m in range(4):
            result[k + 4 * m] = out[m]
    return result


def iota(shape, dim):
    return lax.broadcasted_iota(jnp.int32, shape, dim)


def sum_lanes(x):
    return jnp.sum(x, axis=1, keepdims=True)


def sum_rows(x):
    return jnp.sum(x, axis=0, keepdims=True)


def split_bf16(x):
    high = x.astype(bf16)
    low = (x - high.astype(f32)).astype(bf16)
    return high, low


def three_pass(high, low, table_high, table_low):
    def dot(a, b):
        return jnp.dot(a, b, preferred_element_type=f32)

    return dot(high, table_high) + (dot(low, table_high) + dot(high, table_low))


def main_kernel(
    count_paired, n_rve, n_mesh,
    disp_h, grads_h, weight_h, conn_h, halo_h, owner_h, sweeps_h, warm_h, moduli_h, plane_h, coef_h,
    nodal_o, stress_o, out_h,
    warm_v, moduli_v, plane_v, coef_v, field, mod, tau_h, tau_l, spec_0, spec_a, spec_b, payload, got1_a, got1_b, got2, mixed, sums_v, stage,
    tile_v, gathered, halo_out, halo_in, force_out, force_in, own_out, own_in,
    perm_v, perm_s, table_v, table_s, column_v,
    disp_s, grads_v, weight_v, conn_v, halo_v, owner_v, sweeps_v, small_sem,
    in_sem, out_sem, idx_sem, gather_send, gather_recv, halo_send, halo_recv,
    send1, recv1, send2, recv2, fhalo_send, fhalo_recv, own_send, own_recv,
):
    me = lax.axis_index("rve")
    part = lax.axis_index("mesh")
    others = n_rve - 1

    def after_me(k):
        return jnp.where(me + k >= n_rve, me + k - n_rve, me + k)

    got1 = (got1_a, got1_b)
    last_row = others * SENT + HALF - 1
    has_below = part > 0
    has_above = part < n_mesh - 1

    small = [
        pltpu.make_async_copy(source, target, small_sem.at[at])
        for at, (source, target) in enumerate((
            (owner_h, owner_v), (sweeps_h, sweeps_v), (disp_h, disp_s), (halo_h, halo_v),
            (conn_h, conn_v), (grads_h, grads_v), (weight_h, weight_v),
        ))
    ]
    for load in small:
        load.start()

    def load_tile(t):
        at = pl.multiple_of(t * LANES, LANES)
        return pltpu.make_async_copy(
            warm_h.at[:, pl.ds(at, LANES)], warm_v.at[t, pl.ds(0, COMPS * 16), :], in_sem.at[0]
        )

    def start_tile(t, carry):
        load_tile(t).start()
        return carry

    lax.fori_loop(0, TILES, start_tile, 0)
    big_loads = [
        pltpu.make_async_copy(moduli_h, moduli_v, in_sem.at[1]),
        pltpu.make_async_copy(plane_h, plane_v, in_sem.at[2]),
        pltpu.make_async_copy(coef_h, coef_v, in_sem.at[3]),
    ]
    for load in big_loads:
        load.start()

    barrier = pltpu.get_barrier_semaphore()

    for k in range(1, n_rve):
        pl.semaphore_signal(barrier, inc=1, device_id={"rve": after_me(k)}, device_id_type=MESH)

    @pl.when(has_below)
    def _():
        pl.semaphore_signal(barrier, inc=1, device_id={"mesh": part - 1}, device_id_type=MESH)

    @pl.when(has_above)
    def _():
        pl.semaphore_signal(barrier, inc=1, device_id={"mesh": part + 1}, device_id_type=MESH)

    for load in small:
        load.wait()

    owner_row = owner_v[...].astype(f32)
    sub16, lane16 = iota((16, 16), 0), iota((16, 16), 1)
    owner_col = sum_lanes(jnp.where(sub16 == lane16, jnp.broadcast_to(owner_row, (16, 16)), 0.0))
    place = 0.5 * sum_rows(jnp.where(owner_col < owner_row, 1.0, 0.0))
    rank = sum_rows(jnp.where((owner_col == owner_row) & (sub16 < lane16), 1.0, 0.0))
    slot_row = 8.0 * rank + place
    chosen = jnp.where(slot_row == sub16.astype(f32), 1.0, 0.0)
    perm_col = sum_lanes(chosen * lane16.astype(f32))
    perm_v[...] = jnp.broadcast_to(perm_col, (16, LANES)).astype(jnp.int32)
    count_col = sum_lanes(chosen * sweeps_v[...].astype(f32))
    load_perm = pltpu.make_async_copy(perm_v, perm_s, idx_sem.at[0])
    load_perm.start()

    lane_row = iota((1, LANES), 1).astype(f32)
    sends_row = 0.5 * sum_rows(jnp.where(owner_col == lane_row, 1.0, 0.0))
    sub4, lane4 = iota((4, LANES), 0), iota((4, LANES), 1)
    tile = jnp.where(sub4 == 3, sends_row, 0.0)
    for i in range(3):
        for node in range(4):
            tile = jnp.where((sub4 == i) & (lane4 == 4 * me + node), disp_s[i, node], tile)
    tile_v[...] = tile
    gathered[me] = tile

    extra = jnp.where(has_below, 1, 0) + jnp.where(has_above, 1, 0)
    pl.semaphore_wait(barrier, others + extra)

    def to_all(source, target, send, recv):
        def body(k, carry):
            to = after_me(k)
            pltpu.make_async_remote_copy(
                source, target, send, recv, device_id={"rve": to}, device_id_type=MESH
            ).start()
            return carry

        for k in range(1, n_rve):
            body(k, 0)

    def wait_bytes(view, sem):
        pltpu.make_async_copy(view, view, sem).wait()

    to_all(tile_v, gathered.at[me], gather_send, gather_recv)

    load_perm.wait()
    big_loads[0].wait()

    wait_bytes(warm_v.at[:, pl.ds(0, COMPS * 16), :], in_sem.at[0])
    places_at = [
        (half, pos, jnp.clip(perm_s[half * HALF + pos, 0], 0, 15)) for half in range(2) for pos in range(HALF)
    ]

    def place_tile(t, carry):
        at = pl.multiple_of(t * LANES, LANES)
        for half, pos, point in places_at:
            field[half, t, pl.ds(pos, COMPS, stride=HALF), :] = warm_v[t, pl.ds(point, COMPS, stride=16), :]
            mod[half, t, pl.ds(pos, 2, stride=HALF), :] = moduli_v[point, :, pl.ds(at, LANES)]
        return carry

    lax.fori_loop(0, TILES, place_tile, 0)

    def add_up(t, sums):
        return tuple(
            sums[half * COMPS + c] + field[half, t, c * HALF : (c + 1) * HALF, :]
            for half in range(2)
            for c in range(COMPS)
        )

    sums = lax.fori_loop(
        0, TILES, add_up, tuple(jnp.zeros((HALF, LANES), f32) for _ in range(2 * COMPS)), unroll=4
    )
    means = [[sum_lanes(sums[half * COMPS + c]) * (1.0 / 4096.0) for c in range(COMPS)] for half in range(2)]

    big_loads[1].wait()
    big_loads[2].wait()
    odd_lane = iota((HALF, LANES), 1) >= count_paired

    def table_row(k, part_at, row):
        return coef_v[k, part_at, row : row + 1, :]

    def forward_into(planes, put):
        def forward(c, carry):
            planed = three_pass(tau_h[c], tau_l[c], plane_v[0], plane_v[1])
            values = [
                (planed[x * HALF : (x + 1) * HALF, :LANES], planed[x * HALF : (x + 1) * HALF, LANES:])
                for x in range(RES)
            ]
            z = sixteen_point(values, -1)
            for k in range(1, 8):
                a, b = z[k], z[RES - k]
                z[k] = (jnp.where(odd_lane, a[0] + b[0], a[0]), jnp.where(odd_lane, a[1] - b[1], a[1]))
                z[RES - k] = (jnp.where(odd_lane, a[1] + b[1], b[0]), jnp.where(odd_lane, b[0] - a[0], b[1]))
            for k in range(RES):
                put(k, 0, c, z[k][0])
                put(k, 1, c, z[k][1])
            return carry

        lax.fori_loop(0, planes, forward, 0, unroll=2)

    def polarize_into(half, first):
        def polarize(u, carry):
            for b in range(2):
                cats = [[] for _ in range(8)]
                for step in range(2):
                    t = (2 * u + step) * 2 + b
                    eps = [field[half, t, c * HALF : (c + 1) * HALF, :] for c in range(COMPS)]
                    if first:
                        eps = [eps[c] - means[half][c] for c in range(COMPS)]
                    lam = mod[half, t, 0:HALF, :] - 1.1
                    shear = 2.0 * mod[half, t, HALF : 2 * HALF, :] - 2.2
                    pressure = lam * (eps[0] + eps[1] + eps[2])
                    double = shear + shear
                    for c in range(3):
                        cats[c].append(shear * eps[c] + pressure)
                    for c in range(3, 6):
                        cats[c].append(double * eps[c])
                    if first:
                        cats[6].append(lam)
                        cats[7].append(shear)
                for c in range(8 if first else COMPS):
                    high, low = split_bf16(jnp.concatenate(cats[c], axis=0))
                    at = pl.multiple_of(u * 16, 16)
                    tau_h[c, pl.ds(at, 16), b * LANES : (b + 1) * LANES] = high
                    tau_l[c, pl.ds(at, 16), b * LANES : (b + 1) * LANES] = low
            return carry

        lax.fori_loop(0, 8, polarize, 0, unroll=2)

    def start_spectrum(half):
        def put(k, part_at, c, value):
            spec_0[half, k, part_at, c] = value

        polarize_into(half, True)
        forward_into(8, put)

    def apply_green(half, k, part_at, ins, spec, keep):
        rows = [table_row(k, part_at, r) for r in range(len(coef_rows))]
        for c in range(COMPS):
            total = rows[coef_at[(c, 0)]] * ins[0]
            for d in range(1, COMPS):
                total = total + rows[coef_at[(c, d)]] * ins[d]
            if keep is not None:
                total = jnp.where(keep, total, spec_a[k, part_at, c])
            spec[k, part_at, c] = total

    def first_spectrum(half):
        def green(k, carry):
            level = [column_v[half, 1, c] for c in range(COMPS)]
            level = level[:3] + [2.0 * x for x in level[3:]]
            whole = level[0] + level[1] + level[2]
            for part_at in range(2):
                ins = [spec_0[half, k, part_at, c] for c in range(8)]
                pressure = whole * ins[6]
                ins = [ins[c] + level[c] * ins[7] for c in range(COMPS)]
                ins = [ins[c] + pressure if c < 3 else ins[c] for c in range(COMPS)]
                apply_green(half, k, part_at, ins, spec_a, None)
            return carry

        lax.fori_loop(0, RES, green, 0, unroll=2)

    def second_spectrum(half):
        def put(k, part_at, c, value):
            spec_b[half, k, part_at, c] = value

        polarize_into(half, False)
        forward_into(COMPS, put)

        def green(k, carry):
            again = column_v[half, 2, 0] > 1.5
            for part_at in range(2):
                ins = [spec_b[half, k, part_at, c] for c in range(COMPS)]
                apply_green(half, k, part_at, ins, spec_b.at[half], again)
            return carry

        lax.fori_loop(0, RES, green, 0, unroll=2)

    start_spectrum(0)

    wait_bytes(gathered.at[pl.ds(0, others)], gather_recv)
    moved = jnp.sum(gathered[...], axis=0)
    lane8, sub8 = iota((HALF, LANES), 1).astype(f32), iota((HALF, LANES), 0).astype(f32)
    eye8 = iota((HALF, HALF), 0) == iota((HALF, HALF), 1)
    halo_rows = halo_v[...].astype(f32)
    halo_hot = []
    for side in range(2):
        col = sum_lanes(jnp.where(eye8, jnp.broadcast_to(halo_rows[side : side + 1], (HALF, HALF)), 0.0))
        halo_hot.append(jnp.where(col == lane8, 1.0, 0.0))
    out_tile = jnp.zeros((HALF, LANES), f32)
    for side in range(2):
        for i in range(3):
            col = sum_lanes(halo_hot[side] * moved[i : i + 1])
            out_tile = jnp.where(lane8 == 3 * side + i, col, out_tile)
    halo_out[...] = out_tile

    def swap_halo(source, target, send, recv):
        @pl.when(has_below)
        def _():
            pltpu.make_async_remote_copy(
                source, target.at[1], send.at[0], recv.at[1], device_id={"mesh": part - 1}, device_id_type=MESH
            ).start()

        @pl.when(has_above)
        def _():
            pltpu.make_async_remote_copy(
                source, target.at[0], send.at[1], recv.at[0], device_id={"mesh": part + 1}, device_id_type=MESH
            ).start()

    def take_halo(source, target, recv):
        @pl.when(has_below)
        def _():
            wait_bytes(target.at[0], recv.at[0])

        @pl.when(jnp.logical_not(has_below))
        def _():
            target[0] = jnp.zeros((HALF, LANES), f32)

        @pl.when(has_above)
        def _():
            wait_bytes(target.at[1], recv.at[1])

        @pl.when(jnp.logical_not(has_above))
        def _():
            target[1] = jnp.zeros((HALF, LANES), f32)

    swap_halo(halo_out, halo_in, halo_send, halo_recv)

    sends = jnp.concatenate([gathered[s, 3:4] for s in range(n_rve)], axis=0)
    lower = jnp.where(iota((n_rve, n_rve), 1) < iota((n_rve, n_rve), 0), 1.0, 0.0).astype(bf16)
    upper = jnp.where(iota((LANES, LANES), 0) < iota((LANES, LANES), 1), 1.0, 0.0).astype(bf16)
    sends_b = sends.astype(bf16)
    order = jnp.dot(lower, sends_b, preferred_element_type=f32)
    places = jnp.dot(sends_b, upper, preferred_element_type=f32)
    rows_at = iota((n_rve, LANES), 0).astype(f32) * float(SENT) + places
    table = jnp.zeros((HALF, LANES), f32)
    for k in range(HALF):
        row = sum_rows(jnp.where((sends > 0.5) & (order == float(k)), rows_at, 0.0))
        table = jnp.where(sub8 == float(k), row, table)
    table_v[...] = table.astype(jnp.int32)
    load_table = pltpu.make_async_copy(table_v, table_s, idx_sem.at[1])
    load_table.start()

    conn_rows = conn_v[...].astype(f32)
    own_hot, far_hot = [], []
    for e in range(2):
        col = sum_lanes(jnp.where(eye8, jnp.broadcast_to(conn_rows[e : e + 1], (HALF, HALF)), 0.0))
        own_hot.append(jnp.where(col == lane8, 1.0, 0.0))
        far_hot.append(jnp.where(col - float(LANES) == lane8, 1.0, 0.0))
    first_element = iota((HALF, 16), 1) < 8

    start_spectrum(1)
    take_halo(halo_out, halo_in, halo_recv)
    below, above = halo_in[0], halo_in[1]
    spread_disp = []
    for i in range(3):
        far = sum_rows(jnp.where(lane8 == sub8, below[:, 3 + i : 4 + i], 0.0))
        far = far + sum_rows(jnp.where(lane8 == sub8 + 8.0, above[:, i : i + 1], 0.0))
        cols = [sum_lanes(own_hot[e] * moved[i : i + 1] + far_hot[e] * far) for e in range(2)]
        spread_disp.append(jnp.where(first_element, cols[0], cols[1]))
    grads = [grads_v[j] for j in range(3)]
    g = [[sum_rows(spread_disp[i] * grads[j]) for j in range(3)] for i in range(3)]
    macro = [
        g[0][0], g[1][1], g[2][2],
        (g[1][2] + g[2][1]) * 0.5, (g[0][2] + g[2][0]) * 0.5, (g[0][1] + g[1][0]) * 0.5,
    ]
    macro_cols = [sum_lanes(chosen * row) for row in macro]
    for c in range(COMPS):
        for half in range(2):
            col = macro_cols[c][half * HALF : (half + 1) * HALF]
            column_v[half, 1, c] = jnp.broadcast_to(col, (HALF, LANES))
    for half in range(2):
        column_v[half, 2, 0] = jnp.broadcast_to(count_col[half * HALF : (half + 1) * HALF], (HALF, LANES))

    def strain_from(half, spec, take):
        def backward(c, carry):
            z = [(spec[k, 0, c], spec[k, 1, c]) for k in range(RES)]
            for k in range(1, 8):
                a, b = z[k], z[RES - k]
                z[k] = (jnp.where(odd_lane, a[0] - b[1], a[0]), jnp.where(odd_lane, a[1] + b[0], a[1]))
                z[RES - k] = (jnp.where(odd_lane, a[0] + b[1], b[0]), jnp.where(odd_lane, b[0] - a[1], b[1]))
            values = sixteen_point(z, 1)
            lined = jnp.concatenate(
                [
                    jnp.concatenate([values[x][0] for x in range(RES)], axis=0),
                    jnp.concatenate([values[x][1] for x in range(RES)], axis=0),
                ],
                axis=1,
            )
            high, low = split_bf16(lined)
            fluct = three_pass(high, low, plane_v[2], plane_v[3])
            level = column_v[half, 1, c]
            take(
                c,
                [
                    level - fluct[t // 2 * HALF : (t // 2 + 1) * HALF, t % 2 * LANES : (t % 2 + 1) * LANES]
                    for t in range(TILES)
                ],
            )
            return carry

        lax.fori_loop(0, COMPS, backward, 0, unroll=2)

    def keep_field(half):
        def take(c, tiles):
            at = pl.multiple_of(c * HALF, HALF)
            for t in range(TILES):
                field[half, t, pl.ds(at, HALF), :] = tiles[t]

        strain_from(half, spec_a, take)

    def mean_stress(half):
        def take(c, tiles):
            for which in range(2):
                parts = [
                    mod[half, t, which * HALF : (which + 1) * HALF, :] * tiles[t] for t in range(TILES)
                ]
                while len(parts) > 1:
                    parts = [p + q for p, q in zip(parts[::2], parts[1::2])]
                sums_v[which, c] = parts[0]

        strain_from(half, spec_b.at[half], take)
        pressure = sums_v[0, 0] + sums_v[0, 1] + sums_v[0, 2]
        result = []
        for c in range(COMPS):
            total = 2.0 * sums_v[1, c]
            if c < 3:
                total = total + pressure
            result.append(sum_lanes(total) * (1.0 / 4096.0))
        return result

    packed_group = iota((HALF, LANES), 1) // 16

    def encode(half):
        def extras(k, part_at, eps):
            first = jnp.where(table_row(k, part_at, CHOOSE) > 0.5, eps[5], eps[4])
            second = jnp.where(table_row(k, part_at, CHOOSE + 1) > 0.5, eps[4], eps[3])
            return first, second

        def body(i, carry):
            packed = jnp.zeros((HALF, LANES), f32)
            for step in range(2):
                k = 2 * i + step
                for part_at in range(2):
                    eps = [spec_b[half, k, part_at, c] for c in range(COMPS)]
                    for j in range(3):
                        total = table_row(k, part_at, ENCODE + 6 * j) * eps[0]
                        for c in range(1, COMPS):
                            total = total + table_row(k, part_at, ENCODE + 6 * j + c) * eps[c]
                        payload[half, 2 * k + part_at, j * HALF : (j + 1) * HALF, :] = total
                    for e, value in enumerate(extras(k, part_at, eps)):
                        piece = (2 * step + part_at) * 2 + e
                        shift = (16 * piece + 16) % LANES
                        if shift:
                            value = pltpu.roll(value, shift, 1)
                        packed = jnp.where(packed_group == piece, value, packed)
            payload[half, i, SHORT:SENT, :] = packed
            return carry

        lax.fori_loop(0, 8, body, 0)
        for part_at in range(2):
            eps = [spec_b[half, RES // 2, part_at, c] for c in range(COMPS)]
            for e, value in enumerate(extras(RES // 2, part_at, eps)):
                payload[half, 8 + 2 * part_at + e, SHORT:SENT, :] = value
        levels = jnp.zeros((HALF, LANES), f32)
        for c in range(COMPS):
            levels = jnp.where(lane8 == float(c), column_v[half, 1, c], levels)
        payload[half, EXTRA - 1, SHORT:SENT, :] = levels

    def decode(half):
        def restore(k, part_at, first, second):
            d = [got2[half, 2 * k + part_at, j * HALF : (j + 1) * HALF, :] for j in range(3)]
            row = [table_row(k, part_at, DECODE + r) for r in range(13)]
            for c in range(3):
                spec_a[k, part_at, c] = row[c] * d[c]
            spec_a[k, part_at, 3] = row[3] * d[1] + row[4] * d[2] + row[12] * second
            spec_a[k, part_at, 4] = row[5] * d[0] + row[6] * d[2] + (row[10] * first + row[11] * second)
            spec_a[k, part_at, 5] = row[7] * d[0] + row[8] * d[1] + row[9] * first

        def body(i, carry):
            packed = got2[half, i, SHORT:SENT, :]
            for step in range(2):
                for part_at in range(2):
                    values = []
                    for e in range(2):
                        piece = (2 * step + part_at) * 2 + e
                        shift = (LANES - (16 * piece + 16) % LANES) % LANES
                        values.append(pltpu.roll(packed, shift, 1) if shift else packed)
                    restore(2 * i + step, part_at, *values)
            return carry

        lax.fori_loop(0, 8, body, 0)
        for part_at in range(2):
            restore(
                RES // 2, part_at,
                got2[half, 8 + 2 * part_at, SHORT:SENT, :], got2[half, 9 + 2 * part_at, SHORT:SENT, :],
            )
        levels = got2[half, EXTRA - 1, SHORT:SENT, :]
        for c in range(COMPS):
            column_v[half, 1, c] = jnp.broadcast_to(levels[:, c : c + 1], (HALF, LANES))

        def take(c, tiles):
            at = pl.multiple_of(c * 2 * HALF, 2 * HALF)
            for t in range(TILES):
                mixed[t, pl.ds(at + half, HALF, stride=2), :] = tiles[t]

        strain_from(half, spec_a, take)

    long_rows = jnp.where(me < EXTRA, 1, 0) == 1

    def by_me(action):
        @pl.when(long_rows)
        def _():
            action(SENT)

        @pl.when(jnp.logical_not(long_rows))
        def _():
            action(SHORT)

    def wait_mine(sem):
        by_me(lambda rows: wait_bytes(got2.at[0, pl.ds(0, others), pl.ds(0, rows), :], sem))

    def wait_all(sem):
        full = EXTRA * SENT + (n_rve - EXTRA) * SHORT
        by_me(lambda rows: wait_bytes(got1_a.at[pl.ds(0, full - rows), :], sem))

    def send_spread(half):
        at = pl.multiple_of(me * SENT, SENT)
        for j in range(4):
            rows = pl.multiple_of(me * SENT + j * HALF, HALF)
            got1[half][pl.ds(rows, HALF), :] = payload[half, me, j * HALF : (j + 1) * HALF, :]

        def body(k, carry):
            to = after_me(k)

            def send(rows):
                pltpu.make_async_remote_copy(
                    payload.at[half, to, pl.ds(0, rows), :], got1[half].at[pl.ds(at, rows), :],
                    send1.at[half], recv1.at[half], device_id={"rve": to}, device_id_type=MESH,
                ).start()

            @pl.when(to < EXTRA)
            def _():
                send(SENT)

            @pl.when(to >= EXTRA)
            def _():
                send(SHORT)

            return carry

        for k in range(1, n_rve):
            body(k, 0)

    def send_owned(half):
        wait_mine(recv1.at[half])

        def collect(to):
            for at in range(HALF):
                row = jnp.clip(table_s[at, to], 0, last_row)
                stage[half, to, pl.ds(at, 4, stride=HALF), :] = got1[half][pl.ds(row, 4, stride=HALF), :]

        def body(k, carry):
            to = after_me(k)
            collect(to)
            by_me(
                lambda rows: pltpu.make_async_remote_copy(
                    stage.at[half, to, pl.ds(0, rows), :], got2.at[half, me, pl.ds(0, rows), :],
                    send2.at[half], recv2.at[half], device_id={"rve": to}, device_id_type=MESH,
                ).start()
            )
            return carry

        for k in range(1, n_rve):
            body(k, 0)
        collect(me)
        for j in range(4):
            got2[half, me, j * HALF : (j + 1) * HALF, :] = stage[half, me, j * HALF : (j + 1) * HALF, :]

    load_table.wait()
    for half in range(2):
        first_spectrum(half)
        keep_field(half)
        if half == 1:
            send_owned(0)
        second_spectrum(half)
        encode(half)
        send_spread(half)
    stress = [mean_stress(0), mean_stress(1)]

    weights = weight_v[...]
    sigma = []
    for c in range(COMPS):
        col = jnp.concatenate([stress[0][c], stress[1][c]], axis=0)
        row = sum_rows(chosen * col)
        stress_o[c : c + 1, :] = row
        sigma.append(row * weights)
    grid = ((0, 5, 4), (5, 1, 3), (4, 3, 2))
    force_tile = jnp.zeros((HALF, LANES), f32)
    own_rows = []
    for i in range(3):
        point_force = sigma[grid[i][0]] * grads[0] + sigma[grid[i][1]] * grads[1] + sigma[grid[i][2]] * grads[2]
        cols = [
            sum_lanes(jnp.where(first_element, point_force, 0.0)),
            sum_lanes(jnp.where(first_element, 0.0, point_force)),
        ]
        own_rows.append(sum_rows(own_hot[0] * cols[0] + own_hot[1] * cols[1]))
        far = sum_rows(far_hot[0] * cols[0] + far_hot[1] * cols[1])
        force_tile = jnp.where(sub8 == float(i), far, force_tile)
    force_out[...] = force_tile
    swap_halo(force_out, force_in, fhalo_send, fhalo_recv)
    take_halo(force_out, force_in, fhalo_recv)
    below, above = force_in[0], force_in[1]
    own_tile = jnp.zeros((4, LANES), f32)
    for i in range(3):
        low = sum_lanes(jnp.where(lane8 == sub8 + 8.0, below[i : i + 1], 0.0))
        high = sum_lanes(jnp.where(lane8 == sub8, above[i : i + 1], 0.0))
        row = own_rows[i] + sum_rows(halo_hot[0] * low + halo_hot[1] * high)
        own_tile = jnp.where(sub4 == i, row, own_tile)
    own_out[...] = own_tile
    own_in[me] = own_tile
    to_all(own_out, own_in.at[me], own_send, own_recv)
    send_owned(1)
    wait_all(recv2.at[0])
    decode(0)
    wait_all(recv2.at[1])
    decode(1)

    def copy_out(t):
        at = pl.multiple_of(t * LANES, LANES)
        return pltpu.make_async_copy(
            mixed.at[t, pl.ds(0, 2 * ROWS), :], out_h.at[:, pl.ds(at, LANES)], out_sem
        )

    def start_out(t, carry):
        copy_out(t).start()
        return carry

    lax.fori_loop(0, TILES, start_out, 0)
    wait_bytes(own_in.at[pl.ds(0, others)], own_recv)
    total = jnp.sum(own_in[...], axis=0)
    mine = jnp.zeros((4, LANES), f32)
    for node in range(4):
        mine = jnp.where(lane4 == node, sum_lanes(jnp.where(lane4 == 4 * me + node, total, 0.0)), mine)
    nodal_o[...] = mine[:3, :4]
    wait_bytes(mixed.at[:, pl.ds(0, 2 * ROWS), :], out_sem)
    wait_bytes(gathered.at[pl.ds(0, others)], gather_send)
    wait_bytes(own_in.at[pl.ds(0, others)], own_send)
    for half in range(2):
        wait_all(send1.at[half])
        wait_mine(send2.at[half])
    for send, source in ((halo_send, halo_out), (fhalo_send, force_out)):
        @pl.when(has_below)
        def _(send=send, source=source):
            wait_bytes(source, send.at[0])

        @pl.when(has_above)
        def _(send=send, source=source):
            wait_bytes(source, send.at[1])


def hand_over_kernel(field_h, nodal_h, stress_h, field_o, nodal_o, stress_o, held, nodal_v, stress_v, in_sem, out_sem):
    through = [
        (field_h.at[pl.ds(at, HALF), :], held.at[pl.ds(at, HALF), :], field_o.at[pl.ds(at, HALF), :])
        for at in range(0, 2 * ROWS, HALF)
    ]
    through = [(nodal_h, nodal_v, nodal_o), (stress_h, stress_v, stress_o)] + through
    taken = [pltpu.make_async_copy(a, b, in_sem.at[n]) for n, (a, b, _) in enumerate(through)]
    given = [pltpu.make_async_copy(b, c, out_sem.at[n]) for n, (_, b, c) in enumerate(through)]
    for copy in taken:
        copy.start()
    for copy, onward in zip(taken, given):
        copy.wait()
        onward.start()
    for onward in given:
        onward.wait()


def hand_over(field, nodal, stress):
    hbm = pl.BlockSpec(memory_space=pltpu.HBM)
    count = 2 * ROWS // HALF + 2
    return pl.pallas_call(
        hand_over_kernel,
        in_specs=[hbm, hbm, hbm],
        out_specs=[hbm, hbm, hbm],
        out_shape=[jax.ShapeDtypeStruct(x.shape, f32) for x in (field, nodal, stress)],
        scratch_shapes=[pltpu.VMEM(x.shape, f32) for x in (field, nodal, stress)]
        + [pltpu.SemaphoreType.DMA((count,)), pltpu.SemaphoreType.DMA((count,))],
        compiler_params=pltpu.CompilerParams(vmem_limit_bytes=63 * 1024 * 1024),
        name="hand_over",
    )(field, nodal, stress)


def solution(mesh):
    n_rve, n_mesh = mesh.shape["rve"], mesh.shape["mesh"]
    planes, coef, count_paired = tables()

    def on_device(displacement, shape_grads, point_weights, conn, halo_nodes, warm_strain, moduli, owner, sweeps):
        points, voxels = warm_strain.shape[0], warm_strain.shape[2]
        warm = warm_strain.transpose(1, 0, 2).reshape(COMPS * points, voxels)
        vmem = pl.BlockSpec(memory_space=pltpu.VMEM)
        hbm = pl.BlockSpec(memory_space=pltpu.HBM)
        dma = pltpu.SemaphoreType.DMA
        scratch = [
            pltpu.VMEM((TILES, 8 * points, LANES), f32),
            pltpu.VMEM((points, 2, voxels), f32),
            pltpu.VMEM(planes.shape, bf16),
            pltpu.VMEM(coef.shape, f32),
            pltpu.VMEM((2, TILES, SPAN, LANES), f32),
            pltpu.VMEM((2, TILES, SPAN, LANES), f32),
            pltpu.VMEM((8, RES * HALF, PLANE), bf16),
            pltpu.VMEM((8, RES * HALF, PLANE), bf16),
            pltpu.VMEM((2, RES, 2, 8, HALF, LANES), f32),
            pltpu.VMEM((RES, 2, COMPS, HALF, LANES), f32),
            pltpu.VMEM((2, RES, 2, COMPS, HALF, LANES), f32),
            pltpu.VMEM((2, n_rve, SENT, LANES), f32),
            pltpu.VMEM((n_rve * SENT + SPAN, LANES), f32),
            pltpu.VMEM((n_rve * SENT + SPAN, LANES), f32),
            pltpu.VMEM((2, n_rve, SENT, LANES), f32),
            pltpu.VMEM((TILES, 2 * ROWS + HALF, LANES), f32),
            pltpu.VMEM((2, COMPS, HALF, LANES), f32),
            pltpu.VMEM((2, n_rve, SPAN, LANES), f32),
            pltpu.VMEM((4, LANES), f32),
            pltpu.VMEM((n_rve, 4, LANES), f32),
            pltpu.VMEM((HALF, LANES), f32),
            pltpu.VMEM((2, HALF, LANES), f32),
            pltpu.VMEM((HALF, LANES), f32),
            pltpu.VMEM((2, HALF, LANES), f32),
            pltpu.VMEM((4, LANES), f32),
            pltpu.VMEM((n_rve, 4, LANES), f32),
            pltpu.VMEM((16, LANES), jnp.int32),
            pltpu.SMEM((16, LANES), jnp.int32),
            pltpu.VMEM((HALF, LANES), jnp.int32),
            pltpu.SMEM((HALF, LANES), jnp.int32),
            pltpu.VMEM((2, 3, COMPS, HALF, LANES), f32),
            pltpu.SMEM((3, 4), f32),
            pltpu.VMEM(shape_grads.shape, f32),
            pltpu.VMEM((1, points), f32),
            pltpu.VMEM((2, 8), jnp.int32),
            pltpu.VMEM((2, 8), jnp.int32),
            pltpu.VMEM((1, points), jnp.int32),
            pltpu.VMEM((1, points), jnp.int32),
            dma((7,)),
            dma((4,)), dma, dma((2,)), dma, dma, dma((2,)), dma((2,)),
            dma((2,)), dma((2,)), dma((2,)), dma((2,)), dma((2,)), dma((2,)), dma, dma,
        ]
        nodal, stress, out = pl.pallas_call(
            functools.partial(main_kernel, count_paired, n_rve, n_mesh),
            in_specs=[hbm] * 11,
            out_specs=[vmem, vmem, hbm],
            out_shape=[
                jax.ShapeDtypeStruct((3, 4), f32),
                jax.ShapeDtypeStruct((COMPS, points), f32),
                jax.ShapeDtypeStruct((2 * ROWS, voxels), f32),
            ],
            scratch_shapes=scratch,
            compiler_params=pltpu.CompilerParams(
                collective_id=0, has_side_effects=True, vmem_limit_bytes=63 * 1024 * 1024
            ),
            name="solve_and_exchange",
        )(
            displacement, shape_grads, point_weights.reshape(1, points), conn.T, halo_nodes,
            owner.reshape(1, points), sweeps.reshape(1, points), warm, moduli,
            jnp.asarray(planes), jnp.asarray(coef),
        )
        micro, nodal, stress = hand_over(out, nodal, stress)
        micro = micro.reshape(COMPS, points, voxels).transpose(1, 0, 2)
        return nodal, stress, micro

    both = ("mesh", "rve")
    in_specs = (
        P(None, both), P(None, None, both), P(both), P(None, both), P(None, "mesh"),
        P(both, None, None), P(both, None, None), P(both), P(both),
    )
    out_specs = (P(None, both), P(None, both), P(both, None, None))
    return jax.shard_map(on_device, mesh=mesh, in_specs=in_specs, out_specs=out_specs, check_vma=False)
```

```python
import functools
import math

import jax
import jax.numpy as jnp
import numpy as np
from jax import lax
from jax.experimental import pallas as pl
from jax.experimental.pallas import tpu as pltpu
from jax.sharding import PartitionSpec as P

RES = 16
PLANE = 256
LANES = 128
TILES = 32
COMPS = 6
HALF = 8
ROWS = COMPS * HALF
SPAN = 8 * HALF
SENT = 4 * HALF
SHORT = 3 * HALF
EXTRA = 13
MIXED_LANE = 112
ENCODE, CHOOSE, DECODE, TABLE_ROWS = 21, 39, 41, 56
MESH = pl.DeviceIdType.MESH
f32 = jnp.float32
bf16 = jnp.bfloat16
index_pairs = ((0, 0), (1, 1), (2, 2), (1, 2), (0, 2), (0, 1))
coef_rows = [(c, d) for c in range(6) for d in range(c, 6)]
coef_at = {}
for _at, (_c, _d) in enumerate(coef_rows):
    coef_at[(_c, _d)] = _at
    coef_at[(_d, _c)] = _at


def half_planes():
    own = [(0, 0), (0, 8), (8, 0), (8, 8)]
    pairs, seen = [], set(own)
    for y in range(RES):
        for z in range(RES):
            if (y, z) not in seen:
                seen.add((y, z))
                seen.add(((-y) % RES, (-z) % RES))
                pairs.append((y, z))
    pairs.sort(key=lambda q: RES // 2 in q)
    lane_a = pairs + [(0, 0), (0, 8)]
    lane_b = pairs + [(8, 0), (8, 8)]
    return np.array(lane_a), np.array(lane_b), len(pairs)


def green_matrix(kx, ky, kz):
    def one(x, y, z):
        k = np.stack([x % RES, y % RES, z % RES]).astype(np.int64)
        xi = np.where(k < RES // 2, k, k - RES).astype(np.float64)
        size = np.sqrt((xi * xi).sum(0))
        n = np.where(size > 0, xi / np.where(size > 0, size, 1.0), 0.0)
        out = np.zeros((6, 6) + size.shape)
        for d, (i, j) in enumerate(index_pairs):
            t = np.zeros((3,) + size.shape)
            t[i] += n[j]
            if i != j:
                t[j] += n[i]
            s = (n * t).sum(0)
            weight = 1.0 if i == j else 2.0
            for c, (k_, h_) in enumerate(index_pairs):
                value = (n[k_] * t[h_] + n[h_] * t[k_]) / 2.2
                value = value - (2.2 / (1.1 * 3.3)) * n[k_] * n[h_] * s
                out[c, d] = value / weight
        return out

    return 0.5 * (one(kx, ky, kz) + one(-kx, -ky, -kz))


def transport_rows(k):
    xi = np.array([i if i < RES // 2 else i - RES for i in k], np.float64)
    size = np.sqrt((xi * xi).sum())
    n = xi / size if size > 0 else xi
    edge = [i == RES // 2 for i in k]
    back = np.zeros((6, 3))
    mixed = {}
    for c, (i, j) in enumerate(index_pairs):
        if i == j:
            back[c, i] = n[i]
        elif edge[i] == edge[j]:
            back[c, i], back[c, j] = 0.5 * n[j], 0.5 * n[i]
        else:
            mixed[c] = True
    rows = np.zeros(TABLE_ROWS)
    into = np.linalg.pinv(back)
    rows[ENCODE : ENCODE + 18] = into.reshape(-1)
    first, second = (sorted(mixed, reverse=True) + [5, 4])[:2]
    rows[CHOOSE], rows[CHOOSE + 1] = float(first == 5), float(second == 4)
    rows[DECODE : DECODE + 3] = n
    rows[DECODE + 3 : DECODE + 9] = back[3, 1], back[3, 2], back[4, 0], back[4, 2], back[5, 0], back[5, 1]
    if mixed:
        rows[DECODE + 9] = float(first == 5)
        rows[DECODE + 10] = float(first == 4)
        rows[DECODE + 11] = float(second == 4)
        rows[DECODE + 12] = float(second == 3)
    return rows


@functools.lru_cache(None)
def tables():
    lane_a, lane_b, count = half_planes()
    v = np.arange(PLANE)
    vy, vz = v // RES, v % RES
    angle = 2.0 * math.pi / RES

    def phase(lane):
        return angle * ((np.outer(vy, lane[:, 0]) + np.outer(vz, lane[:, 1])) % RES)

    paired = (np.arange(LANES) < count)[None, :]
    forward = np.concatenate(
        [np.cos(phase(lane_a)), np.where(paired, -np.sin(phase(lane_b)), np.cos(phase(lane_b)))], axis=1
    )
    coef = np.zeros((RES, 2, TABLE_ROWS, LANES))
    moved_by = functools.lru_cache(None)(transport_rows)
    for slot in range(RES):
        for part in range(2):
            ky, kz, kx, scale = [], [], [], []
            for lane in range(LANES):
                if lane < count:
                    y, z, x, weight = *lane_a[lane], slot, 2.0
                elif slot in (0, RES // 2):
                    y, z = lane_a[lane] if part == 0 else lane_b[lane]
                    x, weight = slot, 1.0
                else:
                    y, z = lane_a[lane] if slot < RES // 2 else lane_b[lane]
                    x, weight = (slot if slot < RES // 2 else RES - slot), 0.5
                ky.append(y), kz.append(z), kx.append(x), scale.append(weight / RES**3)
            for lane in range(LANES):
                coef[slot, part, :, lane] = moved_by((kx[lane] % RES, int(ky[lane]) % RES, int(kz[lane]) % RES))
            matrix = green_matrix(np.array(kx), np.array(ky), np.array(kz)) * np.array(scale)
            for row, (c, d) in enumerate(coef_rows):
                coef[slot, part, row] = matrix[c, d]

    def split(table):
        high = jnp.asarray(table, f32).astype(bf16)
        low = (np.asarray(table, np.float64) - np.asarray(high).astype(np.float64)).astype(np.float32)
        return np.asarray(high), np.asarray(jnp.asarray(low).astype(bf16))

    with jax.ensure_compile_time_eval():
        fh, fl = split(forward)
        ih, il = split(forward.T)
    return np.stack([fh, fl, ih, il]), coef.astype(np.float32), count


def complex_mul(a, b):
    re, im = a
    cr, ci = b
    if abs(ci) < 1e-12 and abs(cr - 1) < 1e-12:
        return a
    if abs(cr) < 1e-12:
        return (im, -re) if ci < 0 else (-im, re)
    if abs(abs(cr) - abs(ci)) < 1e-12:
        h = abs(cr)
        sr, si = cr > 0, ci > 0
        if sr and not si:
            return (h * (re + im), h * (im - re))
        if not sr and not si:
            return (h * (im - re), -h * (re + im))
        if sr and si:
            return (h * (re - im), h * (im + re))
        return (-h * (re + im), h * (re - im))
    return (cr * re - ci * im, cr * im + ci * re)


def four_point(a, b, c, d, sign):
    s0 = (a[0] + c[0], a[1] + c[1])
    s1 = (a[0] - c[0], a[1] - c[1])
    s2 = (b[0] + d[0], b[1] + d[1])
    s3 = (b[0] - d[0], b[1] - d[1])
    turned = (s3[1], -s3[0]) if sign < 0 else (-s3[1], s3[0])
    return (
        (s0[0] + s2[0], s0[1] + s2[1]),
        (s1[0] + turned[0], s1[1] + turned[1]),
        (s0[0] - s2[0], s0[1] - s2[1]),
        (s1[0] - turned[0], s1[1] - turned[1]),
    )


def sixteen_point(values, sign):
    columns = []
    for r in range(4):
        out = four_point(values[r], values[r + 4], values[r + 8], values[r + 12], sign)
        columns.append(
            [
                complex_mul(out[k], (math.cos(2 * math.pi * r * k / 16), sign * math.sin(2 * math.pi * r * k / 16)))
                for k in range(4)
            ]
        )
    result = [None] * 16
    for k in range(4):
        out = four_point(columns[0][k], columns[1][k], columns[2][k], columns[3][k], sign)
        for m in range(4):
            result[k + 4 * m] = out[m]
    return result


def iota(shape, dim):
    return lax.broadcasted_iota(jnp.int32, shape, dim)


def sum_lanes(x):
    return jnp.sum(x, axis=1, keepdims=True)


def sum_rows(x):
    return jnp.sum(x, axis=0, keepdims=True)


def split_bf16(x):
    high = x.astype(bf16)
    low = (x - high.astype(f32)).astype(bf16)
    return high, low


def three_pass(high, low, table_high, table_low):
    def dot(a, b):
        return jnp.dot(a, b, preferred_element_type=f32)

    return dot(high, table_high) + (dot(low, table_high) + dot(high, table_low))


def main_kernel(
    count_paired, n_rve, n_mesh,
    disp_h, grads_h, weight_h, conn_h, halo_h, owner_h, sweeps_h, warm_h, moduli_h, plane_h, coef_h,
    nodal_o, stress_o, out_h,
    warm_v, moduli_v, plane_v, coef_v, field, mod, tau_h, tau_l, spec_0, spec_a, spec_b, payload, got1_a, got1_b, got2, mixed, sums_v, stage,
    tile_v, gathered, halo_out, halo_in, force_out, force_in, own_out, own_in,
    perm_v, perm_s, table_v, table_s, column_v,
    disp_s, grads_v, weight_v, conn_v, halo_v, owner_v, sweeps_v, small_sem,
    in_sem, out_sem, idx_sem, gather_send, gather_recv, halo_send, halo_recv,
    send1, recv1, send2, recv2, fhalo_send, fhalo_recv, own_send, own_recv,
):
    me = lax.axis_index("rve")
    part = lax.axis_index("mesh")
    others = n_rve - 1

    def after_me(k):
        return jnp.where(me + k >= n_rve, me + k - n_rve, me + k)

    got1 = (got1_a, got1_b)
    last_row = others * SENT + HALF - 1
    has_below = part > 0
    has_above = part < n_mesh - 1

    small = [
        pltpu.make_async_copy(source, target, small_sem.at[at])
        for at, (source, target) in enumerate((
            (owner_h, owner_v), (sweeps_h, sweeps_v), (disp_h, disp_s), (halo_h, halo_v),
            (conn_h, conn_v), (grads_h, grads_v), (weight_h, weight_v),
        ))
    ]
    for load in small:
        load.start()

    def load_tile(t):
        at = pl.multiple_of(t * LANES, LANES)
        return pltpu.make_async_copy(
            warm_h.at[:, pl.ds(at, LANES)], warm_v.at[t, pl.ds(0, COMPS * 16), :], in_sem.at[0]
        )

    def start_tile(t, carry):
        load_tile(t).start()
        return carry

    lax.fori_loop(0, TILES, start_tile, 0)
    big_loads = [
        pltpu.make_async_copy(moduli_h, moduli_v, in_sem.at[1]),
        pltpu.make_async_copy(plane_h, plane_v, in_sem.at[2]),
        pltpu.make_async_copy(coef_h, coef_v, in_sem.at[3]),
    ]
    for load in big_loads:
        load.start()

    barrier = pltpu.get_barrier_semaphore()

    for k in range(1, n_rve):
        pl.semaphore_signal(barrier, inc=1, device_id={"rve": after_me(k)}, device_id_type=MESH)

    @pl.when(has_below)
    def _():
        pl.semaphore_signal(barrier, inc=1, device_id={"mesh": part - 1}, device_id_type=MESH)

    @pl.when(has_above)
    def _():
        pl.semaphore_signal(barrier, inc=1, device_id={"mesh": part + 1}, device_id_type=MESH)

    for load in small:
        load.wait()

    owner_row = owner_v[...].astype(f32)
    sub16, lane16 = iota((16, 16), 0), iota((16, 16), 1)
    owner_col = sum_lanes(jnp.where(sub16 == lane16, jnp.broadcast_to(owner_row, (16, 16)), 0.0))
    place = 0.5 * sum_rows(jnp.where(owner_col < owner_row, 1.0, 0.0))
    rank = sum_rows(jnp.where((owner_col == owner_row) & (sub16 < lane16), 1.0, 0.0))
    slot_row = 8.0 * rank + place
    chosen = jnp.where(slot_row == sub16.astype(f32), 1.0, 0.0)
    perm_col = sum_lanes(chosen * lane16.astype(f32))
    perm_v[...] = jnp.broadcast_to(perm_col, (16, LANES)).astype(jnp.int32)
    count_col = sum_lanes(chosen * sweeps_v[...].astype(f32))
    load_perm = pltpu.make_async_copy(perm_v, perm_s, idx_sem.at[0])
    load_perm.start()

    lane_row = iota((1, LANES), 1).astype(f32)
    sends_row = 0.5 * sum_rows(jnp.where(owner_col == lane_row, 1.0, 0.0))
    sub4, lane4 = iota((4, LANES), 0), iota((4, LANES), 1)
    tile = jnp.where(sub4 == 3, sends_row, 0.0)
    for i in range(3):
        for node in range(4):
            tile = jnp.where((sub4 == i) & (lane4 == 4 * me + node), disp_s[i, node], tile)
    tile_v[...] = tile
    gathered[me] = tile

    extra = jnp.where(has_below, 1, 0) + jnp.where(has_above, 1, 0)
    pl.semaphore_wait(barrier, others + extra)

    def to_all(source, target, send, recv):
        def body(k, carry):
            to = after_me(k)
            pltpu.make_async_remote_copy(
                source, target, send, recv, device_id={"rve": to}, device_id_type=MESH
            ).start()
            return carry

        for k in range(1, n_rve):
            body(k, 0)

    def wait_bytes(view, sem):
        pltpu.make_async_copy(view, view, sem).wait()

    to_all(tile_v, gathered.at[me], gather_send, gather_recv)

    load_perm.wait()
    big_loads[0].wait()

    wait_bytes(warm_v.at[:, pl.ds(0, COMPS * 16), :], in_sem.at[0])
    places_at = [
        (half, pos, jnp.clip(perm_s[half * HALF + pos, 0], 0, 15)) for half in range(2) for pos in range(HALF)
    ]

    def place_tile(t, carry):
        at = pl.multiple_of(t * LANES, LANES)
        for half, pos, point in places_at:
            field[half, t, pl.ds(pos, COMPS, stride=HALF), :] = warm_v[t, pl.ds(point, COMPS, stride=16), :]
            mod[half, t, pl.ds(pos, 2, stride=HALF), :] = moduli_v[point, :, pl.ds(at, LANES)]
        return carry

    lax.fori_loop(0, TILES, place_tile, 0)

    def add_up(t, sums):
        return tuple(
            sums[half * COMPS + c] + field[half, t, c * HALF : (c + 1) * HALF, :]
            for half in range(2)
            for c in range(COMPS)
        )

    sums = lax.fori_loop(
        0, TILES, add_up, tuple(jnp.zeros((HALF, LANES), f32) for _ in range(2 * COMPS)), unroll=4
    )
    means = [[sum_lanes(sums[half * COMPS + c]) * (1.0 / 4096.0) for c in range(COMPS)] for half in range(2)]

    big_loads[1].wait()
    big_loads[2].wait()
    odd_lane = iota((HALF, LANES), 1) >= count_paired

    def table_row(k, part_at, row):
        return coef_v[k, part_at, row : row + 1, :]

    def forward_into(planes, put):
        def forward(c, carry):
            planed = three_pass(tau_h[c], tau_l[c], plane_v[0], plane_v[1])
            values = [
                (planed[x * HALF : (x + 1) * HALF, :LANES], planed[x * HALF : (x + 1) * HALF, LANES:])
                for x in range(RES)
            ]
            z = sixteen_point(values, -1)
            for k in range(1, 8):
                a, b = z[k], z[RES - k]
                z[k] = (jnp.where(odd_lane, a[0] + b[0], a[0]), jnp.where(odd_lane, a[1] - b[1], a[1]))
                z[RES - k] = (jnp.where(odd_lane, a[1] + b[1], b[0]), jnp.where(odd_lane, b[0] - a[0], b[1]))
            for k in range(RES):
                put(k, 0, c, z[k][0])
                put(k, 1, c, z[k][1])
            return carry

        lax.fori_loop(0, planes, forward, 0, unroll=planes // 2)

    def polarize_into(half, first):
        def polarize(u, carry):
            for b in range(2):
                cats = [[] for _ in range(8)]
                for step in range(2):
                    t = (2 * u + step) * 2 + b
                    eps = [field[half, t, c * HALF : (c + 1) * HALF, :] for c in range(COMPS)]
                    if first:
                        eps = [eps[c] - means[half][c] for c in range(COMPS)]
                    lam = mod[half, t, 0:HALF, :] - 1.1
                    shear = 2.0 * mod[half, t, HALF : 2 * HALF, :] - 2.2
                    pressure = lam * (eps[0] + eps[1] + eps[2])
                    double = shear + shear
                    for c in range(3):
                        cats[c].append(shear * eps[c] + pressure)
                    for c in range(3, 6):
                        cats[c].append(double * eps[c])
                    if first:
                        cats[6].append(lam)
                        cats[7].append(shear)
                for c in range(8 if first else COMPS):
                    high, low = split_bf16(jnp.concatenate(cats[c], axis=0))
                    at = pl.multiple_of(u * 16, 16)
                    tau_h[c, pl.ds(at, 16), b * LANES : (b + 1) * LANES] = high
                    tau_l[c, pl.ds(at, 16), b * LANES : (b + 1) * LANES] = low
            return carry

        lax.fori_loop(0, 8, polarize, 0, unroll=2)

    def start_spectrum(half):
        def put(k, part_at, c, value):
            spec_0[half, k, part_at, c] = value

        polarize_into(half, True)
        forward_into(8, put)

    def apply_green(half, k, part_at, ins, spec, keep):
        rows = [table_row(k, part_at, r) for r in range(len(coef_rows))]
        for c in range(COMPS):
            total = rows[coef_at[(c, 0)]] * ins[0]
            for d in range(1, COMPS):
                total = total + rows[coef_at[(c, d)]] * ins[d]
            if keep is not None:
                total = jnp.where(keep, total, spec_a[k, part_at, c])
            spec[k, part_at, c] = total

    def first_spectrum(half):
        def green(k, carry):
            level = [column_v[half, 1, c] for c in range(COMPS)]
            level = level[:3] + [2.0 * x for x in level[3:]]
            whole = level[0] + level[1] + level[2]
            for part_at in range(2):
                ins = [spec_0[half, k, part_at, c] for c in range(8)]
                pressure = whole * ins[6]
                ins = [ins[c] + level[c] * ins[7] for c in range(COMPS)]
                ins = [ins[c] + pressure if c < 3 else ins[c] for c in range(COMPS)]
                apply_green(half, k, part_at, ins, spec_a, None)
            return carry

        lax.fori_loop(0, RES, green, 0, unroll=2)

    def second_spectrum(half):
        def put(k, part_at, c, value):
            spec_b[half, k, part_at, c] = value

        polarize_into(half, False)
        forward_into(COMPS, put)

        def green(k, carry):
            again = column_v[half, 2, 0] > 1.5
            for part_at in range(2):
                ins = [spec_b[half, k, part_at, c] for c in range(COMPS)]
                apply_green(half, k, part_at, ins, spec_b.at[half], again)
            return carry

        lax.fori_loop(0, RES, green, 0, unroll=2)

    start_spectrum(0)

    wait_bytes(gathered.at[pl.ds(0, others)], gather_recv)
    moved = jnp.sum(gathered[...], axis=0)
    lane8, sub8 = iota((HALF, LANES), 1).astype(f32), iota((HALF, LANES), 0).astype(f32)
    eye8 = iota((HALF, HALF), 0) == iota((HALF, HALF), 1)
    halo_rows = halo_v[...].astype(f32)
    halo_hot = []
    for side in range(2):
        col = sum_lanes(jnp.where(eye8, jnp.broadcast_to(halo_rows[side : side + 1], (HALF, HALF)), 0.0))
        halo_hot.append(jnp.where(col == lane8, 1.0, 0.0))
    out_tile = jnp.zeros((HALF, LANES), f32)
    for side in range(2):
        for i in range(3):
            col = sum_lanes(halo_hot[side] * moved[i : i + 1])
            out_tile = jnp.where(lane8 == 3 * side + i, col, out_tile)
    halo_out[...] = out_tile

    def swap_halo(source, target, send, recv):
        @pl.when(has_below)
        def _():
            pltpu.make_async_remote_copy(
                source, target.at[1], send.at[0], recv.at[1], device_id={"mesh": part - 1}, device_id_type=MESH
            ).start()

        @pl.when(has_above)
        def _():
            pltpu.make_async_remote_copy(
                source, target.at[0], send.at[1], recv.at[0], device_id={"mesh": part + 1}, device_id_type=MESH
            ).start()

    def take_halo(source, target, recv):
        @pl.when(has_below)
        def _():
            wait_bytes(target.at[0], recv.at[0])

        @pl.when(jnp.logical_not(has_below))
        def _():
            target[0] = jnp.zeros((HALF, LANES), f32)

        @pl.when(has_above)
        def _():
            wait_bytes(target.at[1], recv.at[1])

        @pl.when(jnp.logical_not(has_above))
        def _():
            target[1] = jnp.zeros((HALF, LANES), f32)

    swap_halo(halo_out, halo_in, halo_send, halo_recv)

    sends = jnp.concatenate([gathered[s, 3:4] for s in range(n_rve)], axis=0)
    lower = jnp.where(iota((n_rve, n_rve), 1) < iota((n_rve, n_rve), 0), 1.0, 0.0).astype(bf16)
    upper = jnp.where(iota((LANES, LANES), 0) < iota((LANES, LANES), 1), 1.0, 0.0).astype(bf16)
    sends_b = sends.astype(bf16)
    order = jnp.dot(lower, sends_b, preferred_element_type=f32)
    places = jnp.dot(sends_b, upper, preferred_element_type=f32)
    rows_at = iota((n_rve, LANES), 0).astype(f32) * float(SENT) + places
    table = jnp.zeros((HALF, LANES), f32)
    for k in range(HALF):
        row = sum_rows(jnp.where((sends > 0.5) & (order == float(k)), rows_at, 0.0))
        table = jnp.where(sub8 == float(k), row, table)
    table_v[...] = table.astype(jnp.int32)
    load_table = pltpu.make_async_copy(table_v, table_s, idx_sem.at[1])
    load_table.start()

    conn_rows = conn_v[...].astype(f32)
    own_hot, far_hot = [], []
    for e in range(2):
        col = sum_lanes(jnp.where(eye8, jnp.broadcast_to(conn_rows[e : e + 1], (HALF, HALF)), 0.0))
        own_hot.append(jnp.where(col == lane8, 1.0, 0.0))
        far_hot.append(jnp.where(col - float(LANES) == lane8, 1.0, 0.0))
    first_element = iota((HALF, 16), 1) < 8

    start_spectrum(1)
    take_halo(halo_out, halo_in, halo_recv)
    below, above = halo_in[0], halo_in[1]
    spread_disp = []
    for i in range(3):
        far = sum_rows(jnp.where(lane8 == sub8, below[:, 3 + i : 4 + i], 0.0))
        far = far + sum_rows(jnp.where(lane8 == sub8 + 8.0, above[:, i : i + 1], 0.0))
        cols = [sum_lanes(own_hot[e] * moved[i : i + 1] + far_hot[e] * far) for e in range(2)]
        spread_disp.append(jnp.where(first_element, cols[0], cols[1]))
    grads = [grads_v[j] for j in range(3)]
    g = [[sum_rows(spread_disp[i] * grads[j]) for j in range(3)] for i in range(3)]
    macro = [
        g[0][0], g[1][1], g[2][2],
        (g[1][2] + g[2][1]) * 0.5, (g[0][2] + g[2][0]) * 0.5, (g[0][1] + g[1][0]) * 0.5,
    ]
    macro_cols = [sum_lanes(chosen * row) for row in macro]
    for c in range(COMPS):
        for half in range(2):
            col = macro_cols[c][half * HALF : (half + 1) * HALF]
            column_v[half, 1, c] = jnp.broadcast_to(col, (HALF, LANES))
    for half in range(2):
        column_v[half, 2, 0] = jnp.broadcast_to(count_col[half * HALF : (half + 1) * HALF], (HALF, LANES))

    def strain_from(half, spec, take):
        def backward(c, carry):
            z = [(spec[k, 0, c], spec[k, 1, c]) for k in range(RES)]
            for k in range(1, 8):
                a, b = z[k], z[RES - k]
                z[k] = (jnp.where(odd_lane, a[0] - b[1], a[0]), jnp.where(odd_lane, a[1] + b[0], a[1]))
                z[RES - k] = (jnp.where(odd_lane, a[0] + b[1], b[0]), jnp.where(odd_lane, b[0] - a[1], b[1]))
            values = sixteen_point(z, 1)
            lined = jnp.concatenate(
                [
                    jnp.concatenate([values[x][0] for x in range(RES)], axis=0),
                    jnp.concatenate([values[x][1] for x in range(RES)], axis=0),
                ],
                axis=1,
            )
            high, low = split_bf16(lined)
            fluct = three_pass(high, low, plane_v[2], plane_v[3])
            level = column_v[half, 1, c]
            take(
                c,
                [
                    level - fluct[t // 2 * HALF : (t // 2 + 1) * HALF, t % 2 * LANES : (t % 2 + 1) * LANES]
                    for t in range(TILES)
                ],
            )
            return carry

        lax.fori_loop(0, COMPS, backward, 0, unroll=3)

    def keep_field(half):
        def take(c, tiles):
            at = pl.multiple_of(c * HALF, HALF)
            for t in range(TILES):
                field[half, t, pl.ds(at, HALF), :] = tiles[t]

        strain_from(half, spec_a, take)

    def mean_stress(half):
        def take(c, tiles):
            for which in range(2):
                parts = [
                    mod[half, t, which * HALF : (which + 1) * HALF, :] * tiles[t] for t in range(TILES)
                ]
                while len(parts) > 1:
                    parts = [p + q for p, q in zip(parts[::2], parts[1::2])]
                sums_v[which, c] = parts[0]

        strain_from(half, spec_b.at[half], take)
        pressure = sums_v[0, 0] + sums_v[0, 1] + sums_v[0, 2]
        result = []
        for c in range(COMPS):
            total = 2.0 * sums_v[1, c]
            if c < 3:
                total = total + pressure
            result.append(sum_lanes(total) * (1.0 / 4096.0))
        return result

    packed_group = iota((HALF, LANES), 1) // 16

    def encode(half):
        def extras(k, part_at, eps):
            first = jnp.where(table_row(k, part_at, CHOOSE) > 0.5, eps[5], eps[4])
            second = jnp.where(table_row(k, part_at, CHOOSE + 1) > 0.5, eps[4], eps[3])
            return first, second

        def body(i, carry):
            packed = jnp.zeros((HALF, LANES), f32)
            for step in range(2):
                k = 2 * i + step
                for part_at in range(2):
                    eps = [spec_b[half, k, part_at, c] for c in range(COMPS)]
                    for j in range(3):
                        total = table_row(k, part_at, ENCODE + 6 * j) * eps[0]
                        for c in range(1, COMPS):
                            total = total + table_row(k, part_at, ENCODE + 6 * j + c) * eps[c]
                        payload[half, 2 * k + part_at, j * HALF : (j + 1) * HALF, :] = total
                    for e, value in enumerate(extras(k, part_at, eps)):
                        piece = (2 * step + part_at) * 2 + e
                        shift = (16 * piece + 16) % LANES
                        if shift:
                            value = pltpu.roll(value, shift, 1)
                        packed = jnp.where(packed_group == piece, value, packed)
            payload[half, i, SHORT:SENT, :] = packed
            return carry

        lax.fori_loop(0, 8, body, 0, unroll=2)
        for part_at in range(2):
            eps = [spec_b[half, RES // 2, part_at, c] for c in range(COMPS)]
            for e, value in enumerate(extras(RES // 2, part_at, eps)):
                payload[half, 8 + 2 * part_at + e, SHORT:SENT, :] = value
        levels = jnp.zeros((HALF, LANES), f32)
        for c in range(COMPS):
            levels = jnp.where(lane8 == float(c), column_v[half, 1, c], levels)
        payload[half, EXTRA - 1, SHORT:SENT, :] = levels

    def decode(half):
        def restore(k, part_at, first, second):
            d = [got2[half, 2 * k + part_at, j * HALF : (j + 1) * HALF, :] for j in range(3)]
            row = [table_row(k, part_at, DECODE + r) for r in range(13)]
            for c in range(3):
                spec_a[k, part_at, c] = row[c] * d[c]
            spec_a[k, part_at, 3] = row[3] * d[1] + row[4] * d[2] + row[12] * second
            spec_a[k, part_at, 4] = row[5] * d[0] + row[6] * d[2] + (row[10] * first + row[11] * second)
            spec_a[k, part_at, 5] = row[7] * d[0] + row[8] * d[1] + row[9] * first

        def body(i, carry):
            packed = got2[half, i, SHORT:SENT, :]
            for step in range(2):
                for part_at in range(2):
                    values = []
                    for e in range(2):
                        piece = (2 * step + part_at) * 2 + e
                        shift = (LANES - (16 * piece + 16) % LANES) % LANES
                        values.append(pltpu.roll(packed, shift, 1) if shift else packed)
                    restore(2 * i + step, part_at, *values)
            return carry

        lax.fori_loop(0, 8, body, 0, unroll=2)
        for part_at in range(2):
            restore(
                RES // 2, part_at,
                got2[half, 8 + 2 * part_at, SHORT:SENT, :], got2[half, 9 + 2 * part_at, SHORT:SENT, :],
            )
        levels = got2[half, EXTRA - 1, SHORT:SENT, :]
        for c in range(COMPS):
            column_v[half, 1, c] = jnp.broadcast_to(levels[:, c : c + 1], (HALF, LANES))

        def take(c, tiles):
            at = pl.multiple_of(c * 2 * HALF, 2 * HALF)
            for t in range(TILES):
                mixed[t, pl.ds(at + half, HALF, stride=2), :] = tiles[t]

        strain_from(half, spec_a, take)

    long_rows = jnp.where(me < EXTRA, 1, 0) == 1

    def by_me(action):
        @pl.when(long_rows)
        def _():
            action(SENT)

        @pl.when(jnp.logical_not(long_rows))
        def _():
            action(SHORT)

    def wait_mine(sem):
        by_me(lambda rows: wait_bytes(got2.at[0, pl.ds(0, others), pl.ds(0, rows), :], sem))

    def wait_all(sem):
        full = EXTRA * SENT + (n_rve - EXTRA) * SHORT
        by_me(lambda rows: wait_bytes(got1_a.at[pl.ds(0, full - rows), :], sem))

    def send_spread(half):
        at = pl.multiple_of(me * SENT, SENT)
        for j in range(4):
            rows = pl.multiple_of(me * SENT + j * HALF, HALF)
            got1[half][pl.ds(rows, HALF), :] = payload[half, me, j * HALF : (j + 1) * HALF, :]

        def body(k, carry):
            to = after_me(k)

            def send(rows):
                pltpu.make_async_remote_copy(
                    payload.at[half, to, pl.ds(0, rows), :], got1[half].at[pl.ds(at, rows), :],
                    send1.at[half], recv1.at[half], device_id={"rve": to}, device_id_type=MESH,
                ).start()

            @pl.when(to < EXTRA)
            def _():
                send(SENT)

            @pl.when(to >= EXTRA)
            def _():
                send(SHORT)

            return carry

        for k in range(1, n_rve):
            body(k, 0)

    def send_owned(half):
        wait_mine(recv1.at[half])

        def collect(to):
            for at in range(HALF):
                row = jnp.clip(table_s[at, to], 0, last_row)
                stage[half, to, pl.ds(at, 4, stride=HALF), :] = got1[half][pl.ds(row, 4, stride=HALF), :]

        def body(k, carry):
            to = after_me(k)
            collect(to)
            by_me(
                lambda rows: pltpu.make_async_remote_copy(
                    stage.at[half, to, pl.ds(0, rows), :], got2.at[half, me, pl.ds(0, rows), :],
                    send2.at[half], recv2.at[half], device_id={"rve": to}, device_id_type=MESH,
                ).start()
            )
            return carry

        for k in range(1, n_rve):
            body(k, 0)
        collect(me)
        for j in range(4):
            got2[half, me, j * HALF : (j + 1) * HALF, :] = stage[half, me, j * HALF : (j + 1) * HALF, :]

    load_table.wait()
    for half in range(2):
        first_spectrum(half)
        keep_field(half)
        if half == 1:
            send_owned(0)
        second_spectrum(half)
        encode(half)
        send_spread(half)
    stress = [mean_stress(0), mean_stress(1)]

    weights = weight_v[...]
    sigma = []
    for c in range(COMPS):
        col = jnp.concatenate([stress[0][c], stress[1][c]], axis=0)
        row = sum_rows(chosen * col)
        stress_o[c : c + 1, :] = row
        sigma.append(row * weights)
    grid = ((0, 5, 4), (5, 1, 3), (4, 3, 2))
    force_tile = jnp.zeros((HALF, LANES), f32)
    own_rows = []
    for i in range(3):
        point_force = sigma[grid[i][0]] * grads[0] + sigma[grid[i][1]] * grads[1] + sigma[grid[i][2]] * grads[2]
        cols = [
            sum_lanes(jnp.where(first_element, point_force, 0.0)),
            sum_lanes(jnp.where(first_element, 0.0, point_force)),
        ]
        own_rows.append(sum_rows(own_hot[0] * cols[0] + own_hot[1] * cols[1]))
        far = sum_rows(far_hot[0] * cols[0] + far_hot[1] * cols[1])
        force_tile = jnp.where(sub8 == float(i), far, force_tile)
    force_out[...] = force_tile
    swap_halo(force_out, force_in, fhalo_send, fhalo_recv)
    take_halo(force_out, force_in, fhalo_recv)
    below, above = force_in[0], force_in[1]
    own_tile = jnp.zeros((4, LANES), f32)
    for i in range(3):
        low = sum_lanes(jnp.where(lane8 == sub8 + 8.0, below[i : i + 1], 0.0))
        high = sum_lanes(jnp.where(lane8 == sub8, above[i : i + 1], 0.0))
        row = own_rows[i] + sum_rows(halo_hot[0] * low + halo_hot[1] * high)
        own_tile = jnp.where(sub4 == i, row, own_tile)
    own_out[...] = own_tile
    own_in[me] = own_tile
    to_all(own_out, own_in.at[me], own_send, own_recv)
    send_owned(1)
    wait_all(recv2.at[0])
    decode(0)
    wait_all(recv2.at[1])
    decode(1)

    def copy_out(t):
        at = pl.multiple_of(t * LANES, LANES)
        return pltpu.make_async_copy(
            mixed.at[t, pl.ds(0, 2 * ROWS), :], out_h.at[:, pl.ds(at, LANES)], out_sem
        )

    def start_out(t, carry):
        copy_out(t).start()
        return carry

    lax.fori_loop(0, TILES, start_out, 0)
    wait_bytes(own_in.at[pl.ds(0, others)], own_recv)
    total = jnp.sum(own_in[...], axis=0)
    mine = jnp.zeros((4, LANES), f32)
    for node in range(4):
        mine = jnp.where(lane4 == node, sum_lanes(jnp.where(lane4 == 4 * me + node, total, 0.0)), mine)
    nodal_o[...] = mine[:3, :4]
    wait_bytes(mixed.at[:, pl.ds(0, 2 * ROWS), :], out_sem)
    wait_bytes(gathered.at[pl.ds(0, others)], gather_send)
    wait_bytes(own_in.at[pl.ds(0, others)], own_send)
    for half in range(2):
        wait_all(send1.at[half])
        wait_mine(send2.at[half])
    for send, source in ((halo_send, halo_out), (fhalo_send, force_out)):
        @pl.when(has_below)
        def _(send=send, source=source):
            wait_bytes(source, send.at[0])

        @pl.when(has_above)
        def _(send=send, source=source):
            wait_bytes(source, send.at[1])


def hand_over_kernel(field_h, nodal_h, stress_h, field_o, nodal_o, stress_o, held, nodal_v, stress_v, in_sem, out_sem):
    through = [
        (field_h.at[pl.ds(at, HALF), :], held.at[pl.ds(at, HALF), :], field_o.at[pl.ds(at, HALF), :])
        for at in range(0, 2 * ROWS, HALF)
    ]
    through = [(nodal_h, nodal_v, nodal_o), (stress_h, stress_v, stress_o)] + through
    taken = [pltpu.make_async_copy(a, b, in_sem.at[n]) for n, (a, b, _) in enumerate(through)]
    given = [pltpu.make_async_copy(b, c, out_sem.at[n]) for n, (_, b, c) in enumerate(through)]
    for copy in taken:
        copy.start()
    for copy, onward in zip(taken, given):
        copy.wait()
        onward.start()
    for onward in given:
        onward.wait()


def hand_over(field, nodal, stress):
    hbm = pl.BlockSpec(memory_space=pltpu.HBM)
    count = 2 * ROWS // HALF + 2
    return pl.pallas_call(
        hand_over_kernel,
        in_specs=[hbm, hbm, hbm],
        out_specs=[hbm, hbm, hbm],
        out_shape=[jax.ShapeDtypeStruct(x.shape, f32) for x in (field, nodal, stress)],
        scratch_shapes=[pltpu.VMEM(x.shape, f32) for x in (field, nodal, stress)]
        + [pltpu.SemaphoreType.DMA((count,)), pltpu.SemaphoreType.DMA((count,))],
        compiler_params=pltpu.CompilerParams(vmem_limit_bytes=63 * 1024 * 1024),
        name="hand_over",
    )(field, nodal, stress)


def solution(mesh):
    n_rve, n_mesh = mesh.shape["rve"], mesh.shape["mesh"]
    planes, coef, count_paired = tables()

    def on_device(displacement, shape_grads, point_weights, conn, halo_nodes, warm_strain, moduli, owner, sweeps):
        points, voxels = warm_strain.shape[0], warm_strain.shape[2]
        warm = warm_strain.transpose(1, 0, 2).reshape(COMPS * points, voxels)
        vmem = pl.BlockSpec(memory_space=pltpu.VMEM)
        hbm = pl.BlockSpec(memory_space=pltpu.HBM)
        dma = pltpu.SemaphoreType.DMA
        scratch = [
            pltpu.VMEM((TILES, 8 * points, LANES), f32),
            pltpu.VMEM((points, 2, voxels), f32),
            pltpu.VMEM(planes.shape, bf16),
            pltpu.VMEM(coef.shape, f32),
            pltpu.VMEM((2, TILES, SPAN, LANES), f32),
            pltpu.VMEM((2, TILES, SPAN, LANES), f32),
            pltpu.VMEM((8, RES * HALF, PLANE), bf16),
            pltpu.VMEM((8, RES * HALF, PLANE), bf16),
            pltpu.VMEM((2, RES, 2, 8, HALF, LANES), f32),
            pltpu.VMEM((RES, 2, COMPS, HALF, LANES), f32),
            pltpu.VMEM((2, RES, 2, COMPS, HALF, LANES), f32),
            pltpu.VMEM((2, n_rve, SENT, LANES), f32),
            pltpu.VMEM((n_rve * SENT + SPAN, LANES), f32),
            pltpu.VMEM((n_rve * SENT + SPAN, LANES), f32),
            pltpu.VMEM((2, n_rve, SENT, LANES), f32),
            pltpu.VMEM((TILES, 2 * ROWS + HALF, LANES), f32),
            pltpu.VMEM((2, COMPS, HALF, LANES), f32),
            pltpu.VMEM((2, n_rve, SPAN, LANES), f32),
            pltpu.VMEM((4, LANES), f32),
            pltpu.VMEM((n_rve, 4, LANES), f32),
            pltpu.VMEM((HALF, LANES), f32),
            pltpu.VMEM((2, HALF, LANES), f32),
            pltpu.VMEM((HALF, LANES), f32),
            pltpu.VMEM((2, HALF, LANES), f32),
            pltpu.VMEM((4, LANES), f32),
            pltpu.VMEM((n_rve, 4, LANES), f32),
            pltpu.VMEM((16, LANES), jnp.int32),
            pltpu.SMEM((16, LANES), jnp.int32),
            pltpu.VMEM((HALF, LANES), jnp.int32),
            pltpu.SMEM((HALF, LANES), jnp.int32),
            pltpu.VMEM((2, 3, COMPS, HALF, LANES), f32),
            pltpu.SMEM((3, 4), f32),
            pltpu.VMEM(shape_grads.shape, f32),
            pltpu.VMEM((1, points), f32),
            pltpu.VMEM((2, 8), jnp.int32),
            pltpu.VMEM((2, 8), jnp.int32),
            pltpu.VMEM((1, points), jnp.int32),
            pltpu.VMEM((1, points), jnp.int32),
            dma((7,)),
            dma((4,)), dma, dma((2,)), dma, dma, dma((2,)), dma((2,)),
            dma((2,)), dma((2,)), dma((2,)), dma((2,)), dma((2,)), dma((2,)), dma, dma,
        ]
        nodal, stress, out = pl.pallas_call(
            functools.partial(main_kernel, count_paired, n_rve, n_mesh),
            in_specs=[hbm] * 11,
            out_specs=[vmem, vmem, hbm],
            out_shape=[
                jax.ShapeDtypeStruct((3, 4), f32),
                jax.ShapeDtypeStruct((COMPS, points), f32),
                jax.ShapeDtypeStruct((2 * ROWS, voxels), f32),
            ],
            scratch_shapes=scratch,
            compiler_params=pltpu.CompilerParams(
                collective_id=0, has_side_effects=True, vmem_limit_bytes=63 * 1024 * 1024
            ),
            name="solve_and_exchange",
        )(
            displacement, shape_grads, point_weights.reshape(1, points), conn.T, halo_nodes,
            owner.reshape(1, points), sweeps.reshape(1, points), warm, moduli,
            jnp.asarray(planes), jnp.asarray(coef),
        )
        micro, nodal, stress = hand_over(out, nodal, stress)
        micro = micro.reshape(COMPS, points, voxels).transpose(1, 0, 2)
        return nodal, stress, micro

    both = ("mesh", "rve")
    in_specs = (
        P(None, both), P(None, None, both), P(both), P(None, both), P(None, "mesh"),
        P(both, None, None), P(both, None, None), P(both), P(both),
    )
    out_specs = (P(None, both), P(None, both), P(both, None, None))
    return jax.shard_map(on_device, mesh=mesh, in_specs=in_specs, out_specs=out_specs, check_vma=False)
```
